256 devices in a mesh: dp: 16 (over z_hi, y, core), slab: 16 (over z_lo, x).
Axes of the slice: x: 4, y: 4, z: 8 (z_hi: 2, z_lo: 4; z = z_hi * 4 + z_lo), core: 2. Of those that a mesh axis runs over, the one named last changes fastest.
Arguments:
- features: bfloat16 [16, 160, 64, 256], P('dp', 'slab'), may hold values from -6 to 6
- cotangent: bfloat16 [16, 160, 64, 256], P('dp', 'slab'), may hold values from -6 to 6
- neighbour_table: int32 [16, 160, 27], P('dp', 'slab'), may hold values from 0 to 14, as said below
- send_lists: int32 [16, 16, 2, 2], P('dp', 'slab'), may hold values from 0 to 10, as said below
- block_counts: int32 [16, 16], P('dp', 'slab'), may hold values from 5 to 10, as said below
- weight_one: bfloat16 [6912, 256], replicated, may hold values from -0.078125 to 0.078125
- weight_two: bfloat16 [6912, 256], replicated, may hold values from -0.078125 to 0.078125
Outputs:
- output: bfloat16 [16, 160, 64, 256], P('dp', 'slab')
- grad_features: bfloat16 [16, 160, 64, 256], P('dp', 'slab')
- grad_one: float32 [6912, 256], P('slab', 'dp')
- grad_two: float32 [6912, 256], P('slab', 'dp')
The draws below stay inside these ranges and needn't reach their ends.
Inputs may be any that keep to these rules, and one draw needn't show every extreme that they name: `neighbour_table`: row b of slab l = b // 10 lists where the block at each of the 27 block offsets lies, in the numbering of the gathered step; rows of padding slots hold only 14. The relation is symmetric: a block that names another at an offset is named by it at the opposite offset. `send_lists`: list 0 of a slab names, in increasing order, its occupied blocks in its first block-plane, the ones the previous slab can touch; list 1 those of its last block-plane; 10 fills the remaining slots. `block_counts`: slots at and above a slab's count are padding.
All inputs are finite; a program needn't handle non-finite values.
Results may differ from the reference program's by a relative error of at most 0.013.
Values may be sent and summed in bfloat16 or wider, within the bound.
A program may use at most 128 MiB of HBM per device.

```python
import math
import jax
import jax.numpy as jnp
from jax import lax

WIDTH = 256
GRID_X = 5
GRID_Y = 2
GRID_Z = 2
SLAB_BLOCKS = 10
EDGE = 2
TAPS_IN = 6912
SCENES = 16
SLABS = 16
BLOCKS = 160


def slab_layout(key, filled, sparse):
    plane_size = GRID_Y * GRID_Z
    plane_half = plane_size // 2
    key_counts, key_order = jax.random.split(key)
    per_plane = jax.random.randint(key_counts, (GRID_X,), 1, plane_half + 1).astype(jnp.int32)
    per_plane = jnp.where(sparse, per_plane.at[0].set(1), per_plane)
    per_plane = jnp.where(filled, jnp.full((GRID_X,), plane_half, jnp.int32), per_plane)

    def order_of(sub_key):
        return jax.random.permutation(sub_key, plane_size)
    orders = jax.vmap(order_of)(jax.random.split(key_order, GRID_X))
    ranking = jnp.argsort(orders, axis=1)
    occupied = ranking < per_plane[:, None]
    marked = occupied.reshape(-1).astype(jnp.int32)
    running = (jnp.cumsum(marked) - 1).astype(jnp.int32)
    index_of = jnp.where(marked > 0, running, -1).astype(jnp.int32)
    first_rank = (jnp.cumsum(occupied[0].astype(jnp.int32)) - 1).astype(jnp.int32)
    last_rank = (jnp.cumsum(occupied[GRID_X - 1].astype(jnp.int32)) - 1).astype(jnp.int32)
    places = jnp.arange(plane_size)
    list_first = jnp.full((EDGE + 1,), SLAB_BLOCKS, jnp.int32).at[jnp.where(occupied[0], first_rank, EDGE)].set(index_of[places])[:EDGE]
    list_last = jnp.full((EDGE + 1,), SLAB_BLOCKS, jnp.int32).at[jnp.where(occupied[GRID_X - 1], last_rank, EDGE)].set(index_of[(GRID_X - 1) * plane_size + places])[:EDGE]
    position = jnp.zeros((SLAB_BLOCKS + 1,), jnp.int32).at[jnp.where(marked > 0, running, SLAB_BLOCKS)].set(jnp.arange(GRID_X * plane_size, dtype=jnp.int32))[:SLAB_BLOCKS]
    filled_count = jnp.sum(marked).astype(jnp.int32)
    return (occupied, index_of, first_rank, last_rank, jnp.stack([list_first, list_last]), position, filled_count)


def slab_table(mine, before, after, has_before, has_after):
    plane_size = GRID_Y * GRID_Z
    index_of = mine[1]
    position = mine[5]
    filled_count = mine[6]
    offsets = jnp.arange(27)
    step_x = offsets // 9 - 1
    step_y = offsets // 3 % 3 - 1
    step_z = offsets % 3 - 1
    cell_x = position // plane_size
    cell_y = position % plane_size // GRID_Z
    cell_z = position % GRID_Z
    near_x = cell_x[:, None] + step_x[None, :]
    near_y = cell_y[:, None] + step_y[None, :]
    near_z = cell_z[:, None] + step_z[None, :]
    inside = (near_y >= 0) & (near_y < GRID_Y) & (near_z >= 0) & (near_z < GRID_Z)
    place = jnp.clip(near_y, 0, GRID_Y - 1) * GRID_Z + jnp.clip(near_z, 0, GRID_Z - 1)
    local_value = index_of[jnp.clip(near_x, 0, GRID_X - 1) * plane_size + place]
    is_local = (near_x >= 0) & (near_x < GRID_X) & (local_value >= 0)
    from_before = (near_x == -1) & has_before & before[0][GRID_X - 1][place]
    from_after = (near_x == GRID_X) & has_after & after[0][0][place]
    nothing = SLAB_BLOCKS + 2 * EDGE
    result = jnp.where(inside & is_local, local_value, jnp.where(inside & from_before, SLAB_BLOCKS + before[3][place], jnp.where(inside & from_after, SLAB_BLOCKS + EDGE + after[2][place], nothing)))
    live = jnp.arange(SLAB_BLOCKS)[:, None] < filled_count
    return jnp.where(live, result, nothing).astype(jnp.int32)


def geometry(key):
    base = jax.random.fold_in(key, 4321)

    def one_scene(scene_id):
        scene_key = jax.random.fold_in(base, scene_id)
        chosen = jax.random.randint(jax.random.fold_in(scene_key, 0), (), 0, SLABS)
        slab_ids = jnp.arange(SLABS)

        def layout_of(slab_id):
            return slab_layout(jax.random.fold_in(scene_key, slab_id + 1), slab_id == chosen, slab_id == (chosen + 1) % SLABS)
        layouts = jax.vmap(layout_of)(slab_ids)
        before = jax.tree.map(lambda leaf: jnp.roll(leaf, 1, axis=0), layouts)
        after = jax.tree.map(lambda leaf: jnp.roll(leaf, -1, axis=0), layouts)
        tables = jax.vmap(slab_table)(layouts, before, after, slab_ids > 0, slab_ids < SLABS - 1)
        return (layouts[6], tables, layouts[4])
    return jax.vmap(one_scene)(jnp.arange(SCENES))


def draw_neighbour_table(key, part):
    counts, tables, lists = geometry(key)
    return tables.reshape(SCENES, BLOCKS, 27).astype(jnp.int32)


def draw_send_lists(key, part):
    counts, tables, lists = geometry(key)
    return lists.astype(jnp.int32)


def draw_block_counts(key, part):
    counts, tables, lists = geometry(key)
    return counts.astype(jnp.int32)


def spiked(entries, stream_key, source, target, blocks, factor):
    owner, partner = [(jnp.arange(entries.shape[axis_at]) // (entries.shape[axis_at] // blocks)).reshape([-1 if axis == axis_at else 1 for axis in range(entries.ndim)]) for axis_at in (source, target)]
    chosen = jax.random.permutation(stream_key, blocks)[partner]
    strong = (owner == chosen) | (owner == (partner + blocks // 2) % blocks)
    return jnp.where(strong, factor * entries, entries)


def level_of(rng, shape, shards, low, top_value):
    def one(axis_at, shards_of):
        heights = jax.random.uniform(jax.random.fold_in(jax.random.fold_in(rng, 6), axis_at), (shards_of,), jnp.float32, low / len(shards), top_value / len(shards))
        return jnp.repeat(jnp.exp(heights), shape[axis_at] // shards_of).reshape((-1,) + (1,) * (len(shape) - axis_at - 1))

    gain = one(*shards[0])
    for cut in shards[1:]:
        gain = gain * one(*cut)
    return gain


def normal_values(rng, dims, deviation, reach, cuts=(), held_as=jnp.bfloat16):
    drawn = deviation * jax.random.normal(rng, dims, jnp.float32)
    if cuts:
        drawn = drawn * level_of(rng, dims, cuts, -0.22, 0.18)
    return jnp.clip(drawn, -reach, reach).astype(held_as)


def gaussian_with(rng, shape, spread, bound, cuts, heavy, kind=jnp.bfloat16):
    array = spread * jax.random.normal(rng, shape, jnp.float32)
    if cuts:
        array = array * level_of(rng, shape, cuts, -0.22, 0.18)
    return jnp.clip(spiked(array, jax.random.fold_in(rng, 3), *heavy), -bound, bound).astype(kind)


def setup_inputs(seed: int = 0) -> dict:
    arg_keys = jax.random.split(jax.random.key(seed), 8)
    return {
        "features": normal_values(arg_keys[0], (SCENES, BLOCKS, 64, WIDTH), 1.0, 6.0, ((0, 16), (1, 16))),
        "cotangent": gaussian_with(arg_keys[1], (SCENES, BLOCKS, 64, WIDTH), 1.0, 6.0, ((0, 16), (1, 16)), (0, 3, 16, 2.0)),
        "neighbour_table": draw_neighbour_table(jax.random.fold_in(arg_keys[7], 71), 0),
        "send_lists": draw_send_lists(jax.random.fold_in(arg_keys[7], 71), 0),
        "block_counts": draw_block_counts(jax.random.fold_in(arg_keys[7], 71), 0),
        "weight_one": normal_values(arg_keys[5], (TAPS_IN, WIDTH), TAPS_IN ** -0.5, 0.078125),
        "weight_two": normal_values(arg_keys[6], (TAPS_IN, WIDTH), TAPS_IN ** -0.5, 0.078125),
    }


OFFSET_LIST = [(along_x, along_y, along_z) for along_x in range(3) for along_y in range(3) for along_z in range(3)]

def columns(extended, lookup):
    blocks = lookup.shape[0]
    channels = extended.shape[-1]
    nearby = extended[lookup].reshape(blocks, 3, 3, 3, 4, 4, 4, channels)
    nearby = nearby.transpose(0, 1, 4, 2, 5, 3, 6, 7).reshape(blocks, 12, 12, 12, channels)
    window = nearby[:, 3:9, 3:9, 3:9]
    pieces = [window[:, along_x:along_x + 4, along_y:along_y + 4, along_z:along_z + 4].reshape(blocks * 64, channels) for along_x, along_y, along_z in OFFSET_LIST]
    return jnp.concatenate(pieces, axis=1)

def flipped(weight):
    channels = weight.shape[1]
    return jnp.transpose(weight.reshape(27, channels, channels)[::-1], (0, 2, 1)).reshape(27 * channels, channels)

def extend_all(source, edge_lists):
    slabs = source.shape[0]
    channels = source.shape[-1]
    edges = edge_lists.shape[-1]
    zero_one = jnp.zeros((slabs, 1, 64, channels), source.dtype)
    padded = jnp.concatenate([source, zero_one], axis=1)

    def pick(slab_rows, slab_lists):
        return slab_rows[slab_lists]
    picked = jax.vmap(pick)(padded, edge_lists)
    empty_edge = jnp.zeros((1, edges, 64, channels), source.dtype)
    from_prev = jnp.concatenate([empty_edge, picked[:-1, 1]], axis=0)
    from_next = jnp.concatenate([picked[1:, 0], empty_edge], axis=0)
    return jnp.concatenate([source, from_prev, from_next, zero_one], axis=1)

def reference(features, cotangent, neighbour_table, send_lists, block_counts, weight_one, weight_two):
    width_all = weight_one.shape[0]
    channels = weight_one.shape[1]
    contract = (((0,), (0,)), ((), ()))

    def scene_pass(totals, scene):
        scene_feat, scene_cot, lookup, edge_lists, counts = scene
        slabs = edge_lists.shape[0]
        blocks = scene_feat.shape[0] // slabs
        present = (jnp.arange(blocks)[None, :] < counts[:, None]).astype(jnp.float32)[:, :, None, None]
        masked = (scene_feat.reshape(slabs, blocks, 64, channels).astype(jnp.float32) * present).astype(jnp.bfloat16)
        upstream = scene_cot.reshape(slabs, blocks, 64, channels)
        lookups = lookup.reshape(slabs, blocks, 27)

        def gathered(source):
            extended = extend_all(source, edge_lists)
            return jax.vmap(columns)(extended, lookups).reshape(slabs * blocks * 64, 27 * channels)
        cols_in = gathered(masked)
        pre_one = jnp.dot(cols_in, weight_one, preferred_element_type=jnp.float32)
        hidden = jnp.maximum(pre_one, 0.0).astype(jnp.bfloat16)
        cols_hidden = gathered(hidden.reshape(slabs, blocks, 64, channels))
        pre_two = jnp.dot(cols_hidden, weight_two, preferred_element_type=jnp.float32)
        output = (pre_two + masked.reshape(-1, channels).astype(jnp.float32)).astype(jnp.bfloat16)
        back_hidden = jnp.dot(gathered(upstream), flipped(weight_two), preferred_element_type=jnp.float32)
        grad_hidden = jnp.where(hidden > 0, back_hidden, 0.0).astype(jnp.bfloat16)
        back_in = jnp.dot(gathered(grad_hidden.reshape(slabs, blocks, 64, channels)), flipped(weight_one), preferred_element_type=jnp.float32)
        rows_present = jnp.broadcast_to(present, (slabs, blocks, 64, 1)).reshape(-1, 1)
        upstream_rows = upstream.reshape(-1, channels)
        grad_features = ((upstream_rows.astype(jnp.float32) + back_in) * rows_present).astype(jnp.bfloat16)
        sum_two = lax.dot_general(cols_hidden, upstream_rows, contract, preferred_element_type=jnp.float32)
        sum_one = lax.dot_general(cols_in, grad_hidden, contract, preferred_element_type=jnp.float32)
        shaped = (output.reshape(slabs * blocks, 64, channels), grad_features.reshape(slabs * blocks, 64, channels))
        return ((totals[0] + sum_one, totals[1] + sum_two), shaped)
    empty_sum = jnp.zeros((width_all, channels), jnp.float32)
    totals, results = lax.scan(scene_pass, (empty_sum, empty_sum), (features, cotangent, neighbour_table, send_lists, block_counts))
    factor = 1.0 / math.sqrt(SCENES * SLABS * SLAB_BLOCKS * 64)
    return (results[0], results[1], totals[0] * factor, totals[1] * factor)
```

```python
import math

import jax
import jax.numpy as jnp
from jax import lax
from jax.experimental import pallas as pl
from jax.experimental.pallas import tpu as pltpu
from jax.sharding import PartitionSpec as P

F32 = jnp.float32
BF16 = jnp.bfloat16
MESH = pl.DeviceIdType.MESH
ROWS = 160
C = 256
NT = (((1,), (1,)), ((), ()))
TN = (((0,), (0,)), ((), ()))


def dot(a, b, dims=(((1,), (0,)), ((), ()))):
    return lax.dot_general(a, b, dims, preferred_element_type=F32)


def kernel(
    factor,
    counts, lists, table_ref, feat_ref, cot_ref, w1_hbm, w2_hbm,
    out_ref, gf_ref, g1_ref, g2_ref,
    w1, w2, nat, t_own, t_ext, pack, hrecv, t_own2, pack2, hrecv2, sel, win, acc_a, acc_b,
    hid_t, psend, precv, xy, recv_a, recv_b, sum_a, sum_b, recv_a2, recv_b2, zsend, zrecv, fin_t, fin_recv,
    wsem, hs, hr, ps, pr, as_, ar, bs, br, a2s, a2r, b2s, b2r, zs, zr, fs, fr,
):
    dp = lax.axis_index("dp")
    slab = lax.axis_index("slab")
    core = dp % 2
    y = dp // 2 % 4
    z_hi = dp // 8
    x = slab % 4
    z_lo = slab // 4
    z = z_hi * 4 + z_lo

    def dev(x_=x, y_=y, z_=z, core_=core):
        return ((z_ // 4) * 8 + y_ * 2 + core_, (z_ % 4) * 4 + x_)

    after = (slab + 1) % 16
    before = (slab + 15) % 16
    peer = dev(core_=1 - core)
    x_peers = [dev(x_=(x + d) % 4) for d in range(1, 4)]
    y_peers = [dev(y_=(y + d) % 4) for d in range(1, 4)]
    z_peers = [dev(z_=(z + d) % 8) for d in range(1, 8)]
    yc = y * 2 + core
    f_peers = [dev(y_=(yc + d) % 8 // 2, core_=(yc + d) % 2) for d in range(1, 8)]

    barrier = pltpu.get_barrier_semaphore()
    everyone = [(dp, after), (dp, before), peer] + x_peers + y_peers + z_peers + f_peers
    for d in everyone:
        pl.semaphore_signal(barrier, inc=1, device_id=d, device_id_type=MESH)

    load_w1 = pltpu.make_async_copy(w1_hbm, w1, wsem.at[0])
    load_w2 = pltpu.make_async_copy(w2_hbm, w2, wsem.at[1])
    load_w1.start()
    load_w2.start()

    def remote(src, dst, send, recv, to):
        return pltpu.make_async_remote_copy(
            src_ref=src, dst_ref=dst, send_sem=send, recv_sem=recv, device_id=to, device_id_type=MESH
        )

    row = lax.broadcasted_iota(jnp.int32, (640, 1), 0)
    present = jnp.where(row < counts[0, 0] * 64, 1.0, 0.0)
    for part, value in (
        (0, feat_ref[...].reshape(640, C).astype(F32) * present),
        (2, cot_ref[...].reshape(640, C).astype(F32)),
    ):
        nat[part], nat[part + 1] = value[:, 0:128], value[:, 128:]
    for k in range(4):
        part = jnp.concatenate([nat[n, pl.ds(k, ROWS, stride=4), :] for n in range(4)], axis=1)
        part = part.astype(BF16).reshape(10, 16, 2 * C)
        t_own[:, k] = part
        t_ext[0:10, k] = part

    def pack_edges(source, target):
        for side in range(2):
            inside = jnp.where(side == 0, slab > 0, slab < 15)
            for q in range(2):
                named = lists[side, q]
                keep = jnp.where(inside & (named < 10), 1.0, 0.0).astype(BF16)
                target[side, q] = source[jnp.minimum(named, 9)] * keep

    def halo(source, target, e):
        return (
            remote(source.at[1], target.at[0], hs.at[e, 0], hr.at[e, 0], (dp, after)),
            remote(source.at[0], target.at[1], hs.at[e, 1], hr.at[e, 1], (dp, before)),
        )

    pack_edges(t_own, pack)
    pl.semaphore_wait(barrier, len(everyone))
    first = halo(pack, hrecv, 0)
    for copy in first:
        copy.start()

    r = lax.broadcasted_iota(jnp.int32, (ROWS, 1), 0)
    spread = (r // 16 == lax.broadcasted_iota(jnp.int32, (ROWS, 10), 1)).astype(F32)
    rows_of = dot(spread, table_ref[...].astype(F32))
    i_of, j_of = r // 4 % 4, r % 4
    lane = lax.broadcasted_iota(jnp.int32, (ROWS, 224), 1)

    def options(position, step):
        if step == 0:
            return [(0, position == 0), (1, position > 0)]
        if step == 1:
            return [(1, None)]
        return [(1, position < 3), (2, position == 3)]

    for dx in range(3):
        for dy in range(3):
            spot = (i_of + dx + 3) % 4 * 4 + (j_of + dy + 3) % 4
            for bz in range(3):
                block = None
                for bx, cond_x in options(i_of, dx):
                    for by, cond_y in options(j_of, dy):
                        n = 9 * bx + 3 * by + bz
                        value = rows_of[:, n : n + 1]
                        cond = cond_x if cond_y is None else cond_y if cond_x is None else cond_x & cond_y
                        block = value if block is None else jnp.where(cond, value, block)
                source = block.astype(jnp.int32) * 16 + spot
                sel[dx * 3 + dy, bz] = jnp.where(lane == source, 1.0, 0.0).astype(BF16)

    def finish_halo(copies, received, ext):
        for copy in copies:
            copy.wait_recv()
        ext[10:14] = received[...].reshape(4, 4, 16, 2 * C)

    def build(ext):
        def one(g, carry):
            for spot in range(6):
                k = (spot + 3) % 4
                bz = 0 if spot == 0 else 2 if spot == 5 else 1
                win[g, spot] = dot(sel[g, bz], ext[:, k].reshape(224, 2 * C)).astype(BF16)
            return carry

        lax.fori_loop(0, 9, one, 0)

    def view(g, dz, low):
        return win[g, dz : dz + 4, :, low : low + C].reshape(640, C)

    def convolve(w_fwd, w_bwd):
        acc_a[...] = jnp.zeros_like(acc_a)
        acc_b[...] = jnp.zeros_like(acc_b)

        def one(g, carry):
            left = jnp.concatenate([view(g, dz, 0) for dz in range(3)], axis=1)
            acc_a[...] += dot(left, w_fwd[g].reshape(3 * C, C))
            left = jnp.concatenate([view(g, dz, C) for dz in range(3)], axis=1)
            right = jnp.concatenate([w_bwd[8 - g, 2 - dz] for dz in range(3)], axis=1)
            acc_b[...] += dot(left, right, NT)
            return carry

        lax.fori_loop(0, 9, one, 0)

    load_w1.wait()
    load_w2.wait()
    finish_halo(first, hrecv, t_ext)
    build(t_ext)
    convolve(w1, w2)

    hidden = jnp.maximum(acc_a[...], 0.0)
    rounded = hidden.astype(BF16)
    grad_hidden = jnp.where(rounded > 0, acc_b[...].astype(BF16), jnp.zeros((), BF16))
    hid_t[...] = hidden.T.astype(BF16)
    for k in range(4):
        rows = slice(k * ROWS, (k + 1) * ROWS)
        t_own2[:, k, :, 0:C] = rounded[rows].reshape(10, 16, C)
        t_own2[:, k, :, C:] = grad_hidden[rows].reshape(10, 16, C)
        t_ext[0:10, k, :, 0:C] = rounded[rows].reshape(10, 16, C)
        t_ext[0:10, k, :, C:] = grad_hidden[rows].reshape(10, 16, C)
    pack_edges(t_own2, pack2)
    second = halo(pack2, hrecv2, 1)
    for copy in second:
        copy.start()

    def to_peer(g):
        part = pl.ds(pl.multiple_of(g * 768, 768), 768)
        return remote(psend.at[part], precv.at[part], ps.at[g], pr.at[g], peer)

    gh_rows = jnp.concatenate([t_own2[:, k, :, C:].reshape(ROWS, C) for k in range(4)], axis=0)

    def grads(g, carry):
        for dz in range(3):
            one = dot(view(g, dz, 0), gh_rows, TN)
            two = dot(hid_t[...], view(8 - g, 2 - dz, C))
            rows = pl.ds(pl.multiple_of(g * 768 + dz * 256, 256), 256)
            xy[rows] = jnp.where(core == 0, one, two).astype(BF16)
            psend[rows] = jnp.where(core == 0, two, one).astype(BF16)
        to_peer(g).start()
        return carry

    lax.fori_loop(0, 9, grads, 0)
    xy[6912:6928] = jnp.zeros((16, C), BF16)

    def join(g, carry):
        to_peer(g).wait_recv()
        for dz in range(3):
            rows = pl.ds(pl.multiple_of(g * 768 + dz * 256, 256), 256)
            xy[rows] = (xy[rows].astype(F32) + precv[rows].astype(F32)).astype(BF16)
        return carry

    lax.fori_loop(0, 9, join, 0)

    def rows_at(start, size):
        return pl.ds(pl.multiple_of(start, 16), size)

    def copy_a(d, zl):
        where = rows_at(432 * (zl * 4 + (x + d) % 4), 432)
        return remote(xy.at[where], recv_a.at[d - 1, zl], as_.at[d - 1, zl], ar.at[d - 1, zl], x_peers[d - 1])

    def copy_b(d, s):
        where = rows_at(432 * (8 + s) + 112 * ((y + d) % 4), 112)
        return remote(xy.at[where], recv_b.at[d - 1, s], bs.at[d - 1, s], br.at[d - 1, s], y_peers[d - 1])

    stage_a = [copy_a(d, zl) for d in (2, 1, 3) for zl in range(2)]
    stage_b = [copy_b(d, s) for d in (2, 1, 3) for s in range(8)]
    for copy in stage_a + stage_b:
        copy.start()

    finish_halo(second, hrecv2, t_ext)
    build(t_ext)
    convolve(w2, w1)
    for k in range(4):
        rows = slice(k * ROWS, (k + 1) * ROWS)
        for n, acc in enumerate((acc_a, acc_b)):
            for half in range(2):
                nat[2 * n + half, pl.ds(k, ROWS, stride=4), :] = acc[rows, half * 128 : half * 128 + 128]
    masked = feat_ref[...].reshape(640, C).astype(F32) * present
    out_ref[...] = (jnp.concatenate([nat[0], nat[1]], axis=1) + masked).astype(BF16).reshape(10, 64, C)
    upstream = cot_ref[...].reshape(640, C).astype(F32)
    gf_ref[...] = ((upstream + jnp.concatenate([nat[2], nat[3]], axis=1)) * present).astype(BF16).reshape(10, 64, C)

    def total(parts):
        value = parts[0].astype(F32)
        for part in parts[1:]:
            value = value + part.astype(F32)
        return value

    for copy in stage_a:
        copy.wait_recv()

    def add_a(n, carry):
        zl, third = n // 3, n % 3
        inner = rows_at(third * 144, 144)
        own = xy[rows_at(432 * (zl * 4 + x) + third * 144, 144)]
        sum_a[zl, inner] = total([own] + [recv_a[d, zl, inner] for d in range(3)]).astype(BF16)
        return carry

    lax.fori_loop(0, 6, add_a, 0)
    for zl in range(2):
        sum_a[zl, 432:448] = jnp.zeros((16, C), BF16)
    stage_a2 = [
        remote(
            sum_a.at[:, rows_at(112 * ((y + d) % 4), 112)], recv_a2.at[d - 1], a2s.at[d - 1], a2r.at[d - 1], y_peers[d - 1]
        )
        for d in (2, 1, 3)
    ]
    for copy in stage_a2:
        copy.start()

    for copy in stage_b:
        copy.wait_recv()

    def add_b(s, carry):
        own = xy[rows_at(432 * (8 + s) + 112 * y, 112)]
        sum_b[s // 4, s % 4] = total([own] + [recv_b[d, s] for d in range(3)]).astype(BF16)
        return carry

    lax.fori_loop(0, 8, add_b, 0)
    stage_b2 = [
        remote(sum_b.at[:, (x + d) % 4], recv_b2.at[d - 1], b2s.at[d - 1], b2r.at[d - 1], x_peers[d - 1])
        for d in (2, 1, 3)
    ]
    for copy in stage_b2:
        copy.start()

    for copy in stage_a2:
        copy.wait_recv()
    for zl in range(2):
        own = sum_a[zl, rows_at(112 * y, 112)]
        full = total([own] + [recv_a2[d, zl] for d in range(3)]).astype(BF16)
        zsend[0, zl], zsend[1, zl] = full[:, 0:128], full[:, 128:]
    for copy in stage_b2:
        copy.wait_recv()
    for zl in range(2):
        own = sum_b[zl, x]
        full = total([own] + [recv_b2[d, zl] for d in range(3)]).astype(BF16)
        zsend[0, 2 + zl], zsend[1, 2 + zl] = full[:, 0:128], full[:, 128:]

    stage_z = []
    for d in (4, 3, 5, 2, 6, 1, 7):
        to = (z + d) % 8
        stage_z.append(remote(zsend.at[to // 4, to % 4], zrecv.at[d - 1], zs.at[d - 1], zr.at[d - 1], z_peers[d - 1]))
    for copy in stage_z:
        copy.start()
    for copy in stage_z:
        copy.wait_recv()
    whole = total([zsend[z_hi, z_lo]] + [zrecv[d] for d in range(7)]) * factor
    padded = jnp.concatenate([whole, jnp.zeros((16, 128), F32)], axis=0)
    fin_t[...] = padded.T.reshape(8, 16, 128)

    stage_f = []
    for d in range(1, 8):
        to = (yc + d) % 8
        stage_f.append(remote(fin_t.at[to], fin_recv.at[d - 1], fs.at[d - 1], fr.at[d - 1], f_peers[d - 1]))
    for copy in stage_f:
        copy.start()
    for copy in stage_f:
        copy.wait_recv()

    def place(value, source):
        part = value.T[0:112]
        for src_core, target in ((0, g1_ref), (1, g2_ref)):
            for src_y in range(4):
                size = 112 if src_y < 3 else 96

                @pl.when(source == src_y * 2 + src_core)
                def _():
                    target[112 * src_y : 112 * src_y + size] = part[0:size]

    place(fin_t[yc], yc)
    for d in range(1, 8):
        place(fin_recv[d - 1], (yc + 8 - d) % 8)

    for copy in list(first) + list(second) + stage_a + stage_b + stage_a2 + stage_b2 + stage_z + stage_f:
        copy.wait_send()

    def drain(g, carry):
        to_peer(g).wait_send()
        return carry

    lax.fori_loop(0, 9, drain, 0)


def per_device(features, cotangent, neighbour_table, send_lists, block_counts, weight_one, weight_two):
    factor = 1.0 / math.sqrt(lax.axis_size("dp") * lax.axis_size("slab") * 10 * 64)
    smem = pl.BlockSpec(memory_space=pltpu.SMEM)
    vmem = pl.BlockSpec(memory_space=pltpu.VMEM)
    hbm = pl.BlockSpec(memory_space=pl.ANY)
    dma = pltpu.SemaphoreType.DMA
    outs = pl.pallas_call(
        lambda *refs: kernel(factor, *refs),
        out_shape=(
            jax.ShapeDtypeStruct((10, 64, C), BF16),
            jax.ShapeDtypeStruct((10, 64, C), BF16),
            jax.ShapeDtypeStruct((432, 16), F32),
            jax.ShapeDtypeStruct((432, 16), F32),
        ),
        in_specs=[smem, smem, vmem, vmem, vmem, hbm, hbm],
        out_specs=(vmem, vmem, vmem, vmem),
        scratch_shapes=[
            pltpu.VMEM((9, 3, C, C), BF16),
            pltpu.VMEM((9, 3, C, C), BF16),
            pltpu.VMEM((4, 640, 128), F32),
            pltpu.VMEM((10, 4, 16, 2 * C), BF16),
            pltpu.VMEM((14, 4, 16, 2 * C), BF16),
            pltpu.VMEM((2, 2, 4, 16, 2 * C), BF16),
            pltpu.VMEM((2, 2, 4, 16, 2 * C), BF16),
            pltpu.VMEM((10, 4, 16, 2 * C), BF16),
            pltpu.VMEM((2, 2, 4, 16, 2 * C), BF16),
            pltpu.VMEM((2, 2, 4, 16, 2 * C), BF16),
            pltpu.VMEM((9, 3, ROWS, 224), BF16),
            pltpu.VMEM((9, 6, ROWS, 2 * C), BF16),
            pltpu.VMEM((640, C), F32),
            pltpu.VMEM((640, C), F32),
            pltpu.VMEM((C, 640), BF16),
            pltpu.VMEM((6912, C), BF16),
            pltpu.VMEM((6912, C), BF16),
            pltpu.VMEM((6928, C), BF16),
            pltpu.VMEM((3, 2, 432, C), BF16),
            pltpu.VMEM((3, 8, 112, C), BF16),
            pltpu.VMEM((2, 448, C), BF16),
            pltpu.VMEM((2, 4, 112, C), BF16),
            pltpu.VMEM((3, 2, 112, C), BF16),
            pltpu.VMEM((3, 2, 112, C), BF16),
            pltpu.VMEM((2, 4, 112, 128), BF16),
            pltpu.VMEM((7, 112, 128), BF16),
            pltpu.VMEM((8, 16, 128), F32),
            pltpu.VMEM((7, 16, 128), F32),
            dma((2,)),
            dma((2, 2)),
            dma((2, 2)),
            dma((9,)),
            dma((9,)),
            dma((3, 2)),
            dma((3, 2)),
            dma((3, 8)),
            dma((3, 8)),
            dma((3,)),
            dma((3,)),
            dma((3,)),
            dma((3,)),
            dma((7,)),
            dma((7,)),
            dma((7,)),
            dma((7,)),
        ],
        compiler_params=pltpu.CompilerParams(
            collective_id=0, has_side_effects=True, vmem_limit_bytes=60 * 1024 * 1024
        ),
        name="step",
    )(
        block_counts,
        send_lists[0, 0],
        neighbour_table[0],
        features[0],
        cotangent[0],
        weight_one.reshape(9, 3, C, C),
        weight_two.reshape(9, 3, C, C),
    )
    return (outs[0][None], outs[1][None], outs[2], outs[3])


def solution(mesh):
    in_specs = (
        P("dp", "slab", None, None),
        P("dp", "slab", None, None),
        P("dp", "slab", None),
        P("dp", "slab", None, None),
        P("dp", "slab"),
        P(),
        P(),
    )
    out_specs = (
        P("dp", "slab", None, None),
        P("dp", "slab", None, None),
        P("slab", "dp"),
        P("slab", "dp"),
    )
    return jax.shard_map(
        per_device, mesh=mesh, in_specs=in_specs, out_specs=out_specs, check_vma=False
    )
```

```python
import math

import jax
import jax.numpy as jnp
from jax import lax
from jax.experimental import pallas as pl
from jax.experimental.pallas import tpu as pltpu
from jax.sharding import PartitionSpec as P

F32 = jnp.float32
BF16 = jnp.bfloat16
MESH = pl.DeviceIdType.MESH
ROWS = 160
REACH = 176
C = 256
NT = (((1,), (1,)), ((), ()))
TN = (((0,), (0,)), ((), ()))


def dot(a, b, dims=(((1,), (0,)), ((), ()))):
    return lax.dot_general(a, b, dims, preferred_element_type=F32)


def kernel(
    factor,
    counts, lists, table_ref, feat_hbm, cot_hbm, w1_hbm, w2_hbm,
    out_hbm, gf_hbm, fin_ref,
    w1, w2, feat, cot, out_v, gf_v, nat, t_own, t_ext, pack, hrecv, t_own2, pack2, hrecv2, sel, win, acc_a, acc_b,
    hid_t, psend, precv, xy, relay_a, direct_a, summed_a, stage_a, relay_b, direct_b, summed_b, stage_b,
    sum_a, sum_b, recv_a2, recv_b2, zsend, zrecv, fin_t, fin_recv,
    lsem, osem, hs, hr, ps, pr, as_, ar, bs, br, a2s, a2r, b2s, b2r, zs, zr, fs, fr,
):
    dp = lax.axis_index("dp")
    slab = lax.axis_index("slab")
    core = dp % 2
    y = dp // 2 % 4
    z_hi = dp // 8
    x = slab % 4
    z_lo = slab // 4
    z = z_hi * 4 + z_lo

    def dev(x_=x, y_=y, z_=z, core_=core):
        return ((z_ // 4) * 8 + y_ * 2 + core_, (z_ % 4) * 4 + x_)

    after = (slab + 1) % 16
    before = (slab + 15) % 16
    peer = dev(core_=1 - core)
    x_peers = [dev(x_=(x + d) % 4) for d in range(1, 4)]
    y_peers = [dev(y_=(y + d) % 4) for d in range(1, 4)]
    z_peers = [dev(z_=(z + d) % 8) for d in range(1, 8)]
    yc = y * 2 + core
    f_peers = [dev(y_=(yc + d) % 8 // 2, core_=(yc + d) % 2) for d in range(1, 8)]

    barrier = pltpu.get_barrier_semaphore()
    everyone = [(dp, after), (dp, before), peer] + x_peers + y_peers + z_peers + f_peers
    for d in everyone:
        pl.semaphore_signal(barrier, inc=1, device_id=d, device_id_type=MESH)

    loads = [
        pltpu.make_async_copy(source, target, lsem.at[n])
        for n, (source, target) in enumerate(((feat_hbm, feat), (cot_hbm, cot), (w1_hbm, w1), (w2_hbm, w2)))
    ]
    for load in loads:
        load.start()

    def remote(src, dst, send, recv, to):
        return pltpu.make_async_remote_copy(
            src_ref=src, dst_ref=dst, send_sem=send, recv_sem=recv, device_id=to, device_id_type=MESH
        )

    row = lax.broadcasted_iota(jnp.int32, (640, 1), 0)
    present = jnp.where(row < counts[0, 0] * 64, 1.0, 0.0)
    loads[0].wait()
    loads[1].wait()
    for part, value in (
        (0, feat[...].reshape(640, C).astype(F32) * present),
        (2, cot[...].reshape(640, C).astype(F32)),
    ):
        nat[part], nat[part + 1] = value[:, 0:128], value[:, 128:]
    for k in range(4):
        part = jnp.concatenate([nat[n, pl.ds(k, ROWS, stride=4), :] for n in range(4)], axis=1)
        part = part.astype(BF16).reshape(10, 16, 2 * C)
        t_own[:, k] = part
        t_ext[0:10, k] = part

    def pack_edges(source, target):
        for side in range(2):
            inside = jnp.where(side == 0, slab > 0, slab < 15)
            for q in range(2):
                named = lists[side, q]
                keep = jnp.where(inside & (named < 10), 1.0, 0.0)
                block = source[jnp.minimum(named, 9)].astype(F32) * keep
                plane = [block[k, 12 * side : 12 * side + 4] for k in range(4)]
                target[side, q] = jnp.concatenate(plane, axis=0).astype(BF16)

    def halo(source, target, e):
        return (
            remote(source.at[1], target.at[0], hs.at[e, 0], hr.at[e, 0], (dp, after)),
            remote(source.at[0], target.at[1], hs.at[e, 1], hr.at[e, 1], (dp, before)),
        )

    pack_edges(t_own, pack)
    pl.semaphore_wait(barrier, len(everyone))
    first = halo(pack, hrecv, 0)
    for copy in first:
        copy.start()

    r = lax.broadcasted_iota(jnp.int32, (ROWS, 1), 0)
    spread = (r // 16 == lax.broadcasted_iota(jnp.int32, (ROWS, 10), 1)).astype(F32)
    rows_of = dot(spread, table_ref[...].reshape(10, 27).astype(F32))
    i_of, j_of = r // 4 % 4, r % 4
    lane = lax.broadcasted_iota(jnp.int32, (ROWS, REACH), 1)

    def options(position, step):
        if step == 0:
            return [(0, position == 0), (1, position > 0)]
        if step == 1:
            return [(1, None)]
        return [(1, position < 3), (2, position == 3)]

    for dx in range(3):
        for dy in range(3):
            spot_j = (j_of + dy + 3) % 4
            spot = (i_of + dx + 3) % 4 * 4 + spot_j
            for bz in range(3):
                block = None
                for bx, cond_x in options(i_of, dx):
                    for by, cond_y in options(j_of, dy):
                        n = 9 * bx + 3 * by + bz
                        value = rows_of[:, n : n + 1]
                        cond = cond_x if cond_y is None else cond_y if cond_x is None else cond_x & cond_y
                        block = value if block is None else jnp.where(cond, value, block)
                block = block.astype(jnp.int32)
                source = jnp.where(block < 10, block * 16 + spot, 160 + (block - 10) * 4 + spot_j)
                sel[dx * 3 + dy, bz] = jnp.where(lane == source, 1.0, 0.0).astype(BF16)

    def finish_halo(copies, received, ext):
        for copy in copies:
            copy.wait_recv()
        planes = [received[side, q].astype(F32) for side in range(2) for q in range(2)]
        for k in range(4):
            ext[10, k] = jnp.concatenate([plane[4 * k : 4 * k + 4] for plane in planes], axis=0).astype(BF16)

    def build(ext):
        def one(g, carry):
            for spot in range(6):
                k = (spot + 3) % 4
                bz = 0 if spot == 0 else 2 if spot == 5 else 1
                win[g, spot] = dot(sel[g, bz], ext[:, k].reshape(REACH, 2 * C)).astype(BF16)
            return carry

        lax.fori_loop(0, 9, one, 0)

    def view(g, dz, low):
        return win[g, pl.ds(dz, 4), :, low : low + C].reshape(640, C)

    def convolve(w_fwd, w_bwd, start, end):
        if start == 0:
            acc_a[...] = jnp.zeros_like(acc_a)
            acc_b[...] = jnp.zeros_like(acc_b)

        def one(g, carry):
            left = jnp.concatenate([view(g, dz, 0) for dz in range(3)], axis=1)
            acc_a[...] += dot(left, w_fwd[g].reshape(3 * C, C))
            left = jnp.concatenate([view(g, dz, C) for dz in range(3)], axis=1)
            right = jnp.concatenate([w_bwd[8 - g, 2 - dz] for dz in range(3)], axis=1)
            acc_b[...] += dot(left, right, NT)
            return carry

        lax.fori_loop(start, end, one, 0)

    finish_halo(first, hrecv, t_ext)
    build(t_ext)
    loads[2].wait()
    loads[3].wait()
    convolve(w1, w2, 0, 9)

    hidden = jnp.maximum(acc_a[...], 0.0)
    rounded = hidden.astype(BF16)
    grad_hidden = jnp.where(rounded > 0, acc_b[...].astype(BF16), jnp.zeros((), BF16))
    hid_t[...] = hidden.T.astype(BF16)
    for k in range(4):
        rows = slice(k * ROWS, (k + 1) * ROWS)
        t_own2[:, k, :, 0:C] = rounded[rows].reshape(10, 16, C)
        t_own2[:, k, :, C:] = grad_hidden[rows].reshape(10, 16, C)
        t_ext[0:10, k, :, 0:C] = rounded[rows].reshape(10, 16, C)
        t_ext[0:10, k, :, C:] = grad_hidden[rows].reshape(10, 16, C)
    pack_edges(t_own2, pack2)
    second = halo(pack2, hrecv2, 1)
    for copy in second:
        copy.start()

    def block_of(o):
        return pl.ds(pl.multiple_of(o * C, C), C)

    def to_peer(o):
        return remote(psend.at[block_of(o)], precv.at[block_of(o)], ps.at[o], pr.at[o], peer)

    gh_rows = jnp.concatenate([t_own2[:, k, :, C:].reshape(ROWS, C) for k in range(4)], axis=0)

    def grad_at(o):
        one = dot(view(o // 3, o % 3, 0), gh_rows, TN)
        two = dot(hid_t[...], view(8 - o // 3, 2 - o % 3, C))
        xy[block_of(o)] = jnp.where(core == 0, one, two).astype(BF16)
        psend[block_of(o)] = jnp.where(core == 0, two, one).astype(BF16)
        to_peer(o).start()

    def grads(n, carry):
        grad_at(n)
        grad_at(26 - n)
        return carry

    def join(o):
        to_peer(o).wait_recv()
        xy[block_of(o)] = (xy[block_of(o)].astype(F32) + precv[block_of(o)].astype(F32)).astype(BF16)

    def join_ends(n, carry):
        join(n)
        join(26 - n)
        return carry

    def join_middle(n, carry):
        join(n)
        return carry

    def rows_at(start, size):
        return pl.ds(pl.multiple_of(start, 16), size)

    def slab_rows(zl, owner_x):
        return rows_at(432 * (zl * 4 + owner_x), 432)

    def part_rows(zl, s, owner_y):
        return rows_at(432 * (zl * 4 + s) + 112 * owner_y, 112)

    LOW, HIGH = slice(0, 128), slice(128, 256)
    next_x, last_x, far_x = (x + 1) % 4, (x + 3) % 4, (x + 2) % 4
    next_y, last_y, far_y = (y + 1) % 4, (y + 3) % 4, (y + 2) % 4

    def first_copies(h):
        copies = {}
        for phase, (buf_a, buf_b) in enumerate(((relay_a, relay_b), (direct_a, direct_b))):
            for way in range(2):
                to_x, to_y = (x_peers[0], y_peers[0]) if way == 0 else (x_peers[2], y_peers[2])
                if phase == 0:
                    owner_x, owner_y, lanes = far_x, far_y, LOW if way == 0 else HIGH
                else:
                    owner_x, owner_y = (next_x, next_y) if way == 0 else (last_x, last_y)
                    lanes = HIGH if way == 0 else LOW
                copies[phase, way] = [
                    remote(
                        xy.at[slab_rows(h, owner_x), lanes], buf_a.at[h, way],
                        as_.at[h, phase, way], ar.at[h, phase, way], to_x,
                    )
                ] + [
                    remote(
                        xy.at[part_rows(3 - h, s, owner_y), lanes], buf_b.at[h, way, s],
                        bs.at[h, phase, way, s], br.at[h, phase, way, s], to_y,
                    )
                    for s in range(4)
                ]
        for way in range(2):
            to_x, to_y = (x_peers[0], y_peers[0]) if way == 0 else (x_peers[2], y_peers[2])
            copies[2, way] = [
                remote(stage_a.at[h, way], summed_a.at[h, way], as_.at[h, 2, way], ar.at[h, 2, way], to_x),
                remote(stage_b.at[h, way], summed_b.at[h, way], bs.at[h, 2, way, 0], br.at[h, 2, way, 0], to_y),
            ]
        return copies

    copies_of = [first_copies(0), first_copies(1)]

    def start_first(h):
        for phase in range(2):
            a0, b0 = copies_of[h][phase, 0], copies_of[h][phase, 1]
            for copy in [c for pair in zip(a0, b0) for c in pair]:
                copy.start()

    def total(*parts):
        value = parts[0].astype(F32)
        for part in parts[1:]:
            value = value + part.astype(F32)
        return value

    def pass_on(h):
        for way in range(2):
            for copy in copies_of[h][0, way]:
                copy.wait_recv()
        for way, lanes, owner_x, owner_y in ((0, LOW, next_x, next_y), (1, HIGH, last_x, last_y)):
            stage_a[h, way] = total(xy[slab_rows(h, owner_x), lanes], relay_a[h, way]).astype(BF16)
            for s in range(4):
                own = xy[part_rows(3 - h, s, owner_y), lanes]
                stage_b[h, way, s] = total(own, relay_b[h, way, s]).astype(BF16)
            for copy in copies_of[h][2, way]:
                copy.start()

    lax.fori_loop(0, 7, grads, 0)
    xy[6912:6928] = jnp.zeros((16, C), BF16)
    lax.fori_loop(7, 9, grads, 0)
    lax.fori_loop(0, 7, join_ends, 0)
    start_first(0)
    lax.fori_loop(9, 13, grads, 0)
    grad_at(13)
    lax.fori_loop(7, 20, join_middle, 0)
    start_first(1)

    finish_halo(second, hrecv2, t_ext)
    build(t_ext)
    pass_on(0)
    convolve(w2, w1, 0, 4)
    pass_on(1)
    convolve(w2, w1, 4, 9)
    for k in range(4):
        rows = slice(k * ROWS, (k + 1) * ROWS)
        for n, acc in enumerate((acc_a, acc_b)):
            for half in range(2):
                nat[2 * n + half, pl.ds(k, ROWS, stride=4), :] = acc[rows, half * 128 : half * 128 + 128]
    masked = feat[...].reshape(640, C).astype(F32) * present
    out_v[...] = (jnp.concatenate([nat[0], nat[1]], axis=1) + masked).astype(BF16).reshape(10, 64, C)
    upstream = cot[...].reshape(640, C).astype(F32)
    back = jnp.concatenate([nat[2], nat[3]], axis=1)
    gf_v[...] = ((upstream + back) * present).astype(BF16).reshape(10, 64, C)
    stores = [pltpu.make_async_copy(out_v, out_hbm, osem.at[0]), pltpu.make_async_copy(gf_v, gf_hbm, osem.at[1])]
    for store in stores:
        store.start()

    second_copies = []
    for h in range(2):
        to_y = [
            remote(
                sum_a.at[h, rows_at(112 * ((y + d) % 4), 112)], recv_a2.at[h, d - 1], a2s.at[h, d - 1], a2r.at[h, d - 1],
                y_peers[d - 1],
            )
            for d in (2, 1, 3)
        ]
        to_x = [
            remote(sum_b.at[h, (x + d) % 4], recv_b2.at[h, d - 1], b2s.at[h, d - 1], b2r.at[h, d - 1], x_peers[d - 1])
            for d in (2, 1, 3)
        ]
        second_copies.append((to_y, to_x))

    def end_first(h):
        for phase in (1, 2):
            for way in range(2):
                for copy in copies_of[h][phase, way]:
                    copy.wait_recv()
        for lanes, a, b, a_buf, b_buf in (
            (LOW, summed_a, direct_a, 0, 1),
            (HIGH, direct_a, summed_a, 0, 1),
        ):
            value = total(xy[slab_rows(h, x), lanes], a[h, a_buf], b[h, b_buf])
            sum_a[h, 0:432, lanes] = value.astype(BF16)
        sum_a[h, 432:448] = jnp.zeros((16, C), BF16)
        for copy in second_copies[h][0]:
            copy.start()
        for s in range(4):
            for lanes, a, b in ((LOW, summed_b, direct_b), (HIGH, direct_b, summed_b)):
                value = total(xy[part_rows(3 - h, s, y), lanes], a[h, 0, s], b[h, 1, s])
                sum_b[h, s, :, lanes] = value.astype(BF16)
        for copy in second_copies[h][1]:
            copy.start()

    stage_z = []
    for d in (4, 3, 5, 2, 6, 1, 7):
        to = (z + d) % 8
        copy = remote(zsend.at[to // 4, to % 4], zrecv.at[d - 1], zs.at[d - 1], zr.at[d - 1], z_peers[d - 1])
        stage_z.append((to, copy))

    def end_second(h):
        for copy in second_copies[h][0]:
            copy.wait_recv()
        full = total(sum_a[h, rows_at(112 * y, 112)], *[recv_a2[h, d] for d in range(3)]).astype(BF16)
        zsend[0, h], zsend[1, h] = full[:, LOW], full[:, HIGH]
        for copy in second_copies[h][1]:
            copy.wait_recv()
        full = total(sum_b[h, x], *[recv_b2[h, d] for d in range(3)]).astype(BF16)
        zsend[0, 3 - h], zsend[1, 3 - h] = full[:, LOW], full[:, HIGH]
        for to, copy in stage_z:
            outer = (to % 4 == 0) | (to % 4 == 3)

            @pl.when(outer if h == 0 else jnp.logical_not(outer))
            def _():
                copy.start()

    end_first(0)
    end_first(1)
    end_second(0)
    end_second(1)
    for _, copy in stage_z:
        copy.wait_recv()
    whole = total(zsend[z_hi, z_lo], *[zrecv[d] for d in range(7)]) * factor
    padded = jnp.concatenate([whole, jnp.zeros((16, 128), F32)], axis=0)
    fin_t[...] = padded.T.reshape(8, 16, 128)

    stage_f = []
    for d in range(1, 8):
        to = (yc + d) % 8
        stage_f.append(remote(fin_t.at[to], fin_recv.at[d - 1], fs.at[d - 1], fr.at[d - 1], f_peers[d - 1]))
    for copy in stage_f:
        copy.start()
    fin_ref[yc] = fin_t[yc]
    for d in range(1, 8):
        stage_f[d - 1].wait_recv()
    for d in range(1, 8):
        fin_ref[(yc + 8 - d) % 8] = fin_recv[d - 1]

    sent = list(first) + list(second) + [copy for _, copy in stage_z] + stage_f
    for h in range(2):
        sent += [copy for group in copies_of[h].values() for copy in group]
        sent += second_copies[h][0] + second_copies[h][1]
    for copy in sent:
        copy.wait_send()
    for store in stores:
        store.wait()

    def drain(o, carry):
        to_peer(o).wait_send()
        return carry

    lax.fori_loop(0, 27, drain, 0)


def closing(out_in, gf_in, fin, out_ref, gf_ref, g1_ref, g2_ref):
    out_ref[...] = out_in[...]
    gf_ref[...] = gf_in[...]
    for src_core, target in ((0, g1_ref), (1, g2_ref)):
        for src_y in range(4):
            size = 112 if src_y < 3 else 96
            target[:, 112 * src_y : 112 * src_y + size] = fin[src_y * 2 + src_core, :, 0:size]


def per_device(features, cotangent, neighbour_table, send_lists, block_counts, weight_one, weight_two):
    factor = 1.0 / math.sqrt(lax.axis_size("dp") * lax.axis_size("slab") * 10 * 64)
    smem = pl.BlockSpec(memory_space=pltpu.SMEM)
    vmem = pl.BlockSpec(memory_space=pltpu.VMEM)
    hbm = pl.BlockSpec(memory_space=pl.ANY)
    dma = pltpu.SemaphoreType.DMA
    big = jax.ShapeDtypeStruct((10, 64, C), BF16)
    out, gf, fin = pl.pallas_call(
        lambda *refs: kernel(factor, *refs),
        out_shape=(big, big, jax.ShapeDtypeStruct((8, 16, 128), F32)),
        in_specs=[smem, smem, vmem, hbm, hbm, hbm, hbm],
        out_specs=(hbm, hbm, vmem),
        scratch_shapes=[
            pltpu.VMEM((9, 3, C, C), BF16),
            pltpu.VMEM((9, 3, C, C), BF16),
            pltpu.VMEM((10, 64, C), BF16),
            pltpu.VMEM((10, 64, C), BF16),
            pltpu.VMEM((10, 64, C), BF16),
            pltpu.VMEM((10, 64, C), BF16),
            pltpu.VMEM((4, 640, 128), F32),
            pltpu.VMEM((10, 4, 16, 2 * C), BF16),
            pltpu.VMEM((11, 4, 16, 2 * C), BF16),
            pltpu.VMEM((2, 2, 16, 2 * C), BF16),
            pltpu.VMEM((2, 2, 16, 2 * C), BF16),
            pltpu.VMEM((10, 4, 16, 2 * C), BF16),
            pltpu.VMEM((2, 2, 16, 2 * C), BF16),
            pltpu.VMEM((2, 2, 16, 2 * C), BF16),
            pltpu.VMEM((9, 3, ROWS, REACH), BF16),
            pltpu.VMEM((9, 6, ROWS, 2 * C), BF16),
            pltpu.VMEM((640, C), F32),
            pltpu.VMEM((640, C), F32),
            pltpu.VMEM((C, 640), BF16),
            pltpu.VMEM((6912, C), BF16),
            pltpu.VMEM((6912, C), BF16),
            pltpu.VMEM((6928, C), BF16),
            pltpu.VMEM((2, 2, 432, 128), BF16),
            pltpu.VMEM((2, 2, 432, 128), BF16),
            pltpu.VMEM((2, 2, 432, 128), BF16),
            pltpu.VMEM((2, 2, 432, 128), BF16),
            pltpu.VMEM((2, 2, 4, 112, 128), BF16),
            pltpu.VMEM((2, 2, 4, 112, 128), BF16),
            pltpu.VMEM((2, 2, 4, 112, 128), BF16),
            pltpu.VMEM((2, 2, 4, 112, 128), BF16),
            pltpu.VMEM((2, 448, C), BF16),
            pltpu.VMEM((2, 4, 112, C), BF16),
            pltpu.VMEM((2, 3, 112, C), BF16),
            pltpu.VMEM((2, 3, 112, C), BF16),
            pltpu.VMEM((2, 4, 112, 128), BF16),
            pltpu.VMEM((7, 112, 128), BF16),
            pltpu.VMEM((8, 16, 128), F32),
            pltpu.VMEM((7, 16, 128), F32),
            dma((4,)),
            dma((2,)),
            dma((2, 2)),
            dma((2, 2)),
            dma((27,)),
            dma((27,)),
            dma((2, 3, 2)),
            dma((2, 3, 2)),
            dma((2, 3, 2, 4)),
            dma((2, 3, 2, 4)),
            dma((2, 3)),
            dma((2, 3)),
            dma((2, 3)),
            dma((2, 3)),
            dma((7,)),
            dma((7,)),
            dma((7,)),
            dma((7,)),
        ],
        compiler_params=pltpu.CompilerParams(
            collective_id=0, has_side_effects=True, vmem_limit_bytes=60 * 1024 * 1024
        ),
        name="step",
    )(
        block_counts,
        send_lists[0, 0],
        jnp.transpose(neighbour_table, (1, 0, 2)),
        features[0],
        cotangent[0],
        weight_one.reshape(9, 3, C, C),
        weight_two.reshape(9, 3, C, C),
    )
    piece = jax.ShapeDtypeStruct((16, 432), F32)
    out, gf, g1, g2 = pl.pallas_call(
        closing,
        out_shape=(big, big, piece, piece),
        in_specs=[vmem, vmem, vmem],
        out_specs=(vmem, vmem, vmem, vmem),
        name="closing",
    )(out, gf, fin)
    return (out[None], gf[None], g1.T, g2.T)


def solution(mesh):
    in_specs = (
        P("dp", "slab", None, None),
        P("dp", "slab", None, None),
        P("dp", "slab", None),
        P("dp", "slab", None, None),
        P("dp", "slab"),
        P(),
        P(),
    )
    out_specs = (
        P("dp", "slab", None, None),
        P("dp", "slab", None, None),
        P("slab", "dp"),
        P("slab", "dp"),
    )
    return jax.shard_map(
        per_device, mesh=mesh, in_specs=in_specs, out_specs=out_specs, check_vma=False
    )
```

```python
import math

import jax
import jax.numpy as jnp
from jax import lax
from jax.experimental import pallas as pl
from jax.experimental.pallas import tpu as pltpu
from jax.sharding import PartitionSpec as P

F32 = jnp.float32
BF16 = jnp.bfloat16
MESH = pl.DeviceIdType.MESH
ROWS = 160
REACH = 176
C = 256
NT = (((1,), (1,)), ((), ()))
TN = (((0,), (0,)), ((), ()))


def dot(a, b, dims=(((1,), (0,)), ((), ()))):
    return lax.dot_general(a, b, dims, preferred_element_type=F32)


def kernel(
    factor,
    counts, lists, table_ref, feat_hbm, cot_hbm, w1_hbm, w2_hbm,
    out_hbm, gf_hbm, fin_ref,
    w1, w2, feat, cot, out_v, gf_v, nat, t_own, t_ext, pack, hrecv, t_own2, pack2, hrecv2, sel, win, acc_a, acc_b,
    hid_t, mine, precv, relay_a, direct_a, summed_a, stage_a, relay_b, direct_b, summed_b, stage_b,
    sum_a, sum_b, recv_a2, recv_b2, zsend, zrecv, fin_t, fin_recv,
    lsem, osem, hs, hr, ps, pr, as_, ar, bs, br, a2s, a2r, b2s, b2r, zs, zr, fs, fr,
):
    dp = lax.axis_index("dp")
    slab = lax.axis_index("slab")
    core = dp % 2
    y = dp // 2 % 4
    z_hi = dp // 8
    x = slab % 4
    z_lo = slab // 4
    z = z_hi * 4 + z_lo

    def dev(x_=x, y_=y, z_=z, core_=core):
        return ((z_ // 4) * 8 + y_ * 2 + core_, (z_ % 4) * 4 + x_)

    after = (slab + 1) % 16
    before = (slab + 15) % 16
    peer = dev(core_=1 - core)
    x_peers = [dev(x_=(x + d) % 4) for d in range(1, 4)]
    y_peers = [dev(y_=(y + d) % 4) for d in range(1, 4)]
    z_peers = [dev(z_=(z + d) % 8) for d in range(1, 8)]
    yc = y * 2 + core
    f_peers = [dev(y_=(yc + d) % 8 // 2, core_=(yc + d) % 2) for d in range(1, 8)]

    barrier = pltpu.get_barrier_semaphore()
    everyone = [(dp, after), (dp, before), peer] + x_peers + y_peers + z_peers + f_peers
    for d in everyone:
        pl.semaphore_signal(barrier, inc=1, device_id=d, device_id_type=MESH)

    loads = [
        pltpu.make_async_copy(source, target, lsem.at[n])
        for n, (source, target) in enumerate(((feat_hbm, feat), (cot_hbm, cot), (w1_hbm, w1), (w2_hbm, w2)))
    ]
    for load in loads:
        load.start()

    def remote(src, dst, send, recv, to):
        return pltpu.make_async_remote_copy(
            src_ref=src, dst_ref=dst, send_sem=send, recv_sem=recv, device_id=to, device_id_type=MESH
        )

    row = lax.broadcasted_iota(jnp.int32, (640, 1), 0)
    present = jnp.where(row < counts[0, 0] * 64, 1.0, 0.0)
    loads[0].wait()
    loads[1].wait()
    for part, value in (
        (0, feat[...].reshape(640, C).astype(F32) * present),
        (2, cot[...].reshape(640, C).astype(F32)),
    ):
        nat[part], nat[part + 1] = value[:, 0:128], value[:, 128:]
    for k in range(4):
        part = jnp.concatenate([nat[n, pl.ds(k, ROWS, stride=4), :] for n in range(4)], axis=1)
        part = part.astype(BF16).reshape(10, 16, 2 * C)
        t_own[:, k] = part
        t_ext[0:10, k] = part

    def pack_edges(source, target):
        for side in range(2):
            inside = jnp.where(side == 0, slab > 0, slab < 15)
            for q in range(2):
                named = lists[side, q]
                keep = jnp.where(inside & (named < 10), 1.0, 0.0)
                block = source[jnp.minimum(named, 9)].astype(F32) * keep
                plane = [block[k, 12 * side : 12 * side + 4] for k in range(4)]
                target[side, q] = jnp.concatenate(plane, axis=0).astype(BF16)

    def halo(source, target, e):
        return (
            remote(source.at[1], target.at[0], hs.at[e, 0], hr.at[e, 0], (dp, after)),
            remote(source.at[0], target.at[1], hs.at[e, 1], hr.at[e, 1], (dp, before)),
        )

    pack_edges(t_own, pack)
    pl.semaphore_wait(barrier, len(everyone))
    first = halo(pack, hrecv, 0)
    for copy in first:
        copy.start()

    r = lax.broadcasted_iota(jnp.int32, (ROWS, 1), 0)
    spread = (r // 16 == lax.broadcasted_iota(jnp.int32, (ROWS, 10), 1)).astype(F32)
    rows_of = dot(spread, table_ref[...].reshape(10, 27).astype(F32))
    i_of, j_of = r // 4 % 4, r % 4
    lane = lax.broadcasted_iota(jnp.int32, (ROWS, REACH), 1)

    def options(position, step):
        if step == 0:
            return [(0, position == 0), (1, position > 0)]
        if step == 1:
            return [(1, None)]
        return [(1, position < 3), (2, position == 3)]

    for dx in range(3):
        for dy in range(3):
            spot_j = (j_of + dy + 3) % 4
            spot = (i_of + dx + 3) % 4 * 4 + spot_j
            for bz in range(3):
                block = None
                for bx, cond_x in options(i_of, dx):
                    for by, cond_y in options(j_of, dy):
                        n = 9 * bx + 3 * by + bz
                        value = rows_of[:, n : n + 1]
                        cond = cond_x if cond_y is None else cond_y if cond_x is None else cond_x & cond_y
                        block = value if block is None else jnp.where(cond, value, block)
                block = block.astype(jnp.int32)
                source = jnp.where(block < 10, block * 16 + spot, 160 + (block - 10) * 4 + spot_j)
                sel[dx, bz, dy * ROWS : dy * ROWS + ROWS] = jnp.where(lane == source, 1.0, 0.0).astype(BF16)

    def finish_halo(copies, received, ext):
        for copy in copies:
            copy.wait_recv()
        planes = [received[side, q].astype(F32) for side in range(2) for q in range(2)]
        for k in range(4):
            ext[10, k] = jnp.concatenate([plane[4 * k : 4 * k + 4] for plane in planes], axis=0).astype(BF16)

    def build(ext, dx):
        for k in range(4):
            parts = [(k + 1, 1)] + ([(5, 2)] if k == 0 else [(0, 0)] if k == 3 else [])
            left = jnp.concatenate([sel[dx, bz] for _, bz in parts], axis=0)
            rows = dot(left, ext[:, k].reshape(REACH, 2 * C)).astype(BF16)
            for n, (spot, _) in enumerate(parts):
                for dy in range(3):
                    at = (3 * n + dy) * ROWS
                    win[dx * 3 + dy, spot] = rows[at : at + ROWS]

    def view(g, dz, low):
        return win[g, dz : dz + 4, :, low : low + C].reshape(640, C)

    def forward(g, w):
        left = jnp.concatenate([view(g, dz, 0) for dz in range(3)], axis=1)
        acc_a[...] += dot(left, w[g].reshape(3 * C, C))

    def backward(g, w):
        left = jnp.concatenate([view(g, dz, C) for dz in range(3)], axis=1)
        right = jnp.concatenate([w[8 - g, 2 - dz] for dz in range(3)], axis=1)
        acc_b[...] += dot(left, right, NT)

    def each(start, end, step):
        def one(n, carry):
            step(n)
            return carry

        lax.fori_loop(start, end, one, 0)

    def sides(step):
        each(0, 6, lambda n: step(jnp.where(n < 3, n, n + 3)))

    acc_a[...] = jnp.zeros_like(acc_a)
    acc_b[...] = jnp.zeros_like(acc_b)
    for k in range(4):
        t_ext[10, k] = jnp.zeros((16, 2 * C), BF16)
    build(t_ext, 1)
    loads[2].wait()
    each(3, 6, lambda g: forward(g, w1))
    loads[3].wait()
    each(3, 6, lambda g: backward(g, w2))
    finish_halo(first, hrecv, t_ext)
    each(0, 2, lambda n: build(t_ext, 2 * n))
    sides(lambda g: forward(g, w1))

    hidden = jnp.maximum(acc_a[...], 0.0)
    hid_t[...] = hidden.T.astype(BF16)
    hidden = hidden.astype(BF16)
    for k in range(4):
        rows = hidden[k * ROWS : (k + 1) * ROWS].reshape(10, 16, C)
        t_own2[:, k, :, 0:C] = rows
        t_ext[0:10, k, :, 0:C] = rows

    def three(g):
        return pl.ds(pl.multiple_of(g * 768, 768), 768)

    def to_peer(g):
        return remote(mine.at[1, three(g)], precv.at[three(g)], ps.at[g], pr.at[g], peer)

    def grad_two_at(g):
        for dz in range(3):
            value = dot(hid_t[...], view(8 - g, 2 - dz, C))
            mine[1 - core, pl.ds(g * 768 + dz * C, C)] = value.astype(BF16)

    def grad_one_at(g):
        gh_rows = jnp.concatenate([t_own2[:, k, :, C:].reshape(ROWS, C) for k in range(4)], axis=0)
        left = jnp.concatenate([view(g, dz, 0) for dz in range(3)], axis=1)
        mine[core, three(g)] = dot(left, gh_rows, TN).astype(BF16)

    def join(g):
        to_peer(g).wait_recv()
        for n in range(3):
            at = pl.ds(g * 768 + n * C, C)
            xy[at] = (xy[at].astype(F32) + precv[at].astype(F32)).astype(BF16)

    xy = mine.at[0]

    def rows_at(start, size):
        return pl.ds(pl.multiple_of(start, 16), size)

    def slab_rows(zl, owner_x):
        return rows_at(432 * (zl * 4 + owner_x), 432)

    def part_rows(zl, s, owner_y):
        return rows_at(432 * (zl * 4 + s) + 112 * owner_y, 112)

    LOW, HIGH = slice(0, 128), slice(128, 256)
    next_x, last_x, far_x = (x + 1) % 4, (x + 3) % 4, (x + 2) % 4
    next_y, last_y, far_y = (y + 1) % 4, (y + 3) % 4, (y + 2) % 4

    def first_copies(h):
        copies = {}
        for phase, (buf_a, buf_b) in enumerate(((relay_a, relay_b), (direct_a, direct_b))):
            for way in range(2):
                to_x, to_y = (x_peers[0], y_peers[0]) if way == 0 else (x_peers[2], y_peers[2])
                if phase == 0:
                    owner_x, owner_y, lanes = far_x, far_y, LOW if way == 0 else HIGH
                else:
                    owner_x, owner_y = (next_x, next_y) if way == 0 else (last_x, last_y)
                    lanes = HIGH if way == 0 else LOW
                copies[phase, way] = [
                    remote(
                        xy.at[slab_rows(h, owner_x), lanes], buf_a.at[h, way],
                        as_.at[h, phase, way], ar.at[h, phase, way], to_x,
                    )
                ] + [
                    remote(
                        xy.at[part_rows(3 - h, s, owner_y), lanes], buf_b.at[h, way, s],
                        bs.at[h, phase, way, s], br.at[h, phase, way, s], to_y,
                    )
                    for s in range(4)
                ]
        for way in range(2):
            to_x, to_y = (x_peers[0], y_peers[0]) if way == 0 else (x_peers[2], y_peers[2])
            copies[2, way] = [
                remote(stage_a.at[h, way], summed_a.at[h, way], as_.at[h, 2, way], ar.at[h, 2, way], to_x),
                remote(stage_b.at[h, way], summed_b.at[h, way], bs.at[h, 2, way, 0], br.at[h, 2, way, 0], to_y),
            ]
        return copies

    copies_of = [first_copies(0), first_copies(1)]

    def start_slab(s):
        h = min(s // 4, 3 - s // 4)
        for way in range(2):
            if s < 8:
                owner = next_x if way == 0 else last_x

                @pl.when(far_x == s % 4)
                def _():
                    copies_of[h][0, way][0].start()

                @pl.when(owner == s % 4)
                def _():
                    copies_of[h][1, way][0].start()

            else:
                for phase in range(2):
                    copies_of[h][phase, way][1 + s % 4].start()

    def total(*parts):
        value = parts[0].astype(F32)
        for part in parts[1:]:
            value = value + part.astype(F32)
        return value

    def pass_on(h):
        for way in range(2):
            for copy in copies_of[h][0, way]:
                copy.wait_recv()
        for way, lanes, owner_x, owner_y in ((0, LOW, next_x, next_y), (1, HIGH, last_x, last_y)):
            stage_a[h, way] = total(xy[slab_rows(h, owner_x), lanes], relay_a[h, way]).astype(BF16)
            for s in range(4):
                own = xy[part_rows(3 - h, s, owner_y), lanes]
                stage_b[h, way, s] = total(own, relay_b[h, way, s]).astype(BF16)
            for copy in copies_of[h][2, way]:
                copy.start()

    second_copies = []
    for h in range(2):
        to_y = [
            remote(
                sum_a.at[h, rows_at(112 * ((y + d) % 4), 112)], recv_a2.at[h, d - 1], a2s.at[h, d - 1], a2r.at[h, d - 1],
                y_peers[d - 1],
            )
            for d in (2, 1, 3)
        ]
        to_x = [
            remote(sum_b.at[h, (x + d) % 4], recv_b2.at[h, d - 1], b2s.at[h, d - 1], b2r.at[h, d - 1], x_peers[d - 1])
            for d in (2, 1, 3)
        ]
        second_copies.append((to_y, to_x))

    def end_first(h):
        for phase in (1, 2):
            for way in range(2):
                for copy in copies_of[h][phase, way]:
                    copy.wait_recv()
        for lanes, a, b, a_buf, b_buf in (
            (LOW, summed_a, direct_a, 0, 1),
            (HIGH, direct_a, summed_a, 0, 1),
        ):
            value = total(xy[slab_rows(h, x), lanes], a[h, a_buf], b[h, b_buf])
            sum_a[h, 0:432, lanes] = value.astype(BF16)
        sum_a[h, 432:448] = jnp.zeros((16, C), BF16)
        for copy in second_copies[h][0]:
            copy.start()
        for s in range(4):
            for lanes, a, b in ((LOW, summed_b, direct_b), (HIGH, direct_b, summed_b)):
                value = total(xy[part_rows(3 - h, s, y), lanes], a[h, 0, s], b[h, 1, s])
                sum_b[h, s, :, lanes] = value.astype(BF16)
        for copy in second_copies[h][1]:
            copy.start()

    stage_z = []
    for d in (4, 3, 5, 2, 6, 1, 7):
        to = (z + d) % 8
        copy = remote(zsend.at[to // 4, to % 4], zrecv.at[d - 1], zs.at[d - 1], zr.at[d - 1], z_peers[d - 1])
        stage_z.append((to, copy))

    def end_second(h):
        for copy in second_copies[h][0]:
            copy.wait_recv()
        full = total(sum_a[h, rows_at(112 * y, 112)], *[recv_a2[h, d] for d in range(3)]).astype(BF16)
        zsend[0, h], zsend[1, h] = full[:, LOW], full[:, HIGH]
        for copy in second_copies[h][1]:
            copy.wait_recv()
        full = total(sum_b[h, x], *[recv_b2[h, d] for d in range(3)]).astype(BF16)
        zsend[0, 3 - h], zsend[1, 3 - h] = full[:, LOW], full[:, HIGH]
        for to, copy in stage_z:
            outer = (to % 4 == 0) | (to % 4 == 3)

            @pl.when(outer if h == 0 else jnp.logical_not(outer))
            def _():
                copy.start()

    def on(which, *steps):
        @pl.when(core == which)
        def _():
            for step, arg in steps:
                step(arg)

    READY = ((0, 15), (1, 14, 2, 13), (3, 12, 4, 11), (5, 10, 6, 9), (7, 8))

    def gradients(at, keeper, between):
        def finish(n):
            for g in (n, 8 - n) if n < 4 else (4,):
                join(g)
            for s in READY[n]:
                start_slab(s)

        def send(g):
            to_peer(g).start()

        for n in range(5):
            for g in (n, 8 - n) if n < 4 else (4,):
                at(g)
                on(1 - keeper, (send, g))
            if n > 0:
                on(keeper, (finish, n - 1))
            between(n)
        on(keeper, (finish, 4))

    xy[6912:6928] = jnp.zeros((16, C), BF16)
    gradients(grad_two_at, 1, lambda n: None)

    sides(lambda g: backward(g, w2))
    grad_hidden = jnp.where(hidden > 0, acc_b[...].astype(BF16), jnp.zeros((), BF16))
    for k in range(4):
        rows = grad_hidden[k * ROWS : (k + 1) * ROWS].reshape(10, 16, C)
        t_own2[:, k, :, C:] = rows
        t_ext[0:10, k, :, C:] = rows
    pack_edges(t_own2, pack2)
    second = halo(pack2, hrecv2, 1)
    for copy in second:
        copy.start()
    on(1, (pass_on, 0))

    gradients(grad_one_at, 0, lambda n: on(1, (pass_on, 1)) if n == 2 else None)

    finish_halo(second, hrecv2, t_ext)
    each(0, 3, lambda dx: build(t_ext, dx))
    on(0, (pass_on, 0))
    on(1, (end_first, 0))
    acc_a[...] = jnp.zeros_like(acc_a)
    acc_b[...] = jnp.zeros_like(acc_b)
    each(0, 9, lambda g: forward(g, w2))
    on(0, (pass_on, 1))
    on(1, (end_first, 1), (end_second, 0))
    each(0, 9, lambda g: backward(g, w1))
    on(1, (end_second, 1))
    for k in range(4):
        rows = slice(k * ROWS, (k + 1) * ROWS)
        for n, acc in enumerate((acc_a, acc_b)):
            for half in range(2):
                nat[2 * n + half, pl.ds(k, ROWS, stride=4), :] = acc[rows, half * 128 : half * 128 + 128]
    masked = feat[...].reshape(640, C).astype(F32) * present
    out_v[...] = (jnp.concatenate([nat[0], nat[1]], axis=1) + masked).astype(BF16).reshape(10, 64, C)
    upstream = cot[...].reshape(640, C).astype(F32)
    back = jnp.concatenate([nat[2], nat[3]], axis=1)
    gf_v[...] = ((upstream + back) * present).astype(BF16).reshape(10, 64, C)
    stores = [pltpu.make_async_copy(out_v, out_hbm, osem.at[0]), pltpu.make_async_copy(gf_v, gf_hbm, osem.at[1])]
    for store in stores:
        store.start()

    on(0, (end_first, 0), (end_first, 1), (end_second, 0), (end_second, 1))
    for _, copy in stage_z:
        copy.wait_recv()
    whole = total(zsend[z_hi, z_lo], *[zrecv[d] for d in range(7)]) * factor
    padded = jnp.concatenate([whole, jnp.zeros((16, 128), F32)], axis=0)
    fin_t[...] = padded.T.reshape(8, 16, 128)

    stage_f = []
    for d in range(1, 8):
        to = (yc + d) % 8
        stage_f.append(remote(fin_t.at[to], fin_recv.at[d - 1], fs.at[d - 1], fr.at[d - 1], f_peers[d - 1]))
    for copy in stage_f:
        copy.start()
    fin_ref[yc] = fin_t[yc]
    for d in range(1, 8):
        stage_f[d - 1].wait_recv()
    for d in range(1, 8):
        fin_ref[(yc + 8 - d) % 8] = fin_recv[d - 1]

    sent = list(first) + list(second) + [copy for _, copy in stage_z] + stage_f
    for h in range(2):
        sent += [copy for group in copies_of[h].values() for copy in group]
        sent += second_copies[h][0] + second_copies[h][1]
    for copy in sent:
        copy.wait_send()
    for store in stores:
        store.wait()

    each(0, 9, lambda g: to_peer(g).wait_send())


def closing(out_in, gf_in, fin, out_ref, gf_ref, g1_ref, g2_ref):
    out_ref[...] = out_in[...]
    gf_ref[...] = gf_in[...]
    for src_core, target in ((0, g1_ref), (1, g2_ref)):
        for src_y in range(4):
            size = 112 if src_y < 3 else 96
            target[:, 112 * src_y : 112 * src_y + size] = fin[src_y * 2 + src_core, :, 0:size]


def per_device(features, cotangent, neighbour_table, send_lists, block_counts, weight_one, weight_two):
    factor = 1.0 / math.sqrt(lax.axis_size("dp") * lax.axis_size("slab") * 10 * 64)
    smem = pl.BlockSpec(memory_space=pltpu.SMEM)
    vmem = pl.BlockSpec(memory_space=pltpu.VMEM)
    hbm = pl.BlockSpec(memory_space=pl.ANY)
    dma = pltpu.SemaphoreType.DMA
    big = jax.ShapeDtypeStruct((10, 64, C), BF16)
    out, gf, fin = pl.pallas_call(
        lambda *refs: kernel(factor, *refs),
        out_shape=(big, big, jax.ShapeDtypeStruct((8, 16, 128), F32)),
        in_specs=[smem, smem, vmem, hbm, hbm, hbm, hbm],
        out_specs=(hbm, hbm, vmem),
        scratch_shapes=[
            pltpu.VMEM((9, 3, C, C), BF16),
            pltpu.VMEM((9, 3, C, C), BF16),
            pltpu.VMEM((10, 64, C), BF16),
            pltpu.VMEM((10, 64, C), BF16),
            pltpu.VMEM((10, 64, C), BF16),
            pltpu.VMEM((10, 64, C), BF16),
            pltpu.VMEM((4, 640, 128), F32),
            pltpu.VMEM((10, 4, 16, 2 * C), BF16),
            pltpu.VMEM((11, 4, 16, 2 * C), BF16),
            pltpu.VMEM((2, 2, 16, 2 * C), BF16),
            pltpu.VMEM((2, 2, 16, 2 * C), BF16),
            pltpu.VMEM((10, 4, 16, 2 * C), BF16),
            pltpu.VMEM((2, 2, 16, 2 * C), BF16),
            pltpu.VMEM((2, 2, 16, 2 * C), BF16),
            pltpu.VMEM((3, 3, 3 * ROWS, REACH), BF16),
            pltpu.VMEM((9, 6, ROWS, 2 * C), BF16),
            pltpu.VMEM((640, C), F32),
            pltpu.VMEM((640, C), F32),
            pltpu.VMEM((C, 640), BF16),
            pltpu.VMEM((2, 6928, C), BF16),
            pltpu.VMEM((6912, C), BF16),
            pltpu.VMEM((2, 2, 432, 128), BF16),
            pltpu.VMEM((2, 2, 432, 128), BF16),
            pltpu.VMEM((2, 2, 432, 128), BF16),
            pltpu.VMEM((2, 2, 432, 128), BF16),
            pltpu.VMEM((2, 2, 4, 112, 128), BF16),
            pltpu.VMEM((2, 2, 4, 112, 128), BF16),
            pltpu.VMEM((2, 2, 4, 112, 128), BF16),
            pltpu.VMEM((2, 2, 4, 112, 128), BF16),
            pltpu.VMEM((2, 448, C), BF16),
            pltpu.VMEM((2, 4, 112, C), BF16),
            pltpu.VMEM((2, 3, 112, C), BF16),
            pltpu.VMEM((2, 3, 112, C), BF16),
            pltpu.VMEM((2, 4, 112, 128), BF16),
            pltpu.VMEM((7, 112, 128), BF16),
            pltpu.VMEM((8, 16, 128), F32),
            pltpu.VMEM((7, 16, 128), F32),
            dma((4,)),
            dma((2,)),
            dma((2, 2)),
            dma((2, 2)),
            dma((9,)),
            dma((9,)),
            dma((2, 3, 2)),
            dma((2, 3, 2)),
            dma((2, 3, 2, 4)),
            dma((2, 3, 2, 4)),
            dma((2, 3)),
            dma((2, 3)),
            dma((2, 3)),
            dma((2, 3)),
            dma((7,)),
            dma((7,)),
            dma((7,)),
            dma((7,)),
        ],
        compiler_params=pltpu.CompilerParams(
            collective_id=0, has_side_effects=True, vmem_limit_bytes=60 * 1024 * 1024
        ),
        name="step",
    )(
        block_counts,
        send_lists[0, 0],
        jnp.transpose(neighbour_table, (1, 0, 2)),
        features[0],
        cotangent[0],
        weight_one.reshape(9, 3, C, C),
        weight_two.reshape(9, 3, C, C),
    )
    piece = jax.ShapeDtypeStruct((16, 432), F32)
    out, gf, g1, g2 = pl.pallas_call(
        closing,
        out_shape=(big, big, piece, piece),
        in_specs=[vmem, vmem, vmem],
        out_specs=(vmem, vmem, vmem, vmem),
        name="closing",
    )(out, gf, fin)
    return (out[None], gf[None], g1.T, g2.T)


def solution(mesh):
    in_specs = (
        P("dp", "slab", None, None),
        P("dp", "slab", None, None),
        P("dp", "slab", None),
        P("dp", "slab", None, None),
        P("dp", "slab"),
        P(),
        P(),
    )
    out_specs = (
        P("dp", "slab", None, None),
        P("dp", "slab", None, None),
        P("slab", "dp"),
        P("slab", "dp"),
    )
    return jax.shard_map(
        per_device, mesh=mesh, in_specs=in_specs, out_specs=out_specs, check_vma=False
    )
```

```python
import math

import jax
import jax.numpy as jnp
from jax import lax
from jax.experimental import pallas as pl
from jax.experimental.pallas import tpu as pltpu
from jax.sharding import PartitionSpec as P

F32 = jnp.float32
BF16 = jnp.bfloat16
MESH = pl.DeviceIdType.MESH
ROWS = 160
REACH = 176
C = 256
NT = (((1,), (1,)), ((), ()))
TN = (((0,), (0,)), ((), ()))


def dot(a, b, dims=(((1,), (0,)), ((), ()))):
    return lax.dot_general(a, b, dims, preferred_element_type=F32)


def kernel(
    factor,
    counts, lists, table_ref, feat_hbm, cot_hbm, w1_hbm, w2_hbm,
    out_hbm, gf_hbm, fin_ref,
    w1, w2, feat, cot, out_v, gf_v, nat, t_own, t_ext, pack, hrecv, t_own2, pack2, hrecv2, sel, win, acc_a, acc_b,
    hid_t, gh_t, mine, precv, relay_a, direct_a, summed_a, stage_a, relay_b, direct_b, summed_b, stage_b,
    sum_a, sum_b, recv_a2, recv_b2, zsend, zrecv, fin_t, fin_recv,
    lsem, osem, hs, hr, ps, pr, as_, ar, bs, br, a2s, a2r, b2s, b2r, zs, zr, fs, fr,
):
    dp = lax.axis_index("dp")
    slab = lax.axis_index("slab")
    core = dp % 2
    y = dp // 2 % 4
    z_hi = dp // 8
    x = slab % 4
    z_lo = slab // 4
    z = z_hi * 4 + z_lo

    def dev(x_=x, y_=y, z_=z, core_=core):
        return ((z_ // 4) * 8 + y_ * 2 + core_, (z_ % 4) * 4 + x_)

    after = (slab + 1) % 16
    before = (slab + 15) % 16
    peer = dev(core_=1 - core)
    x_peers = [dev(x_=(x + d) % 4) for d in range(1, 4)]
    y_peers = [dev(y_=(y + d) % 4) for d in range(1, 4)]
    z_peers = [dev(z_=(z + d) % 8) for d in range(1, 8)]
    yc = y * 2 + core
    f_peers = [dev(y_=(yc + d) % 8 // 2, core_=(yc + d) % 2) for d in range(1, 8)]

    barrier = pltpu.get_barrier_semaphore()
    everyone = [(dp, after), (dp, before), peer] + x_peers + y_peers + z_peers + f_peers
    for d in everyone:
        pl.semaphore_signal(barrier, inc=1, device_id=d, device_id_type=MESH)

    loads = [
        pltpu.make_async_copy(source, target, lsem.at[n])
        for n, (source, target) in enumerate(((feat_hbm, feat), (cot_hbm, cot), (w1_hbm, w1), (w2_hbm, w2)))
    ]
    for load in loads:
        load.start()

    def remote(src, dst, send, recv, to):
        return pltpu.make_async_remote_copy(
            src_ref=src, dst_ref=dst, send_sem=send, recv_sem=recv, device_id=to, device_id_type=MESH
        )

    row = lax.broadcasted_iota(jnp.int32, (640, 1), 0)
    present = jnp.where(row < counts[0, 0] * 64, 1.0, 0.0)
    loads[0].wait()
    loads[1].wait()
    for part, value in (
        (0, feat[...].reshape(640, C).astype(F32) * present),
        (2, cot[...].reshape(640, C).astype(F32)),
    ):
        nat[part], nat[part + 1] = value[:, 0:128], value[:, 128:]
    for k in range(4):
        part = jnp.concatenate([nat[n, pl.ds(k, ROWS, stride=4), :] for n in range(4)], axis=1)
        part = part.astype(BF16).reshape(10, 16, 2 * C)
        t_own[:, k] = part
        t_ext[0:10, k] = part

    def pack_edges(source, target):
        for side in range(2):
            inside = jnp.where(side == 0, slab > 0, slab < 15)
            for q in range(2):
                named = lists[side, q]
                keep = jnp.where(inside & (named < 10), 1.0, 0.0)
                block = source[jnp.minimum(named, 9)].astype(F32) * keep
                plane = [block[k, 12 * side : 12 * side + 4] for k in range(4)]
                target[side, q] = jnp.concatenate(plane, axis=0).astype(BF16)

    def halo(source, target, e):
        return (
            remote(source.at[1], target.at[0], hs.at[e, 0], hr.at[e, 0], (dp, after)),
            remote(source.at[0], target.at[1], hs.at[e, 1], hr.at[e, 1], (dp, before)),
        )

    pack_edges(t_own, pack)
    pl.semaphore_wait(barrier, len(everyone))
    first = halo(pack, hrecv, 0)
    for copy in first:
        copy.start()

    r = lax.broadcasted_iota(jnp.int32, (ROWS, 1), 0)
    spread = (r // 16 == lax.broadcasted_iota(jnp.int32, (ROWS, 10), 1)).astype(F32)
    rows_of = dot(spread, table_ref[...].reshape(10, 27).astype(F32))
    i_of, j_of = r // 4 % 4, r % 4
    lane = lax.broadcasted_iota(jnp.int32, (ROWS, REACH), 1)

    def options(position, step):
        if step == 0:
            return [(0, position == 0), (1, position > 0)]
        if step == 1:
            return [(1, None)]
        return [(1, position < 3), (2, position == 3)]

    for dx in range(3):
        for dy in range(3):
            spot_j = (j_of + dy + 3) % 4
            spot = (i_of + dx + 3) % 4 * 4 + spot_j
            for bz in range(3):
                block = None
                for bx, cond_x in options(i_of, dx):
                    for by, cond_y in options(j_of, dy):
                        n = 9 * bx + 3 * by + bz
                        value = rows_of[:, n : n + 1]
                        cond = cond_x if cond_y is None else cond_y if cond_x is None else cond_x & cond_y
                        block = value if block is None else jnp.where(cond, value, block)
                block = block.astype(jnp.int32)
                source = jnp.where(block < 10, block * 16 + spot, 160 + (block - 10) * 4 + spot_j)
                sel[dx, bz, dy * ROWS : dy * ROWS + ROWS] = jnp.where(lane == source, 1.0, 0.0).astype(BF16)

    def finish_halo(copies, received, ext):
        for copy in copies:
            copy.wait_recv()
        planes = [received[side, q].astype(F32) for side in range(2) for q in range(2)]
        for k in range(4):
            ext[10, k] = jnp.concatenate([plane[4 * k : 4 * k + 4] for plane in planes], axis=0).astype(BF16)

    def build(ext, dx):
        for k in range(4):
            parts = [(k + 1, 1)] + ([(5, 2)] if k == 0 else [(0, 0)] if k == 3 else [])
            left = jnp.concatenate([sel[dx, bz] for _, bz in parts], axis=0)
            rows = dot(left, ext[:, k].reshape(REACH, 2 * C)).astype(BF16)
            for n, (spot, _) in enumerate(parts):
                for dy in range(3):
                    at = (3 * n + dy) * ROWS
                    win[dx * 3 + dy, spot] = rows[at : at + ROWS]

    def view(g, dz, low):
        return win[g, dz : dz + 4, :, low : low + C].reshape(640, C)

    def views(gs, low):
        return jnp.concatenate([view(g, dz, low) for g in gs for dz in range(3)], axis=1)

    def forward(gs, w):
        right = jnp.concatenate([w[g].reshape(3 * C, C) for g in gs], axis=0)
        acc_a[...] += dot(views(gs, 0), right)

    def backward(gs, w):
        right = jnp.concatenate([w[8 - g, 2 - dz] for g in gs for dz in range(3)], axis=1)
        acc_b[...] += dot(views(gs, C), right, NT)

    def each(start, end, step):
        def one(n, carry):
            step(n)
            return carry

        lax.fori_loop(start, end, one, 0)

    def sides(step):
        each(0, 3, lambda n: step((n, n + 6)))

    acc_a[...] = jnp.zeros_like(acc_a)
    acc_b[...] = jnp.zeros_like(acc_b)
    for k in range(4):
        t_ext[10, k] = jnp.zeros((16, 2 * C), BF16)
    build(t_ext, 1)
    loads[2].wait()
    forward((3, 4, 5), w1)
    loads[3].wait()
    backward((3, 4, 5), w2)
    finish_halo(first, hrecv, t_ext)
    each(0, 2, lambda n: build(t_ext, 2 * n))
    sides(lambda gs: forward(gs, w1))

    hidden = jnp.maximum(acc_a[...], 0.0)
    hid_t[...] = hidden.T.astype(BF16)
    hidden = hidden.astype(BF16)
    for k in range(4):
        rows = hidden[k * ROWS : (k + 1) * ROWS].reshape(10, 16, C)
        t_own2[:, k, :, 0:C] = rows
        t_ext[0:10, k, :, 0:C] = rows

    def three(g):
        return pl.ds(pl.multiple_of(g * 768, 768), 768)

    def to_peer(g):
        return remote(mine.at[1, three(g)], precv.at[three(g)], ps.at[g], pr.at[g], peer)

    def grad_two_at(g):
        value = dot(hid_t[...], jnp.concatenate([view(8 - g, 2 - dz, C) for dz in range(3)], axis=1)).astype(BF16)
        for dz in range(3):
            mine[1 - core, pl.ds(g * 768 + dz * C, C)] = value[:, dz * C : dz * C + C]

    def grad_one_at(g):
        mine[core, three(g)] = dot(gh_t[...], views((g,), 0)).astype(BF16).T

    def join(g):
        to_peer(g).wait_recv()
        for n in range(3):
            at = pl.ds(g * 768 + n * C, C)
            xy[at] = (xy[at].astype(F32) + precv[at].astype(F32)).astype(BF16)

    xy = mine.at[0]

    def rows_at(start, size):
        return pl.ds(pl.multiple_of(start, 16), size)

    def slab_rows(zl, owner_x):
        return rows_at(432 * (zl * 4 + owner_x), 432)

    def part_rows(zl, s, owner_y):
        return rows_at(432 * (zl * 4 + s) + 112 * owner_y, 112)

    LOW, HIGH = slice(0, 128), slice(128, 256)
    next_x, last_x, far_x = (x + 1) % 4, (x + 3) % 4, (x + 2) % 4
    next_y, last_y, far_y = (y + 1) % 4, (y + 3) % 4, (y + 2) % 4

    def first_copies(h):
        copies = {}
        for phase, (buf_a, buf_b) in enumerate(((relay_a, relay_b), (direct_a, direct_b))):
            for way in range(2):
                to_x, to_y = (x_peers[0], y_peers[0]) if way == 0 else (x_peers[2], y_peers[2])
                if phase == 0:
                    owner_x, owner_y, lanes = far_x, far_y, LOW if way == 0 else HIGH
                else:
                    owner_x, owner_y = (next_x, next_y) if way == 0 else (last_x, last_y)
                    lanes = HIGH if way == 0 else LOW
                copies[phase, way] = [
                    remote(
                        xy.at[slab_rows(h, owner_x), lanes], buf_a.at[h, way],
                        as_.at[h, phase, way], ar.at[h, phase, way], to_x,
                    )
                ] + [
                    remote(
                        xy.at[part_rows(3 - h, s, owner_y), lanes], buf_b.at[h, way, s],
                        bs.at[h, phase, way, s], br.at[h, phase, way, s], to_y,
                    )
                    for s in range(4)
                ]
        for way in range(2):
            to_x, to_y = (x_peers[0], y_peers[0]) if way == 0 else (x_peers[2], y_peers[2])
            copies[2, way] = [
                remote(stage_a.at[h, way], summed_a.at[h, way], as_.at[h, 2, way], ar.at[h, 2, way], to_x),
                remote(stage_b.at[h, way], summed_b.at[h, way], bs.at[h, 2, way, 0], br.at[h, 2, way, 0], to_y),
            ]
        return copies

    copies_of = [first_copies(0), first_copies(1)]

    def start_slab(s):
        h = min(s // 4, 3 - s // 4)
        for way in range(2):
            if s < 8:
                owner = next_x if way == 0 else last_x

                @pl.when(far_x == s % 4)
                def _():
                    copies_of[h][0, way][0].start()

                @pl.when(owner == s % 4)
                def _():
                    copies_of[h][1, way][0].start()

            else:
                for phase in range(2):
                    copies_of[h][phase, way][1 + s % 4].start()

    def total(*parts):
        value = parts[0].astype(F32)
        for part in parts[1:]:
            value = value + part.astype(F32)
        return value

    def pass_on(h):
        for way in range(2):
            for copy in copies_of[h][0, way]:
                copy.wait_recv()
        for way, lanes, owner_x, owner_y in ((0, LOW, next_x, next_y), (1, HIGH, last_x, last_y)):
            stage_a[h, way] = total(xy[slab_rows(h, owner_x), lanes], relay_a[h, way]).astype(BF16)
            for s in range(4):
                own = xy[part_rows(3 - h, s, owner_y), lanes]
                stage_b[h, way, s] = total(own, relay_b[h, way, s]).astype(BF16)
            for copy in copies_of[h][2, way]:
                copy.start()

    second_copies = []
    for h in range(2):
        to_y = [
            remote(
                sum_a.at[h, rows_at(112 * ((y + d) % 4), 112)], recv_a2.at[h, d - 1], a2s.at[h, d - 1], a2r.at[h, d - 1],
                y_peers[d - 1],
            )
            for d in (2, 1, 3)
        ]
        to_x = [
            remote(sum_b.at[h, (x + d) % 4], recv_b2.at[h, d - 1], b2s.at[h, d - 1], b2r.at[h, d - 1], x_peers[d - 1])
            for d in (2, 1, 3)
        ]
        second_copies.append((to_y, to_x))

    def end_first(h):
        for phase in (1, 2):
            for way in range(2):
                for copy in copies_of[h][phase, way]:
                    copy.wait_recv()
        for lanes, a, b, a_buf, b_buf in (
            (LOW, summed_a, direct_a, 0, 1),
            (HIGH, direct_a, summed_a, 0, 1),
        ):
            value = total(xy[slab_rows(h, x), lanes], a[h, a_buf], b[h, b_buf])
            sum_a[h, 0:432, lanes] = value.astype(BF16)
        sum_a[h, 432:448] = jnp.zeros((16, C), BF16)
        for copy in second_copies[h][0]:
            copy.start()
        for s in range(4):
            for lanes, a, b in ((LOW, summed_b, direct_b), (HIGH, direct_b, summed_b)):
                value = total(xy[part_rows(3 - h, s, y), lanes], a[h, 0, s], b[h, 1, s])
                sum_b[h, s, :, lanes] = value.astype(BF16)
        for copy in second_copies[h][1]:
            copy.start()

    stage_z = []
    for d in (4, 3, 5, 2, 6, 1, 7):
        to = (z + d) % 8
        copy = remote(zsend.at[to // 4, to % 4], zrecv.at[d - 1], zs.at[d - 1], zr.at[d - 1], z_peers[d - 1])
        stage_z.append((to, copy))

    def end_second(h):
        for copy in second_copies[h][0]:
            copy.wait_recv()
        full = total(sum_a[h, rows_at(112 * y, 112)], *[recv_a2[h, d] for d in range(3)]).astype(BF16)
        zsend[0, h], zsend[1, h] = full[:, LOW], full[:, HIGH]
        for copy in second_copies[h][1]:
            copy.wait_recv()
        full = total(sum_b[h, x], *[recv_b2[h, d] for d in range(3)]).astype(BF16)
        zsend[0, 3 - h], zsend[1, 3 - h] = full[:, LOW], full[:, HIGH]
        for to, copy in stage_z:
            outer = (to % 4 == 0) | (to % 4 == 3)

            @pl.when(outer if h == 0 else jnp.logical_not(outer))
            def _():
                copy.start()

    def on(which, *steps):
        @pl.when(core == which)
        def _():
            for step, arg in steps:
                step(arg)

    READY = ((0, 15), (1, 14, 2, 13), (3, 12, 4, 11), (5, 10, 6, 9), (7, 8))

    def gradients(at, keeper, between):
        def finish(n):
            for g in (n, 8 - n) if n < 4 else (4,):
                join(g)
            for s in READY[n]:
                start_slab(s)

        def send(g):
            to_peer(g).start()

        for n in range(5):
            gs = (n, 8 - n) if n < 4 else (4,)
            for g in gs:
                at(g)
            on(1 - keeper, *[(send, g) for g in gs])
            if n > 0:
                on(keeper, (finish, n - 1))
            between(n)
        on(keeper, (finish, 4))

    xy[6912:6928] = jnp.zeros((16, C), BF16)
    gradients(grad_two_at, 1, lambda n: None)

    sides(lambda gs: backward(gs, w2))
    grad_hidden = jnp.where(hidden > 0, acc_b[...].astype(BF16), jnp.zeros((), BF16))
    gh_t[...] = grad_hidden.T
    for k in range(4):
        rows = grad_hidden[k * ROWS : (k + 1) * ROWS].reshape(10, 16, C)
        t_own2[:, k, :, C:] = rows
        t_ext[0:10, k, :, C:] = rows
    pack_edges(t_own2, pack2)
    second = halo(pack2, hrecv2, 1)
    for copy in second:
        copy.start()
    on(1, (pass_on, 0))

    gradients(grad_one_at, 0, lambda n: on(1, (pass_on, 1)) if n == 2 else None)

    finish_halo(second, hrecv2, t_ext)
    each(0, 3, lambda dx: build(t_ext, dx))
    on(0, (pass_on, 0))
    on(1, (end_first, 0))
    acc_a[...] = jnp.zeros_like(acc_a)
    acc_b[...] = jnp.zeros_like(acc_b)
    each(0, 3, lambda n: forward((3 * n, 3 * n + 1, 3 * n + 2), w2))
    on(0, (pass_on, 1))
    on(1, (end_first, 1), (end_second, 0))
    each(0, 3, lambda n: backward((3 * n, 3 * n + 1, 3 * n + 2), w1))
    on(1, (end_second, 1))
    for k in range(4):
        rows = slice(k * ROWS, (k + 1) * ROWS)
        for n, acc in enumerate((acc_a, acc_b)):
            for half in range(2):
                nat[2 * n + half, pl.ds(k, ROWS, stride=4), :] = acc[rows, half * 128 : half * 128 + 128]
    masked = feat[...].reshape(640, C).astype(F32) * present
    out_v[...] = (jnp.concatenate([nat[0], nat[1]], axis=1) + masked).astype(BF16).reshape(10, 64, C)
    upstream = cot[...].reshape(640, C).astype(F32)
    back = jnp.concatenate([nat[2], nat[3]], axis=1)
    gf_v[...] = ((upstream + back) * present).astype(BF16).reshape(10, 64, C)
    stores = [pltpu.make_async_copy(out_v, out_hbm, osem.at[0]), pltpu.make_async_copy(gf_v, gf_hbm, osem.at[1])]
    for store in stores:
        store.start()

    on(0, (end_first, 0), (end_first, 1), (end_second, 0), (end_second, 1))
    for _, copy in stage_z:
        copy.wait_recv()
    whole = total(zsend[z_hi, z_lo], *[zrecv[d] for d in range(7)]) * factor
    padded = jnp.concatenate([whole, jnp.zeros((16, 128), F32)], axis=0)
    fin_t[...] = padded.T.reshape(8, 16, 128)

    stage_f = []
    for d in range(1, 8):
        to = (yc + d) % 8
        stage_f.append(remote(fin_t.at[to], fin_recv.at[d - 1], fs.at[d - 1], fr.at[d - 1], f_peers[d - 1]))
    for copy in stage_f:
        copy.start()
    fin_ref[yc] = fin_t[yc]
    for d in range(1, 8):
        stage_f[d - 1].wait_recv()
    for d in range(1, 8):
        fin_ref[(yc + 8 - d) % 8] = fin_recv[d - 1]

    sent = list(first) + list(second) + [copy for _, copy in stage_z] + stage_f
    for h in range(2):
        sent += [copy for group in copies_of[h].values() for copy in group]
        sent += second_copies[h][0] + second_copies[h][1]
    for copy in sent:
        copy.wait_send()
    for store in stores:
        store.wait()

    each(0, 9, lambda g: to_peer(g).wait_send())


def closing(out_in, gf_in, fin, out_ref, gf_ref, g1_ref, g2_ref):
    out_ref[...] = out_in[...]
    gf_ref[...] = gf_in[...]
    for src_core, target in ((0, g1_ref), (1, g2_ref)):
        for src_y in range(4):
            size = 112 if src_y < 3 else 96
            target[:, 112 * src_y : 112 * src_y + size] = fin[src_y * 2 + src_core, :, 0:size]


def per_device(features, cotangent, neighbour_table, send_lists, block_counts, weight_one, weight_two):
    factor = 1.0 / math.sqrt(lax.axis_size("dp") * lax.axis_size("slab") * 10 * 64)
    smem = pl.BlockSpec(memory_space=pltpu.SMEM)
    vmem = pl.BlockSpec(memory_space=pltpu.VMEM)
    hbm = pl.BlockSpec(memory_space=pl.ANY)
    dma = pltpu.SemaphoreType.DMA
    big = jax.ShapeDtypeStruct((10, 64, C), BF16)
    out, gf, fin = pl.pallas_call(
        lambda *refs: kernel(factor, *refs),
        out_shape=(big, big, jax.ShapeDtypeStruct((8, 16, 128), F32)),
        in_specs=[smem, smem, vmem, hbm, hbm, hbm, hbm],
        out_specs=(hbm, hbm, vmem),
        scratch_shapes=[
            pltpu.VMEM((9, 3, C, C), BF16),
            pltpu.VMEM((9, 3, C, C), BF16),
            pltpu.VMEM((10, 64, C), BF16),
            pltpu.VMEM((10, 64, C), BF16),
            pltpu.VMEM((10, 64, C), BF16),
            pltpu.VMEM((10, 64, C), BF16),
            pltpu.VMEM((4, 640, 128), F32),
            pltpu.VMEM((10, 4, 16, 2 * C), BF16),
            pltpu.VMEM((11, 4, 16, 2 * C), BF16),
            pltpu.VMEM((2, 2, 16, 2 * C), BF16),
            pltpu.VMEM((2, 2, 16, 2 * C), BF16),
            pltpu.VMEM((10, 4, 16, 2 * C), BF16),
            pltpu.VMEM((2, 2, 16, 2 * C), BF16),
            pltpu.VMEM((2, 2, 16, 2 * C), BF16),
            pltpu.VMEM((3, 3, 3 * ROWS, REACH), BF16),
            pltpu.VMEM((9, 6, ROWS, 2 * C), BF16),
            pltpu.VMEM((640, C), F32),
            pltpu.VMEM((640, C), F32),
            pltpu.VMEM((C, 640), BF16),
            pltpu.VMEM((C, 640), BF16),
            pltpu.VMEM((2, 6928, C), BF16),
            pltpu.VMEM((6912, C), BF16),
            pltpu.VMEM((2, 2, 432, 128), BF16),
            pltpu.VMEM((2, 2, 432, 128), BF16),
            pltpu.VMEM((2, 2, 432, 128), BF16),
            pltpu.VMEM((2, 2, 432, 128), BF16),
            pltpu.VMEM((2, 2, 4, 112, 128), BF16),
            pltpu.VMEM((2, 2, 4, 112, 128), BF16),
            pltpu.VMEM((2, 2, 4, 112, 128), BF16),
            pltpu.VMEM((2, 2, 4, 112, 128), BF16),
            pltpu.VMEM((2, 448, C), BF16),
            pltpu.VMEM((2, 4, 112, C), BF16),
            pltpu.VMEM((2, 3, 112, C), BF16),
            pltpu.VMEM((2, 3, 112, C), BF16),
            pltpu.VMEM((2, 4, 112, 128), BF16),
            pltpu.VMEM((7, 112, 128), BF16),
            pltpu.VMEM((8, 16, 128), F32),
            pltpu.VMEM((7, 16, 128), F32),
            dma((4,)),
            dma((2,)),
            dma((2, 2)),
            dma((2, 2)),
            dma((9,)),
            dma((9,)),
            dma((2, 3, 2)),
            dma((2, 3, 2)),
            dma((2, 3, 2, 4)),
            dma((2, 3, 2, 4)),
            dma((2, 3)),
            dma((2, 3)),
            dma((2, 3)),
            dma((2, 3)),
            dma((7,)),
            dma((7,)),
            dma((7,)),
            dma((7,)),
        ],
        compiler_params=pltpu.CompilerParams(
            collective_id=0, has_side_effects=True, vmem_limit_bytes=60 * 1024 * 1024
        ),
        name="step",
    )(
        block_counts,
        send_lists[0, 0],
        jnp.transpose(neighbour_table, (1, 0, 2)),
        features[0],
        cotangent[0],
        weight_one.reshape(9, 3, C, C),
        weight_two.reshape(9, 3, C, C),
    )
    piece = jax.ShapeDtypeStruct((16, 432), F32)
    out, gf, g1, g2 = pl.pallas_call(
        closing,
        out_shape=(big, big, piece, piece),
        in_specs=[vmem, vmem, vmem],
        out_specs=(vmem, vmem, vmem, vmem),
        name="closing",
    )(out, gf, fin)
    return (out[None], gf[None], g1.T, g2.T)


def solution(mesh):
    in_specs = (
        P("dp", "slab", None, None),
        P("dp", "slab", None, None),
        P("dp", "slab", None),
        P("dp", "slab", None, None),
        P("dp", "slab"),
        P(),
        P(),
    )
    out_specs = (
        P("dp", "slab", None, None),
        P("dp", "slab", None, None),
        P("slab", "dp"),
        P("slab", "dp"),
    )
    return jax.shard_map(
        per_device, mesh=mesh, in_specs=in_specs, out_specs=out_specs, check_vma=False
    )
```

```python
import math

import jax
import jax.numpy as jnp
from jax import lax
from jax.experimental import pallas as pl
from jax.experimental.pallas import tpu as pltpu
from jax.sharding import PartitionSpec as P

F32 = jnp.float32
BF16 = jnp.bfloat16
MESH = pl.DeviceIdType.MESH
ROWS = 160
REACH = 176
C = 256
NT = (((1,), (1,)), ((), ()))
TN = (((0,), (0,)), ((), ()))


def dot(a, b, dims=(((1,), (0,)), ((), ()))):
    return lax.dot_general(a, b, dims, preferred_element_type=F32)


def kernel(
    factor,
    counts, lists, table_ref, feat_hbm, cot_hbm, w1_hbm, w2_hbm,
    out_hbm, gf_hbm, fin_ref,
    w1, w2, feat, cot, out_v, gf_v, nat, t_own, t_ext, pack, hrecv, t_own2, pack2, hrecv2, sel, win, acc_a, acc_b,
    hid_t, gh_t, mine, precv, relay_a, direct_a, summed_a, stage_a, relay_b, direct_b, summed_b, stage_b,
    sum_a, sum_b, recv_a2, recv_b2, zsend, zrecv, fin_t, fin_recv,
    lsem, osem, hs, hr, ps, pr, as_, ar, bs, br, a2s, a2r, b2s, b2r, zs, zr, fs, fr,
):
    dp = lax.axis_index("dp")
    slab = lax.axis_index("slab")
    core = dp % 2
    y = dp // 2 % 4
    z_hi = dp // 8
    x = slab % 4
    z_lo = slab // 4
    z = z_hi * 4 + z_lo

    def dev(x_=x, y_=y, z_=z, core_=core):
        return ((z_ // 4) * 8 + y_ * 2 + core_, (z_ % 4) * 4 + x_)

    after = (slab + 1) % 16
    before = (slab + 15) % 16
    peer = dev(core_=1 - core)
    x_peers = [dev(x_=(x + d) % 4) for d in range(1, 4)]
    y_peers = [dev(y_=(y + d) % 4) for d in range(1, 4)]
    z_peers = [dev(z_=(z + d) % 8) for d in range(1, 8)]
    yc = y * 2 + core
    f_peers = [dev(y_=(yc + d) % 8 // 2, core_=(yc + d) % 2) for d in range(1, 8)]

    barrier = pltpu.get_barrier_semaphore()
    everyone = [(dp, after), (dp, before), peer] + x_peers + y_peers + z_peers + f_peers
    for d in everyone:
        pl.semaphore_signal(barrier, inc=1, device_id=d, device_id_type=MESH)

    loads = [
        pltpu.make_async_copy(source, target, lsem.at[n])
        for n, (source, target) in enumerate(((feat_hbm, feat), (cot_hbm, cot), (w1_hbm, w1), (w2_hbm, w2)))
    ]
    for load in loads:
        load.start()

    def remote(src, dst, send, recv, to):
        return pltpu.make_async_remote_copy(
            src_ref=src, dst_ref=dst, send_sem=send, recv_sem=recv, device_id=to, device_id_type=MESH
        )

    row = lax.broadcasted_iota(jnp.int32, (640, 1), 0)
    present = jnp.where(row < counts[0, 0] * 64, 1.0, 0.0)
    loads[0].wait()
    loads[1].wait()
    for part, value in (
        (0, feat[...].reshape(640, C).astype(F32) * present),
        (2, cot[...].reshape(640, C).astype(F32)),
    ):
        nat[part], nat[part + 1] = value[:, 0:128], value[:, 128:]
    for k in range(4):
        part = jnp.concatenate([nat[n, pl.ds(k, ROWS, stride=4), :] for n in range(4)], axis=1)
        part = part.astype(BF16).reshape(10, 16, 2 * C)
        t_own[:, k] = part
        t_ext[0:10, k] = part

    def pack_edges(source, target):
        for side in range(2):
            inside = jnp.where(side == 0, slab > 0, slab < 15)
            for q in range(2):
                named = lists[side, q]
                keep = jnp.where(inside & (named < 10), 1.0, 0.0)
                block = source[jnp.minimum(named, 9)].astype(F32) * keep
                plane = [block[k, 12 * side : 12 * side + 4] for k in range(4)]
                target[side, q] = jnp.concatenate(plane, axis=0).astype(BF16)

    def halo(source, target, e):
        return (
            remote(source.at[1], target.at[0], hs.at[e, 0], hr.at[e, 0], (dp, after)),
            remote(source.at[0], target.at[1], hs.at[e, 1], hr.at[e, 1], (dp, before)),
        )

    pack_edges(t_own, pack)
    pl.semaphore_wait(barrier, len(everyone))
    first = halo(pack, hrecv, 0)
    for copy in first:
        copy.start()

    r = lax.broadcasted_iota(jnp.int32, (ROWS, 1), 0)
    spread = (r // 16 == lax.broadcasted_iota(jnp.int32, (ROWS, 10), 1)).astype(BF16)
    rows_of = dot(spread, table_ref[...].reshape(10, 27).astype(BF16)).astype(BF16)
    named = lax.broadcasted_iota(jnp.int32, (27, 27), 0)

    def step_of(shape):
        m = lax.broadcasted_iota(jnp.int32, shape, 1)
        return m // 9, m // 3 % 3, m % 3

    step_x, step_y, step_z = step_of((27, 27))
    low = (jnp.minimum(step_x, 1), jnp.minimum(step_y, 1))
    high = (jnp.maximum(step_x, 1), jnp.maximum(step_y, 1))

    def blocks(bx, by):
        return dot(rows_of, (named == 9 * bx + 3 * by + step_z).astype(BF16))

    step_x, step_y, _ = step_of((ROWS, 27))
    at_x, at_y = r // 4 % 4 + step_x - 1, r % 4 + step_y - 1
    first_x = at_x < jnp.where(step_x == 0, 0, 4)
    first_y = at_y < jnp.where(step_y == 0, 0, 4)
    block = jnp.where(
        first_x,
        jnp.where(first_y, blocks(low[0], low[1]), blocks(low[0], high[1])),
        jnp.where(first_y, blocks(high[0], low[1]), blocks(high[0], high[1])),
    ).astype(jnp.int32)
    spot_y = (at_y + 4) % 4
    from_own = block * 16 + (at_x + 4) % 4 * 4 + spot_y
    source = jnp.where(block < 10, from_own, 160 + (block - 10) * 4 + spot_y)
    lane = lax.broadcasted_iota(jnp.int32, (ROWS, REACH), 1)
    for m in range(27):
        chosen = jnp.where(lane == source[:, m : m + 1], 1.0, 0.0).astype(BF16)
        sel[m // 9, m % 3, m // 3 % 3 * ROWS : (m // 3 % 3 + 1) * ROWS] = chosen

    def finish_halo(copies, received, ext):
        for copy in copies:
            copy.wait_recv()
        planes = [received[side, q].astype(F32) for side in range(2) for q in range(2)]
        for k in range(4):
            ext[10, k] = jnp.concatenate([plane[4 * k : 4 * k + 4] for plane in planes], axis=0).astype(BF16)

    def build(ext, dx):
        for k in range(4):
            parts = [(k + 1, 1)] + ([(5, 2)] if k == 0 else [(0, 0)] if k == 3 else [])
            left = jnp.concatenate([sel[dx, bz] for _, bz in parts], axis=0)
            rows = dot(left, ext[:, k].reshape(REACH, 2 * C)).astype(BF16)
            for n, (spot, _) in enumerate(parts):
                for dy in range(3):
                    at = (3 * n + dy) * ROWS
                    win[dx * 3 + dy, spot] = rows[at : at + ROWS]

    def view(g, dz, low):
        return win[g, dz : dz + 4, :, low : low + C].reshape(640, C)

    def views(gs, low):
        return jnp.concatenate([view(g, dz, low) for g in gs for dz in range(3)], axis=1)

    def forward(gs, w):
        right = jnp.concatenate([w[g].reshape(3 * C, C) for g in gs], axis=0)
        acc_a[...] += dot(views(gs, 0), right)

    def backward(gs, w):
        right = jnp.concatenate([w[8 - g, 2 - dz] for g in gs for dz in range(3)], axis=1)
        acc_b[...] += dot(views(gs, C), right, NT)

    def each(start, end, step):
        def one(n, carry):
            step(n)
            return carry

        lax.fori_loop(start, end, one, 0)

    def sides(step):
        each(0, 3, lambda n: step((n, n + 6)))

    acc_a[...] = jnp.zeros_like(acc_a)
    acc_b[...] = jnp.zeros_like(acc_b)
    for k in range(4):
        t_ext[10, k] = jnp.zeros((16, 2 * C), BF16)
    build(t_ext, 1)
    loads[2].wait()
    forward((3, 4, 5), w1)
    loads[3].wait()
    backward((3, 4, 5), w2)
    finish_halo(first, hrecv, t_ext)
    each(0, 2, lambda n: build(t_ext, 2 * n))
    sides(lambda gs: forward(gs, w1))

    hidden = jnp.maximum(acc_a[...], 0.0)
    hid_t[...] = hidden.T.astype(BF16)
    hidden = hidden.astype(BF16)
    for k in range(4):
        rows = hidden[k * ROWS : (k + 1) * ROWS].reshape(10, 16, C)
        t_own2[:, k, :, 0:C] = rows
        t_ext[0:10, k, :, 0:C] = rows

    def three(g):
        return pl.ds(pl.multiple_of(g * 768, 768), 768)

    def to_peer(g):
        return remote(mine.at[1, three(g)], precv.at[three(g)], ps.at[g], pr.at[g], peer)

    def grad_two_at(g):
        value = dot(hid_t[...], jnp.concatenate([view(8 - g, 2 - dz, C) for dz in range(3)], axis=1)).astype(BF16)
        for dz in range(3):
            mine[1 - core, pl.ds(g * 768 + dz * C, C)] = value[:, dz * C : dz * C + C]

    def grad_one_at(g):
        mine[core, three(g)] = dot(gh_t[...], views((g,), 0)).astype(BF16).T

    def join(g):
        to_peer(g).wait_recv()
        for n in range(3):
            at = pl.ds(g * 768 + n * C, C)
            xy[at] = (xy[at].astype(F32) + precv[at].astype(F32)).astype(BF16)

    xy = mine.at[0]

    def rows_at(start, size):
        return pl.ds(pl.multiple_of(start, 16), size)

    def slab_rows(zl, owner_x):
        return rows_at(432 * (zl * 4 + owner_x), 432)

    def part_rows(zl, s, owner_y):
        return rows_at(432 * (zl * 4 + s) + 112 * owner_y, 112)

    LOW, HIGH = slice(0, 128), slice(128, 256)
    next_x, last_x, far_x = (x + 1) % 4, (x + 3) % 4, (x + 2) % 4
    next_y, last_y, far_y = (y + 1) % 4, (y + 3) % 4, (y + 2) % 4

    def first_copies(h):
        copies = {}
        for phase, (buf_a, buf_b) in enumerate(((relay_a, relay_b), (direct_a, direct_b))):
            for way in range(2):
                to_x, to_y = (x_peers[0], y_peers[0]) if way == 0 else (x_peers[2], y_peers[2])
                if phase == 0:
                    owner_x, owner_y, lanes = far_x, far_y, LOW if way == 0 else HIGH
                else:
                    owner_x, owner_y = (next_x, next_y) if way == 0 else (last_x, last_y)
                    lanes = HIGH if way == 0 else LOW
                copies[phase, way] = [
                    remote(
                        xy.at[slab_rows(h, owner_x), lanes], buf_a.at[h, way],
                        as_.at[h, phase, way], ar.at[h, phase, way], to_x,
                    )
                ] + [
                    remote(
                        xy.at[part_rows(3 - h, s, owner_y), lanes], buf_b.at[h, way, s],
                        bs.at[h, phase, way, s], br.at[h, phase, way, s], to_y,
                    )
                    for s in range(4)
                ]
        for way in range(2):
            to_x, to_y = (x_peers[0], y_peers[0]) if way == 0 else (x_peers[2], y_peers[2])
            copies[2, way] = [
                remote(stage_a.at[h, way], summed_a.at[h, way], as_.at[h, 2, way], ar.at[h, 2, way], to_x),
                remote(stage_b.at[h, way], summed_b.at[h, way], bs.at[h, 2, way, 0], br.at[h, 2, way, 0], to_y),
            ]
        return copies

    copies_of = [first_copies(0), first_copies(1)]

    def start_slab(s):
        h = min(s // 4, 3 - s // 4)
        for way in range(2):
            if s < 8:
                owner = next_x if way == 0 else last_x

                @pl.when(far_x == s % 4)
                def _():
                    copies_of[h][0, way][0].start()

                @pl.when(owner == s % 4)
                def _():
                    copies_of[h][1, way][0].start()

            else:
                for phase in range(2):
                    copies_of[h][phase, way][1 + s % 4].start()

    def total(*parts):
        value = parts[0].astype(F32)
        for part in parts[1:]:
            value = value + part.astype(F32)
        return value

    def pass_on(h):
        for way in range(2):
            for copy in copies_of[h][0, way]:
                copy.wait_recv()
        for way, lanes, owner_x, owner_y in ((0, LOW, next_x, next_y), (1, HIGH, last_x, last_y)):
            stage_a[h, way] = total(xy[slab_rows(h, owner_x), lanes], relay_a[h, way]).astype(BF16)
            for s in range(4):
                own = xy[part_rows(3 - h, s, owner_y), lanes]
                stage_b[h, way, s] = total(own, relay_b[h, way, s]).astype(BF16)
            for copy in copies_of[h][2, way]:
                copy.start()

    second_copies = []
    for h in range(2):
        to_y = [
            remote(
                sum_a.at[h, rows_at(112 * ((y + d) % 4), 112)], recv_a2.at[h, d - 1], a2s.at[h, d - 1], a2r.at[h, d - 1],
                y_peers[d - 1],
            )
            for d in (2, 1, 3)
        ]
        to_x = [
            remote(sum_b.at[h, (x + d) % 4], recv_b2.at[h, d - 1], b2s.at[h, d - 1], b2r.at[h, d - 1], x_peers[d - 1])
            for d in (2, 1, 3)
        ]
        second_copies.append((to_y, to_x))

    def end_first(h):
        for phase in (1, 2):
            for way in range(2):
                for copy in copies_of[h][phase, way]:
                    copy.wait_recv()
        for lanes, a, b, a_buf, b_buf in (
            (LOW, summed_a, direct_a, 0, 1),
            (HIGH, direct_a, summed_a, 0, 1),
        ):
            value = total(xy[slab_rows(h, x), lanes], a[h, a_buf], b[h, b_buf])
            sum_a[h, 0:432, lanes] = value.astype(BF16)
        sum_a[h, 432:448] = jnp.zeros((16, C), BF16)
        for copy in second_copies[h][0]:
            copy.start()
        for s in range(4):
            for lanes, a, b in ((LOW, summed_b, direct_b), (HIGH, direct_b, summed_b)):
                value = total(xy[part_rows(3 - h, s, y), lanes], a[h, 0, s], b[h, 1, s])
                sum_b[h, s, :, lanes] = value.astype(BF16)
        for copy in second_copies[h][1]:
            copy.start()

    stage_z = []
    for d in (4, 3, 5, 2, 6, 1, 7):
        to = (z + d) % 8
        copy = remote(zsend.at[to // 4, to % 4], zrecv.at[d - 1], zs.at[d - 1], zr.at[d - 1], z_peers[d - 1])
        stage_z.append((to, copy))

    def end_second(h):
        for copy in second_copies[h][0]:
            copy.wait_recv()
        full = total(sum_a[h, rows_at(112 * y, 112)], *[recv_a2[h, d] for d in range(3)]).astype(BF16)
        zsend[0, h], zsend[1, h] = full[:, LOW], full[:, HIGH]
        for copy in second_copies[h][1]:
            copy.wait_recv()
        full = total(sum_b[h, x], *[recv_b2[h, d] for d in range(3)]).astype(BF16)
        zsend[0, 3 - h], zsend[1, 3 - h] = full[:, LOW], full[:, HIGH]
        for to, copy in stage_z:
            outer = (to % 4 == 0) | (to % 4 == 3)

            @pl.when(outer if h == 0 else jnp.logical_not(outer))
            def _():
                copy.start()

    def on(which, *steps):
        @pl.when(core == which)
        def _():
            for step, arg in steps:
                step(arg)

    READY = ((0, 15), (1, 14, 2, 13), (3, 12, 4, 11), (5, 10, 6, 9), (7, 8))

    def gradients(at, keeper, between):
        def finish(n):
            for g in (n, 8 - n) if n < 4 else (4,):
                join(g)
            for s in READY[n]:
                start_slab(s)

        def send(g):
            to_peer(g).start()

        for n in range(5):
            gs = (n, 8 - n) if n < 4 else (4,)
            for g in gs:
                at(g)
            on(1 - keeper, *[(send, g) for g in gs])
            if n > 0:
                on(keeper, (finish, n - 1))
            between(n)
        on(keeper, (finish, 4))

    xy[6912:6928] = jnp.zeros((16, C), BF16)
    gradients(grad_two_at, 1, lambda n: None)

    sides(lambda gs: backward(gs, w2))
    grad_hidden = jnp.where(hidden > 0, acc_b[...].astype(BF16), jnp.zeros((), BF16))
    gh_t[...] = grad_hidden.T
    for k in range(4):
        rows = grad_hidden[k * ROWS : (k + 1) * ROWS].reshape(10, 16, C)
        t_own2[:, k, :, C:] = rows
        t_ext[0:10, k, :, C:] = rows
    pack_edges(t_own2, pack2)
    second = halo(pack2, hrecv2, 1)
    for copy in second:
        copy.start()
    on(1, (pass_on, 0))

    gradients(grad_one_at, 0, lambda n: on(1, (pass_on, 1)) if n == 2 else None)

    finish_halo(second, hrecv2, t_ext)
    build(t_ext, 0)
    on(0, (pass_on, 0))
    on(1, (end_first, 0))
    each(1, 3, lambda dx: build(t_ext, dx))
    on(0, (pass_on, 1))
    on(1, (end_first, 1))
    acc_a[...] = jnp.zeros_like(acc_a)
    acc_b[...] = jnp.zeros_like(acc_b)
    each(0, 3, lambda n: forward((3 * n, 3 * n + 1, 3 * n + 2), w2))
    on(0, (end_first, 0))
    on(1, (end_second, 0))
    each(0, 3, lambda n: backward((3 * n, 3 * n + 1, 3 * n + 2), w1))
    on(0, (end_first, 1))
    on(1, (end_second, 1))
    for k in range(4):
        rows = slice(k * ROWS, (k + 1) * ROWS)
        for n, acc in enumerate((acc_a, acc_b)):
            for half in range(2):
                nat[2 * n + half, pl.ds(k, ROWS, stride=4), :] = acc[rows, half * 128 : half * 128 + 128]
    masked = feat[...].reshape(640, C).astype(F32) * present
    out_v[...] = (jnp.concatenate([nat[0], nat[1]], axis=1) + masked).astype(BF16).reshape(10, 64, C)
    upstream = cot[...].reshape(640, C).astype(F32)
    back = jnp.concatenate([nat[2], nat[3]], axis=1)
    gf_v[...] = ((upstream + back) * present).astype(BF16).reshape(10, 64, C)
    stores = [pltpu.make_async_copy(out_v, out_hbm, osem.at[0]), pltpu.make_async_copy(gf_v, gf_hbm, osem.at[1])]
    for store in stores:
        store.start()

    on(0, (end_second, 0), (end_second, 1))
    for _, copy in stage_z:
        copy.wait_recv()
    whole = total(zsend[z_hi, z_lo], *[zrecv[d] for d in range(7)]) * factor
    padded = jnp.concatenate([whole, jnp.zeros((16, 128), F32)], axis=0)
    fin_t[...] = padded.T.reshape(8, 16, 128)

    stage_f = []
    for d in range(1, 8):
        to = (yc + d) % 8
        stage_f.append(remote(fin_t.at[to], fin_recv.at[d - 1], fs.at[d - 1], fr.at[d - 1], f_peers[d - 1]))
    for copy in stage_f:
        copy.start()
    fin_ref[yc] = fin_t[yc]
    for d in range(1, 8):
        stage_f[d - 1].wait_recv()
    for d in range(1, 8):
        fin_ref[(yc + 8 - d) % 8] = fin_recv[d - 1]

    sent = list(first) + list(second) + [copy for _, copy in stage_z] + stage_f
    for h in range(2):
        sent += [copy for group in copies_of[h].values() for copy in group]
        sent += second_copies[h][0] + second_copies[h][1]
    for copy in sent:
        copy.wait_send()
    for store in stores:
        store.wait()

    each(0, 9, lambda g: to_peer(g).wait_send())


def closing(out_in, gf_in, fin, out_ref, gf_ref, g1_ref, g2_ref):
    out_ref[...] = out_in[...]
    gf_ref[...] = gf_in[...]
    for src_core, target in ((0, g1_ref), (1, g2_ref)):
        for src_y in range(4):
            size = 112 if src_y < 3 else 96
            target[:, 112 * src_y : 112 * src_y + size] = fin[src_y * 2 + src_core, :, 0:size]


def per_device(features, cotangent, neighbour_table, send_lists, block_counts, weight_one, weight_two):
    factor = 1.0 / math.sqrt(lax.axis_size("dp") * lax.axis_size("slab") * 10 * 64)
    smem = pl.BlockSpec(memory_space=pltpu.SMEM)
    vmem = pl.BlockSpec(memory_space=pltpu.VMEM)
    hbm = pl.BlockSpec(memory_space=pl.ANY)
    dma = pltpu.SemaphoreType.DMA
    big = jax.ShapeDtypeStruct((10, 64, C), BF16)
    out, gf, fin = pl.pallas_call(
        lambda *refs: kernel(factor, *refs),
        out_shape=(big, big, jax.ShapeDtypeStruct((8, 16, 128), F32)),
        in_specs=[smem, smem, vmem, hbm, hbm, hbm, hbm],
        out_specs=(hbm, hbm, vmem),
        scratch_shapes=[
            pltpu.VMEM((9, 3, C, C), BF16),
            pltpu.VMEM((9, 3, C, C), BF16),
            pltpu.VMEM((10, 64, C), BF16),
            pltpu.VMEM((10, 64, C), BF16),
            pltpu.VMEM((10, 64, C), BF16),
            pltpu.VMEM((10, 64, C), BF16),
            pltpu.VMEM((4, 640, 128), F32),
            pltpu.VMEM((10, 4, 16, 2 * C), BF16),
            pltpu.VMEM((11, 4, 16, 2 * C), BF16),
            pltpu.VMEM((2, 2, 16, 2 * C), BF16),
            pltpu.VMEM((2, 2, 16, 2 * C), BF16),
            pltpu.VMEM((10, 4, 16, 2 * C), BF16),
            pltpu.VMEM((2, 2, 16, 2 * C), BF16),
            pltpu.VMEM((2, 2, 16, 2 * C), BF16),
            pltpu.VMEM((3, 3, 3 * ROWS, REACH), BF16),
            pltpu.VMEM((9, 6, ROWS, 2 * C), BF16),
            pltpu.VMEM((640, C), F32),
            pltpu.VMEM((640, C), F32),
            pltpu.VMEM((C, 640), BF16),
            pltpu.VMEM((C, 640), BF16),
            pltpu.VMEM((2, 6928, C), BF16),
            pltpu.VMEM((6912, C), BF16),
            pltpu.VMEM((2, 2, 432, 128), BF16),
            pltpu.VMEM((2, 2, 432, 128), BF16),
            pltpu.VMEM((2, 2, 432, 128), BF16),
            pltpu.VMEM((2, 2, 432, 128), BF16),
            pltpu.VMEM((2, 2, 4, 112, 128), BF16),
            pltpu.VMEM((2, 2, 4, 112, 128), BF16),
            pltpu.VMEM((2, 2, 4, 112, 128), BF16),
            pltpu.VMEM((2, 2, 4, 112, 128), BF16),
            pltpu.VMEM((2, 448, C), BF16),
            pltpu.VMEM((2, 4, 112, C), BF16),
            pltpu.VMEM((2, 3, 112, C), BF16),
            pltpu.VMEM((2, 3, 112, C), BF16),
            pltpu.VMEM((2, 4, 112, 128), BF16),
            pltpu.VMEM((7, 112, 128), BF16),
            pltpu.VMEM((8, 16, 128), F32),
            pltpu.VMEM((7, 16, 128), F32),
            dma((4,)),
            dma((2,)),
            dma((2, 2)),
            dma((2, 2)),
            dma((9,)),
            dma((9,)),
            dma((2, 3, 2)),
            dma((2, 3, 2)),
            dma((2, 3, 2, 4)),
            dma((2, 3, 2, 4)),
            dma((2, 3)),
            dma((2, 3)),
            dma((2, 3)),
            dma((2, 3)),
            dma((7,)),
            dma((7,)),
            dma((7,)),
            dma((7,)),
        ],
        compiler_params=pltpu.CompilerParams(
            collective_id=0, has_side_effects=True, vmem_limit_bytes=60 * 1024 * 1024
        ),
        name="step",
    )(
        block_counts,
        send_lists[0, 0],
        jnp.transpose(neighbour_table, (1, 0, 2)),
        features[0],
        cotangent[0],
        weight_one.reshape(9, 3, C, C),
        weight_two.reshape(9, 3, C, C),
    )
    piece = jax.ShapeDtypeStruct((16, 432), F32)
    out, gf, g1, g2 = pl.pallas_call(
        closing,
        out_shape=(big, big, piece, piece),
        in_specs=[vmem, vmem, vmem],
        out_specs=(vmem, vmem, vmem, vmem),
        name="closing",
    )(out, gf, fin)
    return (out[None], gf[None], g1.T, g2.T)


def solution(mesh):
    in_specs = (
        P("dp", "slab", None, None),
        P("dp", "slab", None, None),
        P("dp", "slab", None),
        P("dp", "slab", None, None),
        P("dp", "slab"),
        P(),
        P(),
    )
    out_specs = (
        P("dp", "slab", None, None),
        P("dp", "slab", None, None),
        P("slab", "dp"),
        P("slab", "dp"),
    )
    return jax.shard_map(
        per_device, mesh=mesh, in_specs=in_specs, out_specs=out_specs, check_vma=False
    )
```

```python
import math

import jax
import jax.numpy as jnp
from jax import lax
from jax.experimental import pallas as pl
from jax.experimental.pallas import tpu as pltpu
from jax.sharding import PartitionSpec as P

F32 = jnp.float32
BF16 = jnp.bfloat16
MESH = pl.DeviceIdType.MESH
ROWS = 160
REACH = 176
C = 256
NT = (((1,), (1,)), ((), ()))
TN = (((0,), (0,)), ((), ()))


def dot(a, b, dims=(((1,), (0,)), ((), ()))):
    return lax.dot_general(a, b, dims, preferred_element_type=F32)


def kernel(
    factor,
    counts, lists, table_ref, feat_hbm, cot_hbm, w1_hbm, w2_hbm,
    out_hbm, gf_hbm, fin_ref,
    w1, w2, feat, cot, out_v, gf_v, nat, t_own, t_ext, pack, hrecv, t_own2, pack2, hrecv2, sel, win, acc_a, acc_b,
    hid_t, gh_t, mine, precv, relay_a, direct_a, summed_a, stage_a, relay_b, direct_b, summed_b, stage_b,
    sum_a, sum_b, recv_a2, recv_b2, zsend, zrecv, fin_t, fin_recv,
    lsem, osem, hs, hr, ps, pr, as_, ar, bs, br, a2s, a2r, b2s, b2r, zs, zr, fs, fr,
):
    loads = [
        pltpu.make_async_copy(source, target, lsem.at[n])
        for n, (source, target) in enumerate(((feat_hbm, feat), (cot_hbm, cot), (w1_hbm, w1), (w2_hbm, w2)))
    ]
    for load in loads:
        load.start()

    dp = lax.axis_index("dp")
    slab = lax.axis_index("slab")
    core = dp % 2
    y = dp // 2 % 4
    z_hi = dp // 8
    x = slab % 4
    z_lo = slab // 4
    z = z_hi * 4 + z_lo

    def dev(x_=x, y_=y, z_=z, core_=core):
        return ((z_ // 4) * 8 + y_ * 2 + core_, (z_ % 4) * 4 + x_)

    after = (slab + 1) % 16
    before = (slab + 15) % 16
    peer = dev(core_=1 - core)
    x_peers = [dev(x_=(x + d) % 4) for d in range(1, 4)]
    y_peers = [dev(y_=(y + d) % 4) for d in range(1, 4)]
    z_peers = [dev(z_=(z + d) % 8) for d in range(1, 8)]
    yc = y * 2 + core
    f_peers = [dev(y_=(yc + d) % 8 // 2, core_=(yc + d) % 2) for d in range(1, 8)]

    barrier = pltpu.get_barrier_semaphore()
    everyone = [(dp, after), (dp, before)] + x_peers + z_peers + f_peers
    for d in everyone:
        pl.semaphore_signal(barrier, inc=1, device_id=d, device_id_type=MESH)

    def remote(src, dst, send, recv, to):
        return pltpu.make_async_remote_copy(
            src_ref=src, dst_ref=dst, send_sem=send, recv_sem=recv, device_id=to, device_id_type=MESH
        )

    row = lax.broadcasted_iota(jnp.int32, (640, 1), 0)
    present = jnp.where(row < counts[0, 0] * 64, 1.0, 0.0)
    loads[0].wait()
    loads[1].wait()
    for part, value in (
        (0, feat[...].reshape(640, C).astype(F32) * present),
        (2, cot[...].reshape(640, C).astype(F32)),
    ):
        nat[part], nat[part + 1] = value[:, 0:128], value[:, 128:]
    for k in range(4):
        part = jnp.concatenate([nat[n, pl.ds(k, ROWS, stride=4), :] for n in range(4)], axis=1)
        part = part.astype(BF16).reshape(10, 16, 2 * C)
        t_own[:, k] = part
        t_ext[0:10, k] = part

    def pack_edges(source, target):
        for side in range(2):
            inside = jnp.where(side == 0, slab > 0, slab < 15)
            for q in range(2):
                named = lists[side, q]
                keep = jnp.where(inside & (named < 10), 1.0, 0.0)
                block = source[jnp.minimum(named, 9)].astype(F32) * keep
                plane = [block[k, 12 * side : 12 * side + 4] for k in range(4)]
                target[side, q] = jnp.concatenate(plane, axis=0).astype(BF16)

    def halo(source, target, e):
        return (
            remote(source.at[1], target.at[0], hs.at[e, 0], hr.at[e, 0], (dp, after)),
            remote(source.at[0], target.at[1], hs.at[e, 1], hr.at[e, 1], (dp, before)),
        )

    pack_edges(t_own, pack)
    pl.semaphore_wait(barrier, len(everyone))
    first = halo(pack, hrecv, 0)
    for copy in first:
        copy.start()

    r = lax.broadcasted_iota(jnp.int32, (ROWS, 1), 0)
    spread = (r // 16 == lax.broadcasted_iota(jnp.int32, (ROWS, 10), 1)).astype(BF16)
    rows_of = dot(spread, table_ref[...].reshape(10, 27).astype(BF16)).astype(BF16)
    named = lax.broadcasted_iota(jnp.int32, (27, 27), 0)

    def step_of(shape):
        m = lax.broadcasted_iota(jnp.int32, shape, 1)
        return m // 9, m // 3 % 3, m % 3

    step_x, step_y, step_z = step_of((27, 27))
    low = (jnp.minimum(step_x, 1), jnp.minimum(step_y, 1))
    high = (jnp.maximum(step_x, 1), jnp.maximum(step_y, 1))

    def blocks(bx, by):
        return dot(rows_of, (named == 9 * bx + 3 * by + step_z).astype(BF16))

    step_x, step_y, _ = step_of((ROWS, 27))
    at_x, at_y = r // 4 % 4 + step_x - 1, r % 4 + step_y - 1
    first_x = at_x < jnp.where(step_x == 0, 0, 4)
    first_y = at_y < jnp.where(step_y == 0, 0, 4)
    block = jnp.where(
        first_x,
        jnp.where(first_y, blocks(low[0], low[1]), blocks(low[0], high[1])),
        jnp.where(first_y, blocks(high[0], low[1]), blocks(high[0], high[1])),
    ).astype(jnp.int32)
    spot_y = (at_y + 4) % 4
    from_own = block * 16 + (at_x + 4) % 4 * 4 + spot_y
    source = jnp.where(block < 10, from_own, 160 + (block - 10) * 4 + spot_y)
    lane = lax.broadcasted_iota(jnp.int32, (ROWS, REACH), 1)
    for m in range(27):
        chosen = jnp.where(lane == source[:, m : m + 1], 1.0, 0.0).astype(BF16)
        sel[m // 9, m % 3, m // 3 % 3 * ROWS : (m // 3 % 3 + 1) * ROWS] = chosen

    def finish_halo(copies, received, ext):
        for copy in copies:
            copy.wait_recv()
        planes = [received[side, q].astype(F32) for side in range(2) for q in range(2)]
        for k in range(4):
            ext[10, k] = jnp.concatenate([plane[4 * k : 4 * k + 4] for plane in planes], axis=0).astype(BF16)

    def build(ext, dx):
        for k in range(4):
            parts = [(k + 1, 1)] + ([(5, 2)] if k == 0 else [(0, 0)] if k == 3 else [])
            left = jnp.concatenate([sel[dx, bz] for _, bz in parts], axis=0)
            rows = dot(left, ext[:, k].reshape(REACH, 2 * C)).astype(BF16)
            for n, (spot, _) in enumerate(parts):
                for dy in range(3):
                    at = (3 * n + dy) * ROWS
                    win[dx * 3 + dy, spot] = rows[at : at + ROWS]

    def view(g, dz, low):
        return win[g, dz : dz + 4, :, low : low + C].reshape(640, C)

    def views(gs, low):
        return jnp.concatenate([view(g, dz, low) for g in gs for dz in range(3)], axis=1)

    def forward(gs, w):
        right = jnp.concatenate([w[g].reshape(3 * C, C) for g in gs], axis=0)
        acc_a[...] += dot(views(gs, 0), right)

    def backward(gs, w):
        right = jnp.concatenate([w[8 - g, 2 - dz] for g in gs for dz in range(3)], axis=1)
        acc_b[...] += dot(views(gs, C), right, NT)

    def each(start, end, step):
        def one(n, carry):
            step(n)
            return carry

        lax.fori_loop(start, end, one, 0)

    def sides(step):
        each(0, 3, lambda n: step((n, n + 6)))

    acc_a[...] = jnp.zeros_like(acc_a)
    acc_b[...] = jnp.zeros_like(acc_b)
    for k in range(4):
        t_ext[10, k] = jnp.zeros((16, 2 * C), BF16)
    build(t_ext, 1)
    loads[2].wait()
    forward((3, 4, 5), w1)
    loads[3].wait()
    backward((3, 4, 5), w2)
    finish_halo(first, hrecv, t_ext)
    each(0, 2, lambda n: build(t_ext, 2 * n))
    sides(lambda gs: forward(gs, w1))

    hidden = jnp.maximum(acc_a[...], 0.0)
    hid_t[...] = hidden.T.astype(BF16)
    hidden = hidden.astype(BF16)
    for k in range(4):
        rows = hidden[k * ROWS : (k + 1) * ROWS].reshape(10, 16, C)
        t_own2[:, k, :, 0:C] = rows
        t_ext[0:10, k, :, 0:C] = rows

    def three(g):
        return pl.ds(pl.multiple_of(g * 768, 768), 768)

    def to_peer(g):
        return remote(mine.at[1, three(g)], precv.at[three(g)], ps.at[g], pr.at[g], peer)

    def grad_two_at(g):
        value = dot(hid_t[...], jnp.concatenate([view(8 - g, 2 - dz, C) for dz in range(3)], axis=1)).astype(BF16)
        for dz in range(3):
            mine[1 - core, pl.ds(g * 768 + dz * C, C)] = value[:, dz * C : dz * C + C]

    def grad_one_at(g):
        mine[core, three(g)] = dot(gh_t[...], views((g,), 0)).astype(BF16).T

    def join(g):
        to_peer(g).wait_recv()
        for n in range(3):
            at = pl.ds(g * 768 + n * C, C)
            xy[at] = (xy[at].astype(F32) + precv[at].astype(F32)).astype(BF16)

    xy = mine.at[0]

    def rows_at(start, size):
        return pl.ds(pl.multiple_of(start, 16), size)

    def slab_rows(zl, owner_x):
        return rows_at(432 * (zl * 4 + owner_x), 432)

    def part_rows(zl, s, owner_y):
        return rows_at(432 * (zl * 4 + s) + 112 * owner_y, 112)

    LOW, HIGH = slice(0, 128), slice(128, 256)
    next_x, last_x, far_x = (x + 1) % 4, (x + 3) % 4, (x + 2) % 4
    next_y, last_y, far_y = (y + 1) % 4, (y + 3) % 4, (y + 2) % 4

    def first_copies(h):
        copies = {}
        for phase, (buf_a, buf_b) in enumerate(((relay_a, relay_b), (direct_a, direct_b))):
            for way in range(2):
                to_x, to_y = (x_peers[0], y_peers[0]) if way == 0 else (x_peers[2], y_peers[2])
                if phase == 0:
                    owner_x, owner_y, lanes = far_x, far_y, LOW if way == 0 else HIGH
                else:
                    owner_x, owner_y = (next_x, next_y) if way == 0 else (last_x, last_y)
                    lanes = HIGH if way == 0 else LOW
                copies[phase, way] = [
                    remote(
                        xy.at[slab_rows(h, owner_x), lanes], buf_a.at[h, way],
                        as_.at[h, phase, way], ar.at[h, phase, way], to_x,
                    )
                ] + [
                    remote(
                        xy.at[part_rows(3 - h, s, owner_y), lanes], buf_b.at[h, way, s],
                        bs.at[h, phase, way, s], br.at[h, phase, way, s], to_y,
                    )
                    for s in range(4)
                ]
        for way in range(2):
            to_x, to_y = (x_peers[0], y_peers[0]) if way == 0 else (x_peers[2], y_peers[2])
            copies[2, way] = [
                remote(stage_a.at[h, way], summed_a.at[h, way], as_.at[h, 2, way], ar.at[h, 2, way], to_x),
                remote(stage_b.at[h, way], summed_b.at[h, way], bs.at[h, 2, way, 0], br.at[h, 2, way, 0], to_y),
            ]
        return copies

    copies_of = [first_copies(0), first_copies(1)]

    def start_slab(s):
        h = min(s // 4, 3 - s // 4)
        for way in range(2):
            if s < 8:
                owner = next_x if way == 0 else last_x

                @pl.when(far_x == s % 4)
                def _():
                    copies_of[h][0, way][0].start()

                @pl.when(owner == s % 4)
                def _():
                    copies_of[h][1, way][0].start()

            else:
                for phase in range(2):
                    copies_of[h][phase, way][1 + s % 4].start()

    def total(*parts):
        value = parts[0].astype(F32)
        for part in parts[1:]:
            value = value + part.astype(F32)
        return value

    def pass_on(h):
        for way in range(2):
            for copy in copies_of[h][0, way]:
                copy.wait_recv()
        for way, lanes, owner_x, owner_y in ((0, LOW, next_x, next_y), (1, HIGH, last_x, last_y)):
            stage_a[h, way] = total(xy[slab_rows(h, owner_x), lanes], relay_a[h, way]).astype(BF16)
            for s in range(4):
                own = xy[part_rows(3 - h, s, owner_y), lanes]
                stage_b[h, way, s] = total(own, relay_b[h, way, s]).astype(BF16)
            for copy in copies_of[h][2, way]:
                copy.start()

    second_copies = []
    for h in range(2):
        to_y = [
            remote(
                sum_a.at[h, rows_at(112 * ((y + d) % 4), 112)], recv_a2.at[h, d - 1], a2s.at[h, d - 1], a2r.at[h, d - 1],
                y_peers[d - 1],
            )
            for d in (2, 1, 3)
        ]
        to_x = [
            remote(sum_b.at[h, (x + d) % 4], recv_b2.at[h, d - 1], b2s.at[h, d - 1], b2r.at[h, d - 1], x_peers[d - 1])
            for d in (2, 1, 3)
        ]
        second_copies.append((to_y, to_x))

    def end_first(h):
        for phase in (1, 2):
            for way in range(2):
                for copy in copies_of[h][phase, way]:
                    copy.wait_recv()
        for lanes, a, b, a_buf, b_buf in (
            (LOW, summed_a, direct_a, 0, 1),
            (HIGH, direct_a, summed_a, 0, 1),
        ):
            value = total(xy[slab_rows(h, x), lanes], a[h, a_buf], b[h, b_buf])
            sum_a[h, 0:432, lanes] = value.astype(BF16)
        sum_a[h, 432:448] = jnp.zeros((16, C), BF16)
        for copy in second_copies[h][0]:
            copy.start()
        for s in range(4):
            for lanes, a, b in ((LOW, summed_b, direct_b), (HIGH, direct_b, summed_b)):
                value = total(xy[part_rows(3 - h, s, y), lanes], a[h, 0, s], b[h, 1, s])
                sum_b[h, s, :, lanes] = value.astype(BF16)
        for copy in second_copies[h][1]:
            copy.start()

    stage_z = []
    for d in (4, 3, 5, 2, 6, 1, 7):
        to = (z + d) % 8
        copy = remote(zsend.at[to // 4, to % 4], zrecv.at[d - 1], zs.at[d - 1], zr.at[d - 1], z_peers[d - 1])
        stage_z.append((to, copy))

    def end_second(h):
        for copy in second_copies[h][0]:
            copy.wait_recv()
        full = total(sum_a[h, rows_at(112 * y, 112)], *[recv_a2[h, d] for d in range(3)]).astype(BF16)
        zsend[0, h], zsend[1, h] = full[:, LOW], full[:, HIGH]
        for copy in second_copies[h][1]:
            copy.wait_recv()
        full = total(sum_b[h, x], *[recv_b2[h, d] for d in range(3)]).astype(BF16)
        zsend[0, 3 - h], zsend[1, 3 - h] = full[:, LOW], full[:, HIGH]
        for to, copy in stage_z:
            outer = (to % 4 == 0) | (to % 4 == 3)

            @pl.when(outer if h == 0 else jnp.logical_not(outer))
            def _():
                copy.start()

    def on(which, *steps):
        @pl.when(core == which)
        def _():
            for step, arg in steps:
                step(arg)

    READY = ((0, 15), (1, 14, 2, 13), (3, 12, 4, 11), (5, 10, 6, 9), (7, 8))

    def gradients(at, keeper, between):
        def finish(n):
            for g in (n, 8 - n) if n < 4 else (4,):
                join(g)
            for s in READY[n]:
                start_slab(s)

        def send(g):
            to_peer(g).start()

        for n in range(5):
            gs = (n, 8 - n) if n < 4 else (4,)
            for g in gs:
                at(g)
            on(1 - keeper, *[(send, g) for g in gs])
            if n > 0:
                on(keeper, (finish, n - 1))
            between(n)
        on(keeper, (finish, 4))

    xy[6912:6928] = jnp.zeros((16, C), BF16)
    gradients(grad_two_at, 1, lambda n: None)

    sides(lambda gs: backward(gs, w2))
    grad_hidden = jnp.where(hidden > 0, acc_b[...].astype(BF16), jnp.zeros((), BF16))
    gh_t[...] = grad_hidden.T
    for k in range(4):
        rows = grad_hidden[k * ROWS : (k + 1) * ROWS].reshape(10, 16, C)
        t_own2[:, k, :, C:] = rows
        t_ext[0:10, k, :, C:] = rows
    pack_edges(t_own2, pack2)
    second = halo(pack2, hrecv2, 1)
    for copy in second:
        copy.start()
    gradients(grad_one_at, 0, lambda n: on(1, (pass_on, 0)) if n == 1 else None)
    on(1, (pass_on, 1))

    finish_halo(second, hrecv2, t_ext)
    build(t_ext, 0)
    on(0, (pass_on, 0))
    on(1, (end_first, 0))
    each(1, 3, lambda dx: build(t_ext, dx))
    on(0, (pass_on, 1))
    on(1, (end_first, 1))
    acc_a[...] = jnp.zeros_like(acc_a)
    acc_b[...] = jnp.zeros_like(acc_b)
    each(0, 3, lambda n: forward((3 * n, 3 * n + 1, 3 * n + 2), w2))
    on(0, (end_first, 0))
    on(1, (end_second, 0))
    each(0, 1, lambda n: backward((3 * n, 3 * n + 1, 3 * n + 2), w1))
    on(0, (end_first, 1))
    on(1, (end_second, 1))
    each(1, 3, lambda n: backward((3 * n, 3 * n + 1, 3 * n + 2), w1))
    on(0, (end_second, 0))
    for k in range(4):
        rows = slice(k * ROWS, (k + 1) * ROWS)
        for n, acc in enumerate((acc_a, acc_b)):
            for half in range(2):
                nat[2 * n + half, pl.ds(k, ROWS, stride=4), :] = acc[rows, half * 128 : half * 128 + 128]
    masked = feat[...].reshape(640, C).astype(F32) * present
    out_v[...] = (jnp.concatenate([nat[0], nat[1]], axis=1) + masked).astype(BF16).reshape(10, 64, C)
    upstream = cot[...].reshape(640, C).astype(F32)
    back = jnp.concatenate([nat[2], nat[3]], axis=1)
    gf_v[...] = ((upstream + back) * present).astype(BF16).reshape(10, 64, C)
    stores = [pltpu.make_async_copy(out_v, out_hbm, osem.at[0]), pltpu.make_async_copy(gf_v, gf_hbm, osem.at[1])]
    for store in stores:
        store.start()

    on(0, (end_second, 1))
    for _, copy in stage_z:
        copy.wait_recv()
    whole = total(zsend[z_hi, z_lo], *[zrecv[d] for d in range(7)]) * factor
    padded = jnp.concatenate([whole, jnp.zeros((16, 128), F32)], axis=0)
    fin_t[...] = padded.T.reshape(8, 16, 128)

    stage_f = []
    for d in range(1, 8):
        to = (yc + d) % 8
        stage_f.append(remote(fin_t.at[to], fin_recv.at[d - 1], fs.at[d - 1], fr.at[d - 1], f_peers[d - 1]))
    for copy in stage_f:
        copy.start()
    fin_ref[yc] = fin_t[yc]
    for d in range(1, 8):
        stage_f[d - 1].wait_recv()
    for d in range(1, 8):
        fin_ref[(yc + 8 - d) % 8] = fin_recv[d - 1]

    sent = list(first) + list(second) + [copy for _, copy in stage_z] + stage_f
    for h in range(2):
        sent += [copy for group in copies_of[h].values() for copy in group]
        sent += second_copies[h][0] + second_copies[h][1]
    for copy in sent:
        copy.wait_send()
    for store in stores:
        store.wait()

    each(0, 9, lambda g: to_peer(g).wait_send())


def closing(out_in, gf_in, fin, out_ref, gf_ref, g1_ref, g2_ref):
    out_ref[...] = out_in[...]
    gf_ref[...] = gf_in[...]
    for src_core, target in ((0, g1_ref), (1, g2_ref)):
        for src_y in range(4):
            size = 112 if src_y < 3 else 96
            target[:, 112 * src_y : 112 * src_y + size] = fin[src_y * 2 + src_core, :, 0:size]


def per_device(features, cotangent, neighbour_table, send_lists, block_counts, weight_one, weight_two):
    factor = 1.0 / math.sqrt(lax.axis_size("dp") * lax.axis_size("slab") * 10 * 64)
    smem = pl.BlockSpec(memory_space=pltpu.SMEM)
    vmem = pl.BlockSpec(memory_space=pltpu.VMEM)
    hbm = pl.BlockSpec(memory_space=pl.ANY)
    dma = pltpu.SemaphoreType.DMA
    big = jax.ShapeDtypeStruct((10, 64, C), BF16)
    out, gf, fin = pl.pallas_call(
        lambda *refs: kernel(factor, *refs),
        out_shape=(big, big, jax.ShapeDtypeStruct((8, 16, 128), F32)),
        in_specs=[smem, smem, vmem, hbm, hbm, hbm, hbm],
        out_specs=(hbm, hbm, vmem),
        scratch_shapes=[
            pltpu.VMEM((9, 3, C, C), BF16),
            pltpu.VMEM((9, 3, C, C), BF16),
            pltpu.VMEM((10, 64, C), BF16),
            pltpu.VMEM((10, 64, C), BF16),
            pltpu.VMEM((10, 64, C), BF16),
            pltpu.VMEM((10, 64, C), BF16),
            pltpu.VMEM((4, 640, 128), F32),
            pltpu.VMEM((10, 4, 16, 2 * C), BF16),
            pltpu.VMEM((11, 4, 16, 2 * C), BF16),
            pltpu.VMEM((2, 2, 16, 2 * C), BF16),
            pltpu.VMEM((2, 2, 16, 2 * C), BF16),
            pltpu.VMEM((10, 4, 16, 2 * C), BF16),
            pltpu.VMEM((2, 2, 16, 2 * C), BF16),
            pltpu.VMEM((2, 2, 16, 2 * C), BF16),
            pltpu.VMEM((3, 3, 3 * ROWS, REACH), BF16),
            pltpu.VMEM((9, 6, ROWS, 2 * C), BF16),
            pltpu.VMEM((640, C), F32),
            pltpu.VMEM((640, C), F32),
            pltpu.VMEM((C, 640), BF16),
            pltpu.VMEM((C, 640), BF16),
            pltpu.VMEM((2, 6928, C), BF16),
            pltpu.VMEM((6912, C), BF16),
            pltpu.VMEM((2, 2, 432, 128), BF16),
            pltpu.VMEM((2, 2, 432, 128), BF16),
            pltpu.VMEM((2, 2, 432, 128), BF16),
            pltpu.VMEM((2, 2, 432, 128), BF16),
            pltpu.VMEM((2, 2, 4, 112, 128), BF16),
            pltpu.VMEM((2, 2, 4, 112, 128), BF16),
            pltpu.VMEM((2, 2, 4, 112, 128), BF16),
            pltpu.VMEM((2, 2, 4, 112, 128), BF16),
            pltpu.VMEM((2, 448, C), BF16),
            pltpu.VMEM((2, 4, 112, C), BF16),
            pltpu.VMEM((2, 3, 112, C), BF16),
            pltpu.VMEM((2, 3, 112, C), BF16),
            pltpu.VMEM((2, 4, 112, 128), BF16),
            pltpu.VMEM((7, 112, 128), BF16),
            pltpu.VMEM((8, 16, 128), F32),
            pltpu.VMEM((7, 16, 128), F32),
            dma((4,)),
            dma((2,)),
            dma((2, 2)),
            dma((2, 2)),
            dma((9,)),
            dma((9,)),
            dma((2, 3, 2)),
            dma((2, 3, 2)),
            dma((2, 3, 2, 4)),
            dma((2, 3, 2, 4)),
            dma((2, 3)),
            dma((2, 3)),
            dma((2, 3)),
            dma((2, 3)),
            dma((7,)),
            dma((7,)),
            dma((7,)),
            dma((7,)),
        ],
        compiler_params=pltpu.CompilerParams(
            collective_id=0, has_side_effects=True, vmem_limit_bytes=60 * 1024 * 1024
        ),
        name="step",
    )(
        block_counts,
        send_lists[0, 0],
        jnp.transpose(neighbour_table, (1, 0, 2)),
        features[0],
        cotangent[0],
        weight_one.reshape(9, 3, C, C),
        weight_two.reshape(9, 3, C, C),
    )
    piece = jax.ShapeDtypeStruct((16, 432), F32)
    out, gf, g1, g2 = pl.pallas_call(
        closing,
        out_shape=(big, big, piece, piece),
        in_specs=[vmem, vmem, vmem],
        out_specs=(vmem, vmem, vmem, vmem),
        name="closing",
    )(out, gf, fin)
    return (out[None], gf[None], g1.T, g2.T)


def solution(mesh):
    in_specs = (
        P("dp", "slab", None, None),
        P("dp", "slab", None, None),
        P("dp", "slab", None),
        P("dp", "slab", None, None),
        P("dp", "slab"),
        P(),
        P(),
    )
    out_specs = (
        P("dp", "slab", None, None),
        P("dp", "slab", None, None),
        P("slab", "dp"),
        P("slab", "dp"),
    )
    return jax.shard_map(
        per_device, mesh=mesh, in_specs=in_specs, out_specs=out_specs, check_vma=False
    )
```

```python
import math

import jax
import jax.numpy as jnp
from jax import lax
from jax.experimental import pallas as pl
from jax.experimental.pallas import tpu as pltpu
from jax.sharding import PartitionSpec as P

F32 = jnp.float32
BF16 = jnp.bfloat16
MESH = pl.DeviceIdType.MESH
ROWS = 160
REACH = 176
C = 256
NT = (((1,), (1,)), ((), ()))
TN = (((0,), (0,)), ((), ()))


def dot(a, b, dims=(((1,), (0,)), ((), ()))):
    return lax.dot_general(a, b, dims, preferred_element_type=F32)


def kernel(
    factor,
    counts, lists, table_ref, feat_hbm, cot_hbm, w1_hbm, w2_hbm,
    out_hbm, gf_hbm, fin_ref,
    w1, w2, feat, cot, out_v, gf_v, nat, t_own, t_ext, pack, hrecv, t_own2, pack2, hrecv2, sel, win, acc_a, acc_b,
    hid_t, gh_t, mine, precv, relay_a, direct_a, summed_a, stage_a, relay_b, direct_b, summed_b, stage_b,
    sum_a, sum_b, recv_a2, recv_b2, zsend, zrecv,
    tail_z, tail_z_in, tail_x, tail_x_in, tail_y, tail_y_in, fin_t, fin_recv,
    lsem, osem, hs, hr, ps, pr, as_, ar, bs, br, a2s, a2r, b2s, b2r, zs, zr, fs, fr, tzs, tzr, txs, txr, tys, tyr,
):
    loads = [
        pltpu.make_async_copy(source, target, lsem.at[n])
        for n, (source, target) in enumerate(((feat_hbm, feat), (cot_hbm, cot), (w1_hbm, w1), (w2_hbm, w2)))
    ]
    for load in loads:
        load.start()

    dp = lax.axis_index("dp")
    slab = lax.axis_index("slab")
    core = dp % 2
    y = dp // 2 % 4
    z_hi = dp // 8
    x = slab % 4
    z_lo = slab // 4
    z = z_hi * 4 + z_lo

    def dev(x_=x, y_=y, z_=z, core_=core):
        return ((z_ // 4) * 8 + y_ * 2 + core_, (z_ % 4) * 4 + x_)

    after = (slab + 1) % 16
    before = (slab + 15) % 16
    peer = dev(core_=1 - core)
    x_peers = [dev(x_=(x + d) % 4) for d in range(1, 4)]
    y_peers = [dev(y_=(y + d) % 4) for d in range(1, 4)]
    z_peers = [dev(z_=(z + d) % 8) for d in range(1, 8)]
    yc = y * 2 + core
    f_peers = [dev(y_=(yc + d) % 8 // 2, core_=(yc + d) % 2) for d in range(1, 8)]

    barrier = pltpu.get_barrier_semaphore()
    everyone = [(dp, after), (dp, before)] + x_peers + z_peers + f_peers
    for d in everyone:
        pl.semaphore_signal(barrier, inc=1, device_id=d, device_id_type=MESH)

    def remote(src, dst, send, recv, to):
        return pltpu.make_async_remote_copy(
            src_ref=src, dst_ref=dst, send_sem=send, recv_sem=recv, device_id=to, device_id_type=MESH
        )

    row = lax.broadcasted_iota(jnp.int32, (640, 1), 0)
    present = jnp.where(row < counts[0, 0] * 64, 1.0, 0.0)
    loads[0].wait()
    loads[1].wait()
    for part, value in (
        (0, feat[...].reshape(640, C).astype(F32) * present),
        (2, cot[...].reshape(640, C).astype(F32)),
    ):
        nat[part], nat[part + 1] = value[:, 0:128], value[:, 128:]
    for k in range(4):
        part = jnp.concatenate([nat[n, pl.ds(k, ROWS, stride=4), :] for n in range(4)], axis=1)
        part = part.astype(BF16).reshape(10, 16, 2 * C)
        t_own[:, k] = part
        t_ext[0:10, k] = part

    def pack_edges(source, target):
        for side in range(2):
            inside = jnp.where(side == 0, slab > 0, slab < 15)
            for q in range(2):
                named = lists[side, q]
                keep = jnp.where(inside & (named < 10), 1.0, 0.0)
                block = source[jnp.minimum(named, 9)].astype(F32) * keep
                plane = [block[k, 12 * side : 12 * side + 4] for k in range(4)]
                target[side, q] = jnp.concatenate(plane, axis=0).astype(BF16)

    def halo(source, target, e):
        return (
            remote(source.at[1], target.at[0], hs.at[e, 0], hr.at[e, 0], (dp, after)),
            remote(source.at[0], target.at[1], hs.at[e, 1], hr.at[e, 1], (dp, before)),
        )

    pack_edges(t_own, pack)
    pl.semaphore_wait(barrier, len(everyone))
    first = halo(pack, hrecv, 0)
    for copy in first:
        copy.start()

    r = lax.broadcasted_iota(jnp.int32, (ROWS, 1), 0)
    spread = (r // 16 == lax.broadcasted_iota(jnp.int32, (ROWS, 10), 1)).astype(BF16)
    rows_of = dot(spread, table_ref[...].reshape(10, 27).astype(BF16)).astype(BF16)
    named = lax.broadcasted_iota(jnp.int32, (27, 27), 0)

    def step_of(shape):
        m = lax.broadcasted_iota(jnp.int32, shape, 1)
        return m // 9, m // 3 % 3, m % 3

    step_x, step_y, step_z = step_of((27, 27))
    low = (jnp.minimum(step_x, 1), jnp.minimum(step_y, 1))
    high = (jnp.maximum(step_x, 1), jnp.maximum(step_y, 1))

    def blocks(bx, by):
        return dot(rows_of, (named == 9 * bx + 3 * by + step_z).astype(BF16))

    step_x, step_y, _ = step_of((ROWS, 27))
    at_x, at_y = r // 4 % 4 + step_x - 1, r % 4 + step_y - 1
    first_x = at_x < jnp.where(step_x == 0, 0, 4)
    first_y = at_y < jnp.where(step_y == 0, 0, 4)
    block = jnp.where(
        first_x,
        jnp.where(first_y, blocks(low[0], low[1]), blocks(low[0], high[1])),
        jnp.where(first_y, blocks(high[0], low[1]), blocks(high[0], high[1])),
    ).astype(jnp.int32)
    spot_y = (at_y + 4) % 4
    from_own = block * 16 + (at_x + 4) % 4 * 4 + spot_y
    source = jnp.where(block < 10, from_own, 160 + (block - 10) * 4 + spot_y)
    lane = lax.broadcasted_iota(jnp.int32, (ROWS, REACH), 1)
    for m in range(27):
        chosen = jnp.where(lane == source[:, m : m + 1], 1.0, 0.0).astype(BF16)
        sel[m // 9, m % 3, m // 3 % 3 * ROWS : (m // 3 % 3 + 1) * ROWS] = chosen

    def finish_halo(copies, received, ext):
        for copy in copies:
            copy.wait_recv()
        planes = [received[side, q].astype(F32) for side in range(2) for q in range(2)]
        for k in range(4):
            ext[10, k] = jnp.concatenate([plane[4 * k : 4 * k + 4] for plane in planes], axis=0).astype(BF16)

    def build(ext, dx):
        for k in range(4):
            parts = [(k + 1, 1)] + ([(5, 2)] if k == 0 else [(0, 0)] if k == 3 else [])
            left = jnp.concatenate([sel[dx, bz] for _, bz in parts], axis=0)
            rows = dot(left, ext[:, k].reshape(REACH, 2 * C)).astype(BF16)
            for n, (spot, _) in enumerate(parts):
                for dy in range(3):
                    at = (3 * n + dy) * ROWS
                    win[dx * 3 + dy, spot] = rows[at : at + ROWS]

    def view(g, dz, low):
        return win[g, dz : dz + 4, :, low : low + C].reshape(640, C)

    def views(gs, low):
        return jnp.concatenate([view(g, dz, low) for g in gs for dz in range(3)], axis=1)

    def forward(gs, w):
        right = jnp.concatenate([w[g].reshape(3 * C, C) for g in gs], axis=0)
        acc_a[...] += dot(views(gs, 0), right)

    def backward(gs, w):
        right = jnp.concatenate([w[8 - g, 2 - dz] for g in gs for dz in range(3)], axis=1)
        acc_b[...] += dot(views(gs, C), right, NT)

    def each(start, end, step):
        def one(n, carry):
            step(n)
            return carry

        lax.fori_loop(start, end, one, 0)

    def sides(step):
        each(0, 3, lambda n: step((n, n + 6)))

    acc_a[...] = jnp.zeros_like(acc_a)
    acc_b[...] = jnp.zeros_like(acc_b)
    for k in range(4):
        t_ext[10, k] = jnp.zeros((16, 2 * C), BF16)
    build(t_ext, 1)
    loads[2].wait()
    forward((3, 4, 5), w1)
    loads[3].wait()
    backward((3, 4, 5), w2)
    finish_halo(first, hrecv, t_ext)
    each(0, 2, lambda n: build(t_ext, 2 * n))
    sides(lambda gs: forward(gs, w1))

    hidden = jnp.maximum(acc_a[...], 0.0)
    hid_t[...] = hidden.T.astype(BF16)
    hidden = hidden.astype(BF16)
    for k in range(4):
        rows = hidden[k * ROWS : (k + 1) * ROWS].reshape(10, 16, C)
        t_own2[:, k, :, 0:C] = rows
        t_ext[0:10, k, :, 0:C] = rows

    def three(g):
        return pl.ds(pl.multiple_of(g * 768, 768), 768)

    def to_peer(g):
        return remote(mine.at[1, three(g)], precv.at[three(g)], ps.at[g], pr.at[g], peer)

    def grad_two_at(g):
        value = dot(hid_t[...], jnp.concatenate([view(8 - g, 2 - dz, C) for dz in range(3)], axis=1)).astype(BF16)
        for dz in range(3):
            mine[1 - core, pl.ds(g * 768 + dz * C, C)] = value[:, dz * C : dz * C + C]

    def grad_one_at(g):
        mine[core, three(g)] = dot(gh_t[...], views((g,), 0)).astype(BF16).T

    def join(g):
        to_peer(g).wait_recv()
        for n in range(3):
            at = pl.ds(g * 768 + n * C, C)
            xy[at] = (xy[at].astype(F32) + precv[at].astype(F32)).astype(BF16)

    xy = mine.at[0]

    def rows_at(start, size):
        return pl.ds(pl.multiple_of(start, 16), size)

    def slab_rows(zl, owner_x):
        return rows_at(432 * (zl * 4 + owner_x), 384)

    def part_rows(zl, s, owner_y):
        return rows_at(432 * (zl * 4 + s) + 96 * owner_y, 96)

    LOW, HIGH = slice(0, 128), slice(128, 256)
    next_x, last_x, far_x = (x + 1) % 4, (x + 3) % 4, (x + 2) % 4
    next_y, last_y, far_y = (y + 1) % 4, (y + 3) % 4, (y + 2) % 4

    def first_copies(h):
        copies = {}
        for phase, (buf_a, buf_b) in enumerate(((relay_a, relay_b), (direct_a, direct_b))):
            for way in range(2):
                to_x, to_y = (x_peers[0], y_peers[0]) if way == 0 else (x_peers[2], y_peers[2])
                if phase == 0:
                    owner_x, owner_y, lanes = far_x, far_y, LOW if way == 0 else HIGH
                else:
                    owner_x, owner_y = (next_x, next_y) if way == 0 else (last_x, last_y)
                    lanes = HIGH if way == 0 else LOW
                copies[phase, way] = [
                    remote(
                        xy.at[slab_rows(h, owner_x), lanes], buf_a.at[h, way],
                        as_.at[h, phase, way], ar.at[h, phase, way], to_x,
                    )
                ] + [
                    remote(
                        xy.at[part_rows(3 - h, s, owner_y), lanes], buf_b.at[h, way, s],
                        bs.at[h, phase, way, s], br.at[h, phase, way, s], to_y,
                    )
                    for s in range(4)
                ]
        for way in range(2):
            to_x, to_y = (x_peers[0], y_peers[0]) if way == 0 else (x_peers[2], y_peers[2])
            copies[2, way] = [
                remote(stage_a.at[h, way], summed_a.at[h, way], as_.at[h, 2, way], ar.at[h, 2, way], to_x),
                remote(stage_b.at[h, way], summed_b.at[h, way], bs.at[h, 2, way, 0], br.at[h, 2, way, 0], to_y),
            ]
        return copies

    copies_of = [first_copies(0), first_copies(1)]

    def start_slab(s):
        h = min(s // 4, 3 - s // 4)
        for way in range(2):
            if s < 8:
                owner = next_x if way == 0 else last_x

                @pl.when(far_x == s % 4)
                def _():
                    copies_of[h][0, way][0].start()

                @pl.when(owner == s % 4)
                def _():
                    copies_of[h][1, way][0].start()

            else:
                for phase in range(2):
                    copies_of[h][phase, way][1 + s % 4].start()

    def total(*parts):
        value = parts[0].astype(F32)
        for part in parts[1:]:
            value = value + part.astype(F32)
        return value

    def pass_on(h):
        for way in range(2):
            for copy in copies_of[h][0, way]:
                copy.wait_recv()
        for way, lanes, owner_x, owner_y in ((0, LOW, next_x, next_y), (1, HIGH, last_x, last_y)):
            stage_a[h, way] = total(xy[slab_rows(h, owner_x), lanes], relay_a[h, way]).astype(BF16)
            for s in range(4):
                own = xy[part_rows(3 - h, s, owner_y), lanes]
                stage_b[h, way, s] = total(own, relay_b[h, way, s]).astype(BF16)
            for copy in copies_of[h][2, way]:
                copy.start()

    second_copies = []
    for h in range(2):
        to_y = [
            remote(
                sum_a.at[h, rows_at(96 * ((y + d) % 4), 96)], recv_a2.at[h, d - 1], a2s.at[h, d - 1], a2r.at[h, d - 1],
                y_peers[d - 1],
            )
            for d in (2, 1, 3)
        ]
        to_x = [
            remote(sum_b.at[h, (x + d) % 4], recv_b2.at[h, d - 1], b2s.at[h, d - 1], b2r.at[h, d - 1], x_peers[d - 1])
            for d in (2, 1, 3)
        ]
        second_copies.append((to_y, to_x))

    def end_first(h):
        for phase in (1, 2):
            for way in range(2):
                for copy in copies_of[h][phase, way]:
                    copy.wait_recv()
        for lanes, a, b, a_buf, b_buf in (
            (LOW, summed_a, direct_a, 0, 1),
            (HIGH, direct_a, summed_a, 0, 1),
        ):
            value = total(xy[slab_rows(h, x), lanes], a[h, a_buf], b[h, b_buf])
            sum_a[h, :, lanes] = value.astype(BF16)
        for copy in second_copies[h][0]:
            copy.start()
        for s in range(4):
            for lanes, a, b in ((LOW, summed_b, direct_b), (HIGH, direct_b, summed_b)):
                value = total(xy[part_rows(3 - h, s, y), lanes], a[h, 0, s], b[h, 1, s])
                sum_b[h, s, :, lanes] = value.astype(BF16)
        for copy in second_copies[h][1]:
            copy.start()

    stage_z = []
    for d in (4, 3, 5, 2, 6, 1, 7):
        to = (z + d) % 8
        copy = remote(zsend.at[to // 4, to % 4], zrecv.at[d - 1], zs.at[d - 1], zr.at[d - 1], z_peers[d - 1])
        stage_z.append((to, copy))

    def end_second(h):
        for copy in second_copies[h][0]:
            copy.wait_recv()
        full = total(sum_a[h, rows_at(96 * y, 96)], *[recv_a2[h, d] for d in range(3)]).astype(BF16)
        zsend[0, h], zsend[1, h] = full[:, LOW], full[:, HIGH]
        for copy in second_copies[h][1]:
            copy.wait_recv()
        full = total(sum_b[h, x], *[recv_b2[h, d] for d in range(3)]).astype(BF16)
        zsend[0, 3 - h], zsend[1, 3 - h] = full[:, LOW], full[:, HIGH]
        for to, copy in stage_z:
            outer = (to % 4 == 0) | (to % 4 == 3)

            @pl.when(outer if h == 0 else jnp.logical_not(outer))
            def _():
                copy.start()

    tails_z = []
    for d in (4, 3, 5, 2, 6, 1, 7):
        to = (z + d) % 8
        copy = remote(tail_z.at[to // 4, to % 4], tail_z_in.at[d - 1], tzs.at[d - 1], tzr.at[d - 1], z_peers[d - 1])
        tails_z.append((to, copy))
    tails_x = [
        remote(tail_x.at[(x + d) % 4], tail_x_in.at[d - 1], txs.at[d - 1], txr.at[d - 1], x_peers[d - 1]) for d in (2, 1, 3)
    ]
    tails_y = [
        remote(tail_y.at[(y + d) % 4], tail_y_in.at[d - 1], tys.at[d - 1], tyr.at[d - 1], y_peers[d - 1]) for d in (2, 1, 3)
    ]

    def pack_tail(s):
        rows = xy[432 * s + 384 : 432 * s + 432]
        tail_z[0, s // 4, s % 4], tail_z[1, s // 4, s % 4] = rows[:, LOW], rows[:, HIGH]

    def start_tails(h):
        for to, copy in tails_z:
            outer = (to % 4 == 0) | (to % 4 == 3)

            @pl.when(outer if h == 0 else jnp.logical_not(outer))
            def _():
                copy.start()

    def tail_after_z(_):
        for _, copy in tails_z:
            copy.wait_recv()
        for s in range(4):
            tail_x[s] = total(tail_z[z_hi, z_lo, s], *[tail_z_in[d, s] for d in range(7)]).astype(BF16)
        for copy in tails_x:
            copy.start()

    def tail_after_x(_):
        for copy in tails_x:
            copy.wait_recv()
        value = total(tail_x[x], *[tail_x_in[d] for d in range(3)]).astype(BF16)
        for part in range(3):
            tail_y[part] = value[16 * part : 16 * part + 16]
        tail_y[3] = jnp.zeros((16, 128), BF16)
        for copy in tails_y:
            copy.start()

    def on(which, *steps):
        @pl.when(core == which)
        def _():
            for step, arg in steps:
                step(arg)

    READY = ((0, 15), (1, 14, 2, 13), (3, 12, 4, 11), (5, 10, 6, 9), (7, 8))

    def gradients(at, keeper, between):
        def finish(n):
            for g in (n, 8 - n) if n < 4 else (4,):
                join(g)
            for s in READY[n]:
                start_slab(s)
                pack_tail(s)
            if n in (2, 4):
                start_tails(0 if n == 2 else 1)

        def send(g):
            to_peer(g).start()

        for n in range(5):
            gs = (n, 8 - n) if n < 4 else (4,)
            for g in gs:
                at(g)
            on(1 - keeper, *[(send, g) for g in gs])
            if n > 0:
                on(keeper, (finish, n - 1))
            between(n)
        on(keeper, (finish, 4))

    gradients(grad_two_at, 1, lambda n: None)

    sides(lambda gs: backward(gs, w2))
    grad_hidden = jnp.where(hidden > 0, acc_b[...].astype(BF16), jnp.zeros((), BF16))
    gh_t[...] = grad_hidden.T
    for k in range(4):
        rows = grad_hidden[k * ROWS : (k + 1) * ROWS].reshape(10, 16, C)
        t_own2[:, k, :, C:] = rows
        t_ext[0:10, k, :, C:] = rows
    pack_edges(t_own2, pack2)
    second = halo(pack2, hrecv2, 1)
    for copy in second:
        copy.start()
    on(1, (pass_on, 0))

    gradients(grad_one_at, 0, lambda n: on(1, (pass_on, 1)) if n == 2 else None)

    finish_halo(second, hrecv2, t_ext)
    each(0, 3, lambda dx: build(t_ext, dx))
    on(0, (pass_on, 0))
    on(1, (end_first, 0))
    acc_a[...] = jnp.zeros_like(acc_a)
    acc_b[...] = jnp.zeros_like(acc_b)
    each(0, 3, lambda n: forward((3 * n, 3 * n + 1, 3 * n + 2), w2))
    on(0, (pass_on, 1))
    on(1, (end_first, 1), (end_second, 0), (tail_after_z, 0))
    each(0, 3, lambda n: backward((3 * n, 3 * n + 1, 3 * n + 2), w1))
    on(1, (end_second, 1), (tail_after_x, 0))
    for k in range(4):
        rows = slice(k * ROWS, (k + 1) * ROWS)
        for n, acc in enumerate((acc_a, acc_b)):
            for half in range(2):
                nat[2 * n + half, pl.ds(k, ROWS, stride=4), :] = acc[rows, half * 128 : half * 128 + 128]
    masked = feat[...].reshape(640, C).astype(F32) * present
    out_v[...] = (jnp.concatenate([nat[0], nat[1]], axis=1) + masked).astype(BF16).reshape(10, 64, C)
    upstream = cot[...].reshape(640, C).astype(F32)
    back = jnp.concatenate([nat[2], nat[3]], axis=1)
    gf_v[...] = ((upstream + back) * present).astype(BF16).reshape(10, 64, C)
    stores = [pltpu.make_async_copy(out_v, out_hbm, osem.at[0]), pltpu.make_async_copy(gf_v, gf_hbm, osem.at[1])]
    for store in stores:
        store.start()

    on(0, (end_first, 0), (tail_after_z, 0), (end_first, 1), (end_second, 0), (tail_after_x, 0), (end_second, 1))
    for copy in tails_y:
        copy.wait_recv()
    tail = total(tail_y[y], *[tail_y_in[d] for d in range(3)]) * factor
    for _, copy in stage_z:
        copy.wait_recv()
    whole = total(zsend[z_hi, z_lo], *[zrecv[d] for d in range(7)]) * factor
    padded = jnp.concatenate([whole, tail, jnp.zeros((16, 128), F32)], axis=0)
    fin_t[...] = padded.T.reshape(8, 16, 128)

    stage_f = []
    for d in range(1, 8):
        to = (yc + d) % 8
        stage_f.append(remote(fin_t.at[to], fin_recv.at[d - 1], fs.at[d - 1], fr.at[d - 1], f_peers[d - 1]))
    for copy in stage_f:
        copy.start()
    fin_ref[yc] = fin_t[yc]
    for d in range(1, 8):
        stage_f[d - 1].wait_recv()
    for d in range(1, 8):
        fin_ref[(yc + 8 - d) % 8] = fin_recv[d - 1]

    sent = list(first) + list(second) + [copy for _, copy in stage_z + tails_z] + stage_f + tails_x + tails_y
    for h in range(2):
        sent += [copy for group in copies_of[h].values() for copy in group]
        sent += second_copies[h][0] + second_copies[h][1]
    for copy in sent:
        copy.wait_send()
    for store in stores:
        store.wait()

    each(0, 9, lambda g: to_peer(g).wait_send())


def closing(out_in, gf_in, fin, out_ref, gf_ref, g1_ref, g2_ref):
    out_ref[...] = out_in[...]
    gf_ref[...] = gf_in[...]
    for src_core, target in ((0, g1_ref), (1, g2_ref)):
        for src_y in range(4):
            part = fin[src_y * 2 + src_core]
            target[:, 96 * src_y : 96 * src_y + 96] = part[:, 0:96]
            if src_y < 3:
                target[:, 384 + 16 * src_y : 400 + 16 * src_y] = part[:, 96:112]


def per_device(features, cotangent, neighbour_table, send_lists, block_counts, weight_one, weight_two):
    factor = 1.0 / math.sqrt(lax.axis_size("dp") * lax.axis_size("slab") * 10 * 64)
    smem = pl.BlockSpec(memory_space=pltpu.SMEM)
    vmem = pl.BlockSpec(memory_space=pltpu.VMEM)
    hbm = pl.BlockSpec(memory_space=pl.ANY)
    dma = pltpu.SemaphoreType.DMA
    big = jax.ShapeDtypeStruct((10, 64, C), BF16)
    out, gf, fin = pl.pallas_call(
        lambda *refs: kernel(factor, *refs),
        out_shape=(big, big, jax.ShapeDtypeStruct((8, 16, 128), F32)),
        in_specs=[smem, smem, vmem, hbm, hbm, hbm, hbm],
        out_specs=(hbm, hbm, vmem),
        scratch_shapes=[
            pltpu.VMEM((9, 3, C, C), BF16),
            pltpu.VMEM((9, 3, C, C), BF16),
            pltpu.VMEM((10, 64, C), BF16),
            pltpu.VMEM((10, 64, C), BF16),
            pltpu.VMEM((10, 64, C), BF16),
            pltpu.VMEM((10, 64, C), BF16),
            pltpu.VMEM((4, 640, 128), F32),
            pltpu.VMEM((10, 4, 16, 2 * C), BF16),
            pltpu.VMEM((11, 4, 16, 2 * C), BF16),
            pltpu.VMEM((2, 2, 16, 2 * C), BF16),
            pltpu.VMEM((2, 2, 16, 2 * C), BF16),
            pltpu.VMEM((10, 4, 16, 2 * C), BF16),
            pltpu.VMEM((2, 2, 16, 2 * C), BF16),
            pltpu.VMEM((2, 2, 16, 2 * C), BF16),
            pltpu.VMEM((3, 3, 3 * ROWS, REACH), BF16),
            pltpu.VMEM((9, 6, ROWS, 2 * C), BF16),
            pltpu.VMEM((640, C), F32),
            pltpu.VMEM((640, C), F32),
            pltpu.VMEM((C, 640), BF16),
            pltpu.VMEM((C, 640), BF16),
            pltpu.VMEM((2, 6912, C), BF16),
            pltpu.VMEM((6912, C), BF16),
            pltpu.VMEM((2, 2, 384, 128), BF16),
            pltpu.VMEM((2, 2, 384, 128), BF16),
            pltpu.VMEM((2, 2, 384, 128), BF16),
            pltpu.VMEM((2, 2, 384, 128), BF16),
            pltpu.VMEM((2, 2, 4, 96, 128), BF16),
            pltpu.VMEM((2, 2, 4, 96, 128), BF16),
            pltpu.VMEM((2, 2, 4, 96, 128), BF16),
            pltpu.VMEM((2, 2, 4, 96, 128), BF16),
            pltpu.VMEM((2, 384, C), BF16),
            pltpu.VMEM((2, 4, 96, C), BF16),
            pltpu.VMEM((2, 3, 96, C), BF16),
            pltpu.VMEM((2, 3, 96, C), BF16),
            pltpu.VMEM((2, 4, 96, 128), BF16),
            pltpu.VMEM((7, 96, 128), BF16),
            pltpu.VMEM((2, 4, 4, 48, 128), BF16),
            pltpu.VMEM((7, 4, 48, 128), BF16),
            pltpu.VMEM((4, 48, 128), BF16),
            pltpu.VMEM((3, 48, 128), BF16),
            pltpu.VMEM((4, 16, 128), BF16),
            pltpu.VMEM((3, 16, 128), BF16),
            pltpu.VMEM((8, 16, 128), F32),
            pltpu.VMEM((7, 16, 128), F32),
            dma((4,)),
            dma((2,)),
            dma((2, 2)),
            dma((2, 2)),
            dma((9,)),
            dma((9,)),
            dma((2, 3, 2)),
            dma((2, 3, 2)),
            dma((2, 3, 2, 4)),
            dma((2, 3, 2, 4)),
            dma((2, 3)),
            dma((2, 3)),
            dma((2, 3)),
            dma((2, 3)),
            dma((7,)),
            dma((7,)),
            dma((7,)),
            dma((7,)),
            dma((7,)),
            dma((7,)),
            dma((3,)),
            dma((3,)),
            dma((3,)),
            dma((3,)),
        ],
        compiler_params=pltpu.CompilerParams(
            collective_id=0, has_side_effects=True, vmem_limit_bytes=60 * 1024 * 1024
        ),
        name="step",
    )(
        block_counts,
        send_lists[0, 0],
        jnp.transpose(neighbour_table, (1, 0, 2)),
        features[0],
        cotangent[0],
        weight_one.reshape(9, 3, C, C),
        weight_two.reshape(9, 3, C, C),
    )
    piece = jax.ShapeDtypeStruct((16, 432), F32)
    out, gf, g1, g2 = pl.pallas_call(
        closing,
        out_shape=(big, big, piece, piece),
        in_specs=[vmem, vmem, vmem],
        out_specs=(vmem, vmem, vmem, vmem),
        name="closing",
    )(out, gf, fin)
    return (out[None], gf[None], g1.T, g2.T)


def solution(mesh):
    in_specs = (
        P("dp", "slab", None, None),
        P("dp", "slab", None, None),
        P("dp", "slab", None),
        P("dp", "slab", None, None),
        P("dp", "slab"),
        P(),
        P(),
    )
    out_specs = (
        P("dp", "slab", None, None),
        P("dp", "slab", None, None),
        P("slab", "dp"),
        P("slab", "dp"),
    )
    return jax.shard_map(
        per_device, mesh=mesh, in_specs=in_specs, out_specs=out_specs, check_vma=False
    )
```

```python
import math

import jax
import jax.numpy as jnp
from jax import lax
from jax.experimental import pallas as pl
from jax.experimental.pallas import tpu as pltpu
from jax.sharding import PartitionSpec as P

F32 = jnp.float32
BF16 = jnp.bfloat16
MESH = pl.DeviceIdType.MESH
ROWS = 160
REACH = 176
C = 256
NT = (((1,), (1,)), ((), ()))
TN = (((0,), (0,)), ((), ()))


def dot(a, b, dims=(((1,), (0,)), ((), ()))):
    return lax.dot_general(a, b, dims, preferred_element_type=F32)


def kernel(
    factor,
    counts, lists, table_ref, feat_hbm, cot_hbm, w1_hbm, w2_hbm,
    out_hbm, gf_hbm, fin_ref,
    w1, w2, feat, cot, out_v, gf_v, nat, t_own, t_ext, pack, hrecv, t_own2, pack2, hrecv2, sel, win, acc_a, acc_b,
    hid_t, gh_t, mine, precv, relay_a, direct_a, summed_a, stage_a, relay_b, direct_b, summed_b, stage_b,
    sum_a, sum_b, recv_a2, recv_b2, zsend, zrecv,
    tail_z, tail_z_in, tail_x, tail_x_in, tail_y, tail_y_in, fin_t, fin_recv,
    lsem, osem, hs, hr, ps, pr, as_, ar, bs, br, a2s, a2r, b2s, b2r, zs, zr, fs, fr, tzs, tzr, txs, txr, tys, tyr,
):
    loads = [
        pltpu.make_async_copy(source, target, lsem.at[n])
        for n, (source, target) in enumerate(((feat_hbm, feat), (cot_hbm, cot), (w1_hbm, w1), (w2_hbm, w2)))
    ]
    for load in loads:
        load.start()

    dp = lax.axis_index("dp")
    slab = lax.axis_index("slab")
    core = dp % 2
    y = dp // 2 % 4
    z_hi = dp // 8
    x = slab % 4
    z_lo = slab // 4
    z = z_hi * 4 + z_lo

    def dev(x_=x, y_=y, z_=z, core_=core):
        return ((z_ // 4) * 8 + y_ * 2 + core_, (z_ % 4) * 4 + x_)

    after = (slab + 1) % 16
    before = (slab + 15) % 16
    peer = dev(core_=1 - core)
    x_peers = [dev(x_=(x + d) % 4) for d in range(1, 4)]
    y_peers = [dev(y_=(y + d) % 4) for d in range(1, 4)]
    z_peers = [dev(z_=(z + d) % 8) for d in range(1, 8)]
    yc = y * 2 + core
    f_peers = [dev(y_=(yc + d) % 8 // 2, core_=(yc + d) % 2) for d in range(1, 8)]

    barrier = pltpu.get_barrier_semaphore()
    everyone = [(dp, after), (dp, before)] + x_peers + z_peers + f_peers
    for d in everyone:
        pl.semaphore_signal(barrier, inc=1, device_id=d, device_id_type=MESH)

    def remote(src, dst, send, recv, to):
        return pltpu.make_async_remote_copy(
            src_ref=src, dst_ref=dst, send_sem=send, recv_sem=recv, device_id=to, device_id_type=MESH
        )

    row = lax.broadcasted_iota(jnp.int32, (640, 1), 0)
    present = jnp.where(row < counts[0, 0] * 64, 1.0, 0.0)
    loads[0].wait()
    loads[1].wait()
    for part, value in (
        (0, feat[...].reshape(640, C).astype(F32) * present),
        (2, cot[...].reshape(640, C).astype(F32)),
    ):
        nat[part], nat[part + 1] = value[:, 0:128], value[:, 128:]
    for k in range(4):
        part = jnp.concatenate([nat[n, pl.ds(k, ROWS, stride=4), :] for n in range(4)], axis=1)
        part = part.astype(BF16).reshape(10, 16, 2 * C)
        t_own[:, k] = part
        t_ext[0:10, k] = part

    def pack_edges(source, target):
        for side in range(2):
            inside = jnp.where(side == 0, slab > 0, slab < 15)
            for q in range(2):
                named = lists[side, q]
                keep = jnp.where(inside & (named < 10), 1.0, 0.0)
                block = source[jnp.minimum(named, 9)].astype(F32) * keep
                plane = [block[k, 12 * side : 12 * side + 4] for k in range(4)]
                target[side, q] = jnp.concatenate(plane, axis=0).astype(BF16)

    def halo(source, target, e):
        return (
            remote(source.at[1], target.at[0], hs.at[e, 0], hr.at[e, 0], (dp, after)),
            remote(source.at[0], target.at[1], hs.at[e, 1], hr.at[e, 1], (dp, before)),
        )

    pack_edges(t_own, pack)
    pl.semaphore_wait(barrier, len(everyone))
    first = halo(pack, hrecv, 0)
    for copy in first:
        copy.start()

    r = lax.broadcasted_iota(jnp.int32, (ROWS, 1), 0)
    spread = (r // 16 == lax.broadcasted_iota(jnp.int32, (ROWS, 10), 1)).astype(BF16)
    rows_of = dot(spread, table_ref[...].reshape(10, 27).astype(BF16)).astype(BF16)
    named = lax.broadcasted_iota(jnp.int32, (27, 27), 0)

    def step_of(shape):
        m = lax.broadcasted_iota(jnp.int32, shape, 1)
        return m // 9, m // 3 % 3, m % 3

    step_x, step_y, step_z = step_of((27, 27))
    low = (jnp.minimum(step_x, 1), jnp.minimum(step_y, 1))
    high = (jnp.maximum(step_x, 1), jnp.maximum(step_y, 1))

    def blocks(bx, by):
        return dot(rows_of, (named == 9 * bx + 3 * by + step_z).astype(BF16))

    step_x, step_y, _ = step_of((ROWS, 27))
    at_x, at_y = r // 4 % 4 + step_x - 1, r % 4 + step_y - 1
    first_x = at_x < jnp.where(step_x == 0, 0, 4)
    first_y = at_y < jnp.where(step_y == 0, 0, 4)
    block = jnp.where(
        first_x,
        jnp.where(first_y, blocks(low[0], low[1]), blocks(low[0], high[1])),
        jnp.where(first_y, blocks(high[0], low[1]), blocks(high[0], high[1])),
    ).astype(jnp.int32)
    spot_y = (at_y + 4) % 4
    from_own = block * 16 + (at_x + 4) % 4 * 4 + spot_y
    source = jnp.where(block < 10, from_own, 160 + (block - 10) * 4 + spot_y)
    lane = lax.broadcasted_iota(jnp.int32, (ROWS, REACH), 1)
    for m in range(27):
        chosen = jnp.where(lane == source[:, m : m + 1], 1.0, 0.0).astype(BF16)
        sel[m // 9, m % 3, m // 3 % 3 * ROWS : (m // 3 % 3 + 1) * ROWS] = chosen

    def finish_halo(copies, received, ext):
        for copy in copies:
            copy.wait_recv()
        planes = [received[side, q].astype(F32) for side in range(2) for q in range(2)]
        for k in range(4):
            ext[10, k] = jnp.concatenate([plane[4 * k : 4 * k + 4] for plane in planes], axis=0).astype(BF16)

    def build(ext, dx):
        for k in range(4):
            parts = [(k + 1, 1)] + ([(5, 2)] if k == 0 else [(0, 0)] if k == 3 else [])
            left = jnp.concatenate([sel[dx, bz] for _, bz in parts], axis=0)
            rows = dot(left, ext[:, k].reshape(REACH, 2 * C)).astype(BF16)
            for n, (spot, _) in enumerate(parts):
                for dy in range(3):
                    at = (3 * n + dy) * ROWS
                    win[dx * 3 + dy, spot] = rows[at : at + ROWS]

    def view(g, dz, low):
        return win[g, dz : dz + 4, :, low : low + C].reshape(640, C)

    def views(gs, low):
        return jnp.concatenate([view(g, dz, low) for g in gs for dz in range(3)], axis=1)

    def forward(gs, w):
        right = jnp.concatenate([w[g].reshape(3 * C, C) for g in gs], axis=0)
        acc_a[...] += dot(views(gs, 0), right)

    def backward(gs, w):
        right = jnp.concatenate([w[8 - g, 2 - dz] for g in gs for dz in range(3)], axis=1)
        acc_b[...] += dot(views(gs, C), right, NT)

    def each(start, end, step):
        def one(n, carry):
            step(n)
            return carry

        lax.fori_loop(start, end, one, 0)

    def sides(step):
        each(0, 3, lambda n: step((n, n + 6)))

    acc_a[...] = jnp.zeros_like(acc_a)
    acc_b[...] = jnp.zeros_like(acc_b)
    for k in range(4):
        t_ext[10, k] = jnp.zeros((16, 2 * C), BF16)
    build(t_ext, 1)
    loads[2].wait()
    forward((3, 4, 5), w1)
    loads[3].wait()
    backward((3, 4, 5), w2)
    finish_halo(first, hrecv, t_ext)
    each(0, 2, lambda n: build(t_ext, 2 * n))
    sides(lambda gs: forward(gs, w1))

    hidden = jnp.maximum(acc_a[...], 0.0)
    hid_t[...] = hidden.T.astype(BF16)
    hidden = hidden.astype(BF16)
    for k in range(4):
        rows = hidden[k * ROWS : (k + 1) * ROWS].reshape(10, 16, C)
        t_own2[:, k, :, 0:C] = rows
        t_ext[0:10, k, :, 0:C] = rows

    def three(g):
        return pl.ds(pl.multiple_of(g * 768, 768), 768)

    def to_peer(g):
        return remote(mine.at[1, three(g)], precv.at[three(g)], ps.at[g], pr.at[g], peer)

    def grad_two_at(g):
        value = dot(hid_t[...], jnp.concatenate([view(8 - g, 2 - dz, C) for dz in range(3)], axis=1)).astype(BF16)
        for dz in range(3):
            mine[1 - core, pl.ds(g * 768 + dz * C, C)] = value[:, dz * C : dz * C + C]

    def grad_one_at(g):
        mine[core, three(g)] = dot(gh_t[...], views((g,), 0)).astype(BF16).T

    def join(g):
        to_peer(g).wait_recv()
        for n in range(3):
            at = pl.ds(g * 768 + n * C, C)
            xy[at] = (xy[at].astype(F32) + precv[at].astype(F32)).astype(BF16)

    xy = mine.at[0]

    def rows_at(start, size):
        return pl.ds(pl.multiple_of(start, 16), size)

    def slab_rows(zl, owner_x):
        return rows_at(432 * (zl * 4 + owner_x), 384)

    def part_rows(zl, s, owner_y):
        return rows_at(432 * (zl * 4 + s) + 96 * owner_y, 96)

    LOW, HIGH = slice(0, 128), slice(128, 256)
    next_x, last_x, far_x = (x + 1) % 4, (x + 3) % 4, (x + 2) % 4
    next_y, last_y, far_y = (y + 1) % 4, (y + 3) % 4, (y + 2) % 4

    def first_copies(h):
        copies = {}
        for phase, (buf_a, buf_b) in enumerate(((relay_a, relay_b), (direct_a, direct_b))):
            for way in range(2):
                to_x, to_y = (x_peers[0], y_peers[0]) if way == 0 else (x_peers[2], y_peers[2])
                if phase == 0:
                    owner_x, owner_y, lanes = far_x, far_y, LOW if way == 0 else HIGH
                else:
                    owner_x, owner_y = (next_x, next_y) if way == 0 else (last_x, last_y)
                    lanes = HIGH if way == 0 else LOW
                copies[phase, way] = [
                    remote(
                        xy.at[slab_rows(h, owner_x), lanes], buf_a.at[h, way],
                        as_.at[h, phase, way], ar.at[h, phase, way], to_x,
                    )
                ] + [
                    remote(
                        xy.at[part_rows(3 - h, s, owner_y), lanes], buf_b.at[h, way, s],
                        bs.at[h, phase, way, s], br.at[h, phase, way, s], to_y,
                    )
                    for s in range(4)
                ]
        for way in range(2):
            to_x, to_y = (x_peers[0], y_peers[0]) if way == 0 else (x_peers[2], y_peers[2])
            copies[2, way] = [
                remote(stage_a.at[h, way], summed_a.at[h, way], as_.at[h, 2, way], ar.at[h, 2, way], to_x),
                remote(stage_b.at[h, way], summed_b.at[h, way], bs.at[h, 2, way, 0], br.at[h, 2, way, 0], to_y),
            ]
        return copies

    copies_of = [first_copies(0), first_copies(1)]

    def start_slab(s):
        h = min(s // 4, 3 - s // 4)
        for way in range(2):
            if s < 8:
                owner = next_x if way == 0 else last_x

                @pl.when(far_x == s % 4)
                def _():
                    copies_of[h][0, way][0].start()

                @pl.when(owner == s % 4)
                def _():
                    copies_of[h][1, way][0].start()

            else:
                for phase in range(2):
                    copies_of[h][phase, way][1 + s % 4].start()

    def total(*parts):
        value = parts[0].astype(F32)
        for part in parts[1:]:
            value = value + part.astype(F32)
        return value

    def pass_on(h):
        for way in range(2):
            for copy in copies_of[h][0, way]:
                copy.wait_recv()
        for way, lanes, owner_x, owner_y in ((0, LOW, next_x, next_y), (1, HIGH, last_x, last_y)):
            stage_a[h, way] = total(xy[slab_rows(h, owner_x), lanes], relay_a[h, way]).astype(BF16)
            for s in range(4):
                own = xy[part_rows(3 - h, s, owner_y), lanes]
                stage_b[h, way, s] = total(own, relay_b[h, way, s]).astype(BF16)
            for copy in copies_of[h][2, way]:
                copy.start()

    second_copies = []
    for h in range(2):
        to_y = [
            remote(
                sum_a.at[h, rows_at(96 * ((y + d) % 4), 96)], recv_a2.at[h, d - 1], a2s.at[h, d - 1], a2r.at[h, d - 1],
                y_peers[d - 1],
            )
            for d in (2, 1, 3)
        ]
        to_x = [
            remote(sum_b.at[h, (x + d) % 4], recv_b2.at[h, d - 1], b2s.at[h, d - 1], b2r.at[h, d - 1], x_peers[d - 1])
            for d in (2, 1, 3)
        ]
        second_copies.append((to_y, to_x))

    def end_first(h):
        for phase in (1, 2):
            for way in range(2):
                for copy in copies_of[h][phase, way]:
                    copy.wait_recv()
        for lanes, a, b, a_buf, b_buf in (
            (LOW, summed_a, direct_a, 0, 1),
            (HIGH, direct_a, summed_a, 0, 1),
        ):
            value = total(xy[slab_rows(h, x), lanes], a[h, a_buf], b[h, b_buf])
            sum_a[h, :, lanes] = value.astype(BF16)
        for copy in second_copies[h][0]:
            copy.start()
        for s in range(4):
            for lanes, a, b in ((LOW, summed_b, direct_b), (HIGH, direct_b, summed_b)):
                value = total(xy[part_rows(3 - h, s, y), lanes], a[h, 0, s], b[h, 1, s])
                sum_b[h, s, :, lanes] = value.astype(BF16)
        for copy in second_copies[h][1]:
            copy.start()

    stage_z = []
    for d in (4, 3, 5, 2, 6, 1, 7):
        to = (z + d) % 8
        copy = remote(zsend.at[to // 4, to % 4], zrecv.at[d - 1], zs.at[d - 1], zr.at[d - 1], z_peers[d - 1])
        stage_z.append((to, copy))

    def end_second(h):
        for copy in second_copies[h][0]:
            copy.wait_recv()
        full = total(sum_a[h, rows_at(96 * y, 96)], *[recv_a2[h, d] for d in range(3)]).astype(BF16)
        zsend[0, h], zsend[1, h] = full[:, LOW], full[:, HIGH]
        for copy in second_copies[h][1]:
            copy.wait_recv()
        full = total(sum_b[h, x], *[recv_b2[h, d] for d in range(3)]).astype(BF16)
        zsend[0, 3 - h], zsend[1, 3 - h] = full[:, LOW], full[:, HIGH]
        for to, copy in stage_z:
            outer = (to % 4 == 0) | (to % 4 == 3)

            @pl.when(outer if h == 0 else jnp.logical_not(outer))
            def _():
                copy.start()

    tails_z = []
    for d in (4, 3, 5, 2, 6, 1, 7):
        to = (z + d) % 8
        copy = remote(tail_z.at[to // 4, to % 4], tail_z_in.at[d - 1], tzs.at[d - 1], tzr.at[d - 1], z_peers[d - 1])
        tails_z.append((to, copy))
    tails_x = [
        remote(tail_x.at[(x + d) % 4], tail_x_in.at[d - 1], txs.at[d - 1], txr.at[d - 1], x_peers[d - 1]) for d in (2, 1, 3)
    ]
    tails_y = [
        remote(tail_y.at[(y + d) % 4], tail_y_in.at[d - 1], tys.at[d - 1], tyr.at[d - 1], y_peers[d - 1]) for d in (2, 1, 3)
    ]

    def pack_tail(s):
        rows = xy[432 * s + 384 : 432 * s + 432]
        tail_z[0, s // 4, s % 4], tail_z[1, s // 4, s % 4] = rows[:, LOW], rows[:, HIGH]

    def start_tails(h):
        for to, copy in tails_z:
            outer = (to % 4 == 0) | (to % 4 == 3)

            @pl.when(outer if h == 0 else jnp.logical_not(outer))
            def _():
                copy.start()

    def tail_after_z(_):
        for _, copy in tails_z:
            copy.wait_recv()
        for s in range(4):
            tail_x[s] = total(tail_z[z_hi, z_lo, s], *[tail_z_in[d, s] for d in range(7)]).astype(BF16)
        for copy in tails_x:
            copy.start()

    def tail_after_x(_):
        for copy in tails_x:
            copy.wait_recv()
        value = total(tail_x[x], *[tail_x_in[d] for d in range(3)]).astype(BF16)
        for part in range(3):
            tail_y[part] = value[16 * part : 16 * part + 16]
        tail_y[3] = jnp.zeros((16, 128), BF16)
        for copy in tails_y:
            copy.start()

    def on(which, *steps):
        @pl.when(core == which)
        def _():
            for step, arg in steps:
                step(arg)

    READY = ((0, 15), (1, 14, 2, 13), (3, 12, 4, 11), (5, 10, 6, 9), (7, 8))

    def gradients(at, keeper, between):
        def finish(n):
            for g in (n, 8 - n) if n < 4 else (4,):
                join(g)
            for s in READY[n]:
                start_slab(s)
                pack_tail(s)
            if n in (2, 4):
                start_tails(0 if n == 2 else 1)

        def send(g):
            to_peer(g).start()

        for n in range(5):
            gs = (n, 8 - n) if n < 4 else (4,)
            for g in gs:
                at(g)
            on(1 - keeper, *[(send, g) for g in gs])
            if n > 0:
                on(keeper, (finish, n - 1))
            between(n)
        on(keeper, (finish, 4))

    gradients(grad_two_at, 1, lambda n: None)

    sides(lambda gs: backward(gs, w2))
    grad_hidden = jnp.where(hidden > 0, acc_b[...].astype(BF16), jnp.zeros((), BF16))
    gh_t[...] = grad_hidden.T
    for k in range(4):
        rows = grad_hidden[k * ROWS : (k + 1) * ROWS].reshape(10, 16, C)
        t_own2[:, k, :, C:] = rows
        t_ext[0:10, k, :, C:] = rows
    pack_edges(t_own2, pack2)
    second = halo(pack2, hrecv2, 1)
    for copy in second:
        copy.start()
    on(1, (pass_on, 0))

    gradients(grad_one_at, 0, lambda n: on(1, (pass_on, 1)) if n == 2 else None)

    finish_halo(second, hrecv2, t_ext)
    each(0, 3, lambda dx: build(t_ext, dx))
    on(0, (pass_on, 0), (pass_on, 1))
    on(1, (end_first, 0))
    acc_a[...] = jnp.zeros_like(acc_a)
    acc_b[...] = jnp.zeros_like(acc_b)
    each(0, 3, lambda n: forward((3 * n, 3 * n + 1, 3 * n + 2), w2))
    on(0, (end_first, 0), (tail_after_z, 0), (end_first, 1))
    on(1, (end_first, 1), (end_second, 0), (tail_after_z, 0))
    each(0, 3, lambda n: backward((3 * n, 3 * n + 1, 3 * n + 2), w1))
    on(1, (end_second, 1), (tail_after_x, 0))
    on(0, (end_second, 0), (tail_after_x, 0), (end_second, 1))
    for k in range(4):
        rows = slice(k * ROWS, (k + 1) * ROWS)
        for n, acc in enumerate((acc_a, acc_b)):
            for half in range(2):
                nat[2 * n + half, pl.ds(k, ROWS, stride=4), :] = acc[rows, half * 128 : half * 128 + 128]
    masked = feat[...].reshape(640, C).astype(F32) * present
    out_v[...] = (jnp.concatenate([nat[0], nat[1]], axis=1) + masked).astype(BF16).reshape(10, 64, C)
    upstream = cot[...].reshape(640, C).astype(F32)
    back = jnp.concatenate([nat[2], nat[3]], axis=1)
    gf_v[...] = ((upstream + back) * present).astype(BF16).reshape(10, 64, C)
    stores = [pltpu.make_async_copy(out_v, out_hbm, osem.at[0]), pltpu.make_async_copy(gf_v, gf_hbm, osem.at[1])]
    for store in stores:
        store.start()

    for copy in tails_y:
        copy.wait_recv()
    tail = total(tail_y[y], *[tail_y_in[d] for d in range(3)]) * factor
    for _, copy in stage_z:
        copy.wait_recv()
    whole = total(zsend[z_hi, z_lo], *[zrecv[d] for d in range(7)]) * factor
    padded = jnp.concatenate([whole, tail, jnp.zeros((16, 128), F32)], axis=0)
    fin_t[...] = padded.T.reshape(8, 16, 128)

    stage_f = []
    for d in range(1, 8):
        to = (yc + d) % 8
        stage_f.append(remote(fin_t.at[to], fin_recv.at[d - 1], fs.at[d - 1], fr.at[d - 1], f_peers[d - 1]))
    for copy in stage_f:
        copy.start()
    fin_ref[yc] = fin_t[yc]
    for d in range(1, 8):
        stage_f[d - 1].wait_recv()
    for d in range(1, 8):
        fin_ref[(yc + 8 - d) % 8] = fin_recv[d - 1]

    sent = list(first) + list(second) + [copy for _, copy in stage_z + tails_z] + stage_f + tails_x + tails_y
    for h in range(2):
        sent += [copy for group in copies_of[h].values() for copy in group]
        sent += second_copies[h][0] + second_copies[h][1]
    for copy in sent:
        copy.wait_send()
    for store in stores:
        store.wait()

    each(0, 9, lambda g: to_peer(g).wait_send())


def closing(out_in, gf_in, fin, out_ref, gf_ref, g1_ref, g2_ref):
    out_ref[...] = out_in[...]
    gf_ref[...] = gf_in[...]
    for src_core, target in ((0, g1_ref), (1, g2_ref)):
        for src_y in range(4):
            part = fin[src_y * 2 + src_core]
            target[:, 96 * src_y : 96 * src_y + 96] = part[:, 0:96]
            if src_y < 3:
                target[:, 384 + 16 * src_y : 400 + 16 * src_y] = part[:, 96:112]


def per_device(features, cotangent, neighbour_table, send_lists, block_counts, weight_one, weight_two):
    factor = 1.0 / math.sqrt(lax.axis_size("dp") * lax.axis_size("slab") * 10 * 64)
    smem = pl.BlockSpec(memory_space=pltpu.SMEM)
    vmem = pl.BlockSpec(memory_space=pltpu.VMEM)
    hbm = pl.BlockSpec(memory_space=pl.ANY)
    dma = pltpu.SemaphoreType.DMA
    big = jax.ShapeDtypeStruct((10, 64, C), BF16)
    out, gf, fin = pl.pallas_call(
        lambda *refs: kernel(factor, *refs),
        out_shape=(big, big, jax.ShapeDtypeStruct((8, 16, 128), F32)),
        in_specs=[smem, smem, vmem, hbm, hbm, hbm, hbm],
        out_specs=(hbm, hbm, vmem),
        scratch_shapes=[
            pltpu.VMEM((9, 3, C, C), BF16),
            pltpu.VMEM((9, 3, C, C), BF16),
            pltpu.VMEM((10, 64, C), BF16),
            pltpu.VMEM((10, 64, C), BF16),
            pltpu.VMEM((10, 64, C), BF16),
            pltpu.VMEM((10, 64, C), BF16),
            pltpu.VMEM((4, 640, 128), F32),
            pltpu.VMEM((10, 4, 16, 2 * C), BF16),
            pltpu.VMEM((11, 4, 16, 2 * C), BF16),
            pltpu.VMEM((2, 2, 16, 2 * C), BF16),
            pltpu.VMEM((2, 2, 16, 2 * C), BF16),
            pltpu.VMEM((10, 4, 16, 2 * C), BF16),
            pltpu.VMEM((2, 2, 16, 2 * C), BF16),
            pltpu.VMEM((2, 2, 16, 2 * C), BF16),
            pltpu.VMEM((3, 3, 3 * ROWS, REACH), BF16),
            pltpu.VMEM((9, 6, ROWS, 2 * C), BF16),
            pltpu.VMEM((640, C), F32),
            pltpu.VMEM((640, C), F32),
            pltpu.VMEM((C, 640), BF16),
            pltpu.VMEM((C, 640), BF16),
            pltpu.VMEM((2, 6912, C), BF16),
            pltpu.VMEM((6912, C), BF16),
            pltpu.VMEM((2, 2, 384, 128), BF16),
            pltpu.VMEM((2, 2, 384, 128), BF16),
            pltpu.VMEM((2, 2, 384, 128), BF16),
            pltpu.VMEM((2, 2, 384, 128), BF16),
            pltpu.VMEM((2, 2, 4, 96, 128), BF16),
            pltpu.VMEM((2, 2, 4, 96, 128), BF16),
            pltpu.VMEM((2, 2, 4, 96, 128), BF16),
            pltpu.VMEM((2, 2, 4, 96, 128), BF16),
            pltpu.VMEM((2, 384, C), BF16),
            pltpu.VMEM((2, 4, 96, C), BF16),
            pltpu.VMEM((2, 3, 96, C), BF16),
            pltpu.VMEM((2, 3, 96, C), BF16),
            pltpu.VMEM((2, 4, 96, 128), BF16),
            pltpu.VMEM((7, 96, 128), BF16),
            pltpu.VMEM((2, 4, 4, 48, 128), BF16),
            pltpu.VMEM((7, 4, 48, 128), BF16),
            pltpu.VMEM((4, 48, 128), BF16),
            pltpu.VMEM((3, 48, 128), BF16),
            pltpu.VMEM((4, 16, 128), BF16),
            pltpu.VMEM((3, 16, 128), BF16),
            pltpu.VMEM((8, 16, 128), F32),
            pltpu.VMEM((7, 16, 128), F32),
            dma((4,)),
            dma((2,)),
            dma((2, 2)),
            dma((2, 2)),
            dma((9,)),
            dma((9,)),
            dma((2, 3, 2)),
            dma((2, 3, 2)),
            dma((2, 3, 2, 4)),
            dma((2, 3, 2, 4)),
            dma((2, 3)),
            dma((2, 3)),
            dma((2, 3)),
            dma((2, 3)),
            dma((7,)),
            dma((7,)),
            dma((7,)),
            dma((7,)),
            dma((7,)),
            dma((7,)),
            dma((3,)),
            dma((3,)),
            dma((3,)),
            dma((3,)),
        ],
        compiler_params=pltpu.CompilerParams(
            collective_id=0, has_side_effects=True, vmem_limit_bytes=60 * 1024 * 1024
        ),
        name="step",
    )(
        block_counts,
        send_lists[0, 0],
        jnp.transpose(neighbour_table, (1, 0, 2)),
        features[0],
        cotangent[0],
        weight_one.reshape(9, 3, C, C),
        weight_two.reshape(9, 3, C, C),
    )
    piece = jax.ShapeDtypeStruct((16, 432), F32)
    out, gf, g1, g2 = pl.pallas_call(
        closing,
        out_shape=(big, big, piece, piece),
        in_specs=[vmem, vmem, vmem],
        out_specs=(vmem, vmem, vmem, vmem),
        name="closing",
    )(out, gf, fin)
    return (out[None], gf[None], g1.T, g2.T)


def solution(mesh):
    in_specs = (
        P("dp", "slab", None, None),
        P("dp", "slab", None, None),
        P("dp", "slab", None),
        P("dp", "slab", None, None),
        P("dp", "slab"),
        P(),
        P(),
    )
    out_specs = (
        P("dp", "slab", None, None),
        P("dp", "slab", None, None),
        P("slab", "dp"),
        P("slab", "dp"),
    )
    return jax.shard_map(
        per_device, mesh=mesh, in_specs=in_specs, out_specs=out_specs, check_vma=False
    )
```

```python
import math

import jax
import jax.numpy as jnp
from jax import lax
from jax.experimental import pallas as pl
from jax.experimental.pallas import tpu as pltpu
from jax.sharding import PartitionSpec as P

F32 = jnp.float32
BF16 = jnp.bfloat16
MESH = pl.DeviceIdType.MESH
ROWS = 160
REACH = 176
C = 256
NT = (((1,), (1,)), ((), ()))
TN = (((0,), (0,)), ((), ()))


def dot(a, b, dims=(((1,), (0,)), ((), ()))):
    return lax.dot_general(a, b, dims, preferred_element_type=F32)


def kernel(
    factor,
    counts, lists, table_ref, feat_hbm, cot_hbm, w1_hbm, w2_hbm,
    out_hbm, gf_hbm, fin_ref,
    w1, w2, feat, cot, out_v, gf_v, nat, t_own, t_ext, pack, hrecv, t_own2, pack2, hrecv2, sel, win, acc_a, acc_b,
    hid_t, gh_t, mine, precv, relay_a, direct_a, summed_a, stage_a, relay_b, direct_b, summed_b, stage_b,
    sum_a, sum_b, recv_a2, recv_b2, zsend, zrecv,
    tail_z, tail_z_in, tail_x, tail_x_in, tail_y, tail_y_in, fin_t, fin_recv,
    lsem, osem, hs, hr, ps, pr, as_, ar, bs, br, a2s, a2r, b2s, b2r, zs, zr, fs, fr, tzs, tzr, txs, txr, tys, tyr,
):
    loads = [
        pltpu.make_async_copy(source, target, lsem.at[n])
        for n, (source, target) in enumerate(((feat_hbm, feat), (cot_hbm, cot), (w1_hbm, w1), (w2_hbm, w2)))
    ]
    for load in loads:
        load.start()

    dp = lax.axis_index("dp")
    slab = lax.axis_index("slab")
    core = dp % 2
    y = dp // 2 % 4
    z_hi = dp // 8
    x = slab % 4
    z_lo = slab // 4
    z = z_hi * 4 + z_lo

    def dev(x_=x, y_=y, z_=z, core_=core):
        return ((z_ // 4) * 8 + y_ * 2 + core_, (z_ % 4) * 4 + x_)

    after = (slab + 1) % 16
    before = (slab + 15) % 16
    peer = dev(core_=1 - core)
    x_peers = [dev(x_=(x + d) % 4) for d in range(1, 4)]
    y_peers = [dev(y_=(y + d) % 4) for d in range(1, 4)]
    z_peers = [dev(z_=(z + d) % 8) for d in range(1, 8)]
    yc = y * 2 + core
    f_peers = [dev(y_=(yc + d) % 8 // 2, core_=(yc + d) % 2) for d in range(1, 8)]

    barrier = pltpu.get_barrier_semaphore()
    everyone = [(dp, after), (dp, before)] + x_peers + z_peers + f_peers
    for d in everyone:
        pl.semaphore_signal(barrier, inc=1, device_id=d, device_id_type=MESH)

    def remote(src, dst, send, recv, to):
        return pltpu.make_async_remote_copy(
            src_ref=src, dst_ref=dst, send_sem=send, recv_sem=recv, device_id=to, device_id_type=MESH
        )

    row = lax.broadcasted_iota(jnp.int32, (640, 1), 0)
    present = jnp.where(row < counts[0, 0] * 64, 1.0, 0.0)
    loads[0].wait()
    loads[1].wait()
    for part, value in (
        (0, feat[...].reshape(640, C).astype(F32) * present),
        (2, cot[...].reshape(640, C).astype(F32)),
    ):
        nat[part], nat[part + 1] = value[:, 0:128], value[:, 128:]
    for k in range(4):
        part = jnp.concatenate([nat[n, pl.ds(k, ROWS, stride=4), :] for n in range(4)], axis=1)
        part = part.astype(BF16).reshape(10, 16, 2 * C)
        t_own[:, k] = part
        t_ext[0:10, k] = part

    def pack_edges(source, target):
        for side in range(2):
            inside = jnp.where(side == 0, slab > 0, slab < 15)
            for q in range(2):
                named = lists[side, q]
                keep = jnp.where(inside & (named < 10), 1.0, 0.0)
                block = source[jnp.minimum(named, 9)].astype(F32) * keep
                plane = [block[k, 12 * side : 12 * side + 4] for k in range(4)]
                target[side, q] = jnp.concatenate(plane, axis=0).astype(BF16)

    def halo(source, target, e):
        return (
            remote(source.at[1], target.at[0], hs.at[e, 0], hr.at[e, 0], (dp, after)),
            remote(source.at[0], target.at[1], hs.at[e, 1], hr.at[e, 1], (dp, before)),
        )

    pack_edges(t_own, pack)
    pl.semaphore_wait(barrier, len(everyone))
    first = halo(pack, hrecv, 0)
    for copy in first:
        copy.start()

    r = lax.broadcasted_iota(jnp.int32, (ROWS, 1), 0)
    spread = (r // 16 == lax.broadcasted_iota(jnp.int32, (ROWS, 10), 1)).astype(BF16)
    rows_of = dot(spread, table_ref[...].reshape(10, 27).astype(BF16)).astype(BF16)
    named = lax.broadcasted_iota(jnp.int32, (27, 27), 0)

    def step_of(shape):
        m = lax.broadcasted_iota(jnp.int32, shape, 1)
        return m // 9, m // 3 % 3, m % 3

    step_x, step_y, step_z = step_of((27, 27))
    low = (jnp.minimum(step_x, 1), jnp.minimum(step_y, 1))
    high = (jnp.maximum(step_x, 1), jnp.maximum(step_y, 1))

    def blocks(bx, by):
        return dot(rows_of, (named == 9 * bx + 3 * by + step_z).astype(BF16))

    step_x, step_y, _ = step_of((ROWS, 27))
    at_x, at_y = r // 4 % 4 + step_x - 1, r % 4 + step_y - 1
    first_x = at_x < jnp.where(step_x == 0, 0, 4)
    first_y = at_y < jnp.where(step_y == 0, 0, 4)
    block = jnp.where(
        first_x,
        jnp.where(first_y, blocks(low[0], low[1]), blocks(low[0], high[1])),
        jnp.where(first_y, blocks(high[0], low[1]), blocks(high[0], high[1])),
    ).astype(jnp.int32)
    spot_y = (at_y + 4) % 4
    from_own = block * 16 + (at_x + 4) % 4 * 4 + spot_y
    source = jnp.where(block < 10, from_own, 160 + (block - 10) * 4 + spot_y)
    lane = lax.broadcasted_iota(jnp.int32, (ROWS, REACH), 1)
    for m in range(27):
        chosen = jnp.where(lane == source[:, m : m + 1], 1.0, 0.0).astype(BF16)
        sel[m // 9, m % 3, m // 3 % 3 * ROWS : (m // 3 % 3 + 1) * ROWS] = chosen

    def finish_halo(copies, received, ext):
        for copy in copies:
            copy.wait_recv()
        planes = [received[side, q].astype(F32) for side in range(2) for q in range(2)]
        for k in range(4):
            ext[10, k] = jnp.concatenate([plane[4 * k : 4 * k + 4] for plane in planes], axis=0).astype(BF16)

    def build(ext, dx):
        for k in range(4):
            parts = [(k + 1, 1)] + ([(5, 2)] if k == 0 else [(0, 0)] if k == 3 else [])
            left = jnp.concatenate([sel[dx, bz] for _, bz in parts], axis=0)
            rows = dot(left, ext[:, k].reshape(REACH, 2 * C)).astype(BF16)
            for n, (spot, _) in enumerate(parts):
                for dy in range(3):
                    at = (3 * n + dy) * ROWS
                    win[dx * 3 + dy, spot] = rows[at : at + ROWS]

    def view(g, dz, low):
        return win[g, dz : dz + 4, :, low : low + C].reshape(640, C)

    def views(gs, low):
        return jnp.concatenate([view(g, dz, low) for g in gs for dz in range(3)], axis=1)

    def forward(gs, w):
        right = jnp.concatenate([w[g].reshape(3 * C, C) for g in gs], axis=0)
        acc_a[...] += dot(views(gs, 0), right)

    def backward(gs, w):
        right = jnp.concatenate([w[8 - g, 2 - dz] for g in gs for dz in range(3)], axis=1)
        acc_b[...] += dot(views(gs, C), right, NT)

    def each(start, end, step):
        def one(n, carry):
            step(n)
            return carry

        lax.fori_loop(start, end, one, 0)

    def sides(step):
        each(0, 3, lambda n: step((n, n + 6)))

    acc_a[...] = jnp.zeros_like(acc_a)
    acc_b[...] = jnp.zeros_like(acc_b)
    for k in range(4):
        t_ext[10, k] = jnp.zeros((16, 2 * C), BF16)
    build(t_ext, 1)
    loads[2].wait()
    forward((3, 4, 5), w1)
    loads[3].wait()
    backward((3, 4, 5), w2)
    finish_halo(first, hrecv, t_ext)
    each(0, 2, lambda n: build(t_ext, 2 * n))
    sides(lambda gs: forward(gs, w1))

    hidden = jnp.maximum(acc_a[...], 0.0)
    hid_t[...] = hidden.T.astype(BF16)
    hidden = hidden.astype(BF16)
    for k in range(4):
        rows = hidden[k * ROWS : (k + 1) * ROWS].reshape(10, 16, C)
        t_own2[:, k, :, 0:C] = rows
        t_ext[0:10, k, :, 0:C] = rows

    def three(g):
        return pl.ds(pl.multiple_of(g * 768, 768), 768)

    def to_peer(g):
        return remote(mine.at[1, three(g)], precv.at[three(g)], ps.at[g], pr.at[g], peer)

    def grad_two_at(g):
        value = dot(hid_t[...], jnp.concatenate([view(8 - g, 2 - dz, C) for dz in range(3)], axis=1)).astype(BF16)
        for dz in range(3):
            mine[1 - core, pl.ds(g * 768 + dz * C, C)] = value[:, dz * C : dz * C + C]

    def grad_one_at(g):
        mine[core, three(g)] = dot(gh_t[...], views((g,), 0)).astype(BF16).T

    def join(g):
        to_peer(g).wait_recv()
        for n in range(3):
            at = pl.ds(g * 768 + n * C, C)
            xy[at] = (xy[at].astype(F32) + precv[at].astype(F32)).astype(BF16)

    xy = mine.at[0]

    def rows_at(start, size):
        return pl.ds(pl.multiple_of(start, 16), size)

    def slab_rows(zl, owner_x):
        return rows_at(432 * (zl * 4 + owner_x), 384)

    def part_rows(zl, s, owner_y):
        return rows_at(432 * (zl * 4 + s) + 96 * owner_y, 96)

    LOW, HIGH = slice(0, 128), slice(128, 256)
    next_x, last_x, far_x = (x + 1) % 4, (x + 3) % 4, (x + 2) % 4
    next_y, last_y, far_y = (y + 1) % 4, (y + 3) % 4, (y + 2) % 4

    def first_copies(h):
        copies = {}
        for phase, (buf_a, buf_b) in enumerate(((relay_a, relay_b), (direct_a, direct_b))):
            for way in range(2):
                to_x, to_y = (x_peers[0], y_peers[0]) if way == 0 else (x_peers[2], y_peers[2])
                if phase == 0:
                    owner_x, owner_y, lanes = far_x, far_y, LOW if way == 0 else HIGH
                else:
                    owner_x, owner_y = (next_x, next_y) if way == 0 else (last_x, last_y)
                    lanes = HIGH if way == 0 else LOW
                copies[phase, way] = [
                    remote(
                        xy.at[slab_rows(h, owner_x), lanes], buf_a.at[h, way],
                        as_.at[h, phase, way], ar.at[h, phase, way], to_x,
                    )
                ] + [
                    remote(
                        xy.at[part_rows(3 - h, s, owner_y), lanes], buf_b.at[h, way, s],
                        bs.at[h, phase, way, s], br.at[h, phase, way, s], to_y,
                    )
                    for s in range(4)
                ]
        for way in range(2):
            to_x, to_y = (x_peers[0], y_peers[0]) if way == 0 else (x_peers[2], y_peers[2])
            copies[2, way] = [
                remote(stage_a.at[h, way], summed_a.at[h, way], as_.at[h, 2, way], ar.at[h, 2, way], to_x),
                remote(stage_b.at[h, way], summed_b.at[h, way], bs.at[h, 2, way, 0], br.at[h, 2, way, 0], to_y),
            ]
        return copies

    copies_of = [first_copies(0), first_copies(1)]

    def start_slab(s):
        h = min(s // 4, 3 - s // 4)
        for way in range(2):
            if s < 8:
                owner = next_x if way == 0 else last_x

                @pl.when(far_x == s % 4)
                def _():
                    copies_of[h][0, way][0].start()

                @pl.when(owner == s % 4)
                def _():
                    copies_of[h][1, way][0].start()

            else:
                for phase in range(2):
                    copies_of[h][phase, way][1 + s % 4].start()

    def total(*parts):
        value = parts[0].astype(F32)
        for part in parts[1:]:
            value = value + part.astype(F32)
        return value

    def pass_on(h):
        for way in range(2):
            for copy in copies_of[h][0, way]:
                copy.wait_recv()
        for way, lanes, owner_x, owner_y in ((0, LOW, next_x, next_y), (1, HIGH, last_x, last_y)):
            stage_a[h, way] = total(xy[slab_rows(h, owner_x), lanes], relay_a[h, way]).astype(BF16)
            for s in range(4):
                own = xy[part_rows(3 - h, s, owner_y), lanes]
                stage_b[h, way, s] = total(own, relay_b[h, way, s]).astype(BF16)
            for copy in copies_of[h][2, way]:
                copy.start()

    second_copies = []
    for h in range(2):
        to_y = [
            remote(
                sum_a.at[h, rows_at(96 * ((y + d) % 4), 96)], recv_a2.at[h, d - 1], a2s.at[h, d - 1], a2r.at[h, d - 1],
                y_peers[d - 1],
            )
            for d in (2, 1, 3)
        ]
        to_x = [
            remote(sum_b.at[h, (x + d) % 4], recv_b2.at[h, d - 1], b2s.at[h, d - 1], b2r.at[h, d - 1], x_peers[d - 1])
            for d in (2, 1, 3)
        ]
        second_copies.append((to_y, to_x))

    def end_first(h):
        for phase in (1, 2):
            for way in range(2):
                for copy in copies_of[h][phase, way]:
                    copy.wait_recv()
        for lanes, a, b, a_buf, b_buf in (
            (LOW, summed_a, direct_a, 0, 1),
            (HIGH, direct_a, summed_a, 0, 1),
        ):
            value = total(xy[slab_rows(h, x), lanes], a[h, a_buf], b[h, b_buf])
            sum_a[h, :, lanes] = value.astype(BF16)
        for copy in second_copies[h][0]:
            copy.start()
        for s in range(4):
            for lanes, a, b in ((LOW, summed_b, direct_b), (HIGH, direct_b, summed_b)):
                value = total(xy[part_rows(3 - h, s, y), lanes], a[h, 0, s], b[h, 1, s])
                sum_b[h, s, :, lanes] = value.astype(BF16)
        for copy in second_copies[h][1]:
            copy.start()

    stage_z = []
    for d in (4, 3, 5, 2, 6, 1, 7):
        to = (z + d) % 8
        copy = remote(zsend.at[to // 4, to % 4], zrecv.at[d - 1], zs.at[d - 1], zr.at[d - 1], z_peers[d - 1])
        stage_z.append((to, copy))

    def end_second(h):
        for copy in second_copies[h][0]:
            copy.wait_recv()
        full = total(sum_a[h, rows_at(96 * y, 96)], *[recv_a2[h, d] for d in range(3)]).astype(BF16)
        zsend[0, h], zsend[1, h] = full[:, LOW], full[:, HIGH]
        for copy in second_copies[h][1]:
            copy.wait_recv()
        full = total(sum_b[h, x], *[recv_b2[h, d] for d in range(3)]).astype(BF16)
        zsend[0, 3 - h], zsend[1, 3 - h] = full[:, LOW], full[:, HIGH]
        for to, copy in stage_z:
            outer = (to % 4 == 0) | (to % 4 == 3)

            @pl.when(outer if h == 0 else jnp.logical_not(outer))
            def _():
                copy.start()

    tails_z = []
    for d in (4, 3, 5, 2, 6, 1, 7):
        to = (z + d) % 8
        copy = remote(tail_z.at[to // 4, to % 4], tail_z_in.at[d - 1], tzs.at[d - 1], tzr.at[d - 1], z_peers[d - 1])
        tails_z.append((to, copy))
    tails_x = [
        remote(tail_x.at[(x + d) % 4], tail_x_in.at[d - 1], txs.at[d - 1], txr.at[d - 1], x_peers[d - 1]) for d in (2, 1, 3)
    ]
    tails_y = [
        remote(tail_y.at[(y + d) % 4], tail_y_in.at[d - 1], tys.at[d - 1], tyr.at[d - 1], y_peers[d - 1]) for d in (2, 1, 3)
    ]

    def pack_tail(s):
        rows = xy[432 * s + 384 : 432 * s + 432]
        tail_z[0, s // 4, s % 4], tail_z[1, s // 4, s % 4] = rows[:, LOW], rows[:, HIGH]

    def start_tails(h):
        for to, copy in tails_z:
            outer = (to % 4 == 0) | (to % 4 == 3)

            @pl.when(outer if h == 0 else jnp.logical_not(outer))
            def _():
                copy.start()

    def tail_after_z(_):
        for _, copy in tails_z:
            copy.wait_recv()
        for s in range(4):
            tail_x[s] = total(tail_z[z_hi, z_lo, s], *[tail_z_in[d, s] for d in range(7)]).astype(BF16)
        for copy in tails_x:
            copy.start()

    def tail_after_x(_):
        for copy in tails_x:
            copy.wait_recv()
        value = total(tail_x[x], *[tail_x_in[d] for d in range(3)]).astype(BF16)
        for part in range(3):
            tail_y[part] = value[16 * part : 16 * part + 16]
        tail_y[3] = jnp.zeros((16, 128), BF16)
        for copy in tails_y:
            copy.start()

    def on(which, *steps):
        @pl.when(core == which)
        def _():
            for step, arg in steps:
                step(arg)

    READY = ((0, 15), (1, 14, 2, 13), (3, 12, 4, 11), (5, 10, 6, 9), (7, 8))

    def gradients(at, keeper, between):
        def finish(n):
            for g in (n, 8 - n) if n < 4 else (4,):
                join(g)
            for s in READY[n]:
                start_slab(s)
                pack_tail(s)
            if n in (2, 4):
                start_tails(0 if n == 2 else 1)

        def send(g):
            to_peer(g).start()

        for n in range(5):
            gs = (n, 8 - n) if n < 4 else (4,)
            for g in gs:
                at(g)
            on(1 - keeper, *[(send, g) for g in gs])
            if n > 0:
                on(keeper, (finish, n - 1))
            between(n)
        on(keeper, (finish, 4))

    gradients(grad_two_at, 1, lambda n: None)

    sides(lambda gs: backward(gs, w2))
    grad_hidden = jnp.where(hidden > 0, acc_b[...].astype(BF16), jnp.zeros((), BF16))
    gh_t[...] = grad_hidden.T
    for k in range(4):
        rows = grad_hidden[k * ROWS : (k + 1) * ROWS].reshape(10, 16, C)
        t_own2[:, k, :, C:] = rows
        t_ext[0:10, k, :, C:] = rows
    pack_edges(t_own2, pack2)
    second = halo(pack2, hrecv2, 1)
    for copy in second:
        copy.start()
    gradients(grad_one_at, 0, lambda n: on(1, (pass_on, 0)) if n == 1 else None)
    on(1, (pass_on, 1))

    finish_halo(second, hrecv2, t_ext)
    each(0, 3, lambda dx: build(t_ext, dx))
    on(0, (pass_on, 0), (pass_on, 1))
    on(1, (end_first, 0))
    acc_a[...] = jnp.zeros_like(acc_a)
    acc_b[...] = jnp.zeros_like(acc_b)
    each(0, 3, lambda n: forward((3 * n, 3 * n + 1, 3 * n + 2), w2))
    on(0, (end_first, 0), (tail_after_z, 0), (end_first, 1))
    on(1, (end_first, 1), (end_second, 0), (tail_after_z, 0))
    each(0, 3, lambda n: backward((3 * n, 3 * n + 1, 3 * n + 2), w1))
    on(1, (end_second, 1), (tail_after_x, 0))
    on(0, (end_second, 0), (tail_after_x, 0), (end_second, 1))
    for k in range(4):
        rows = slice(k * ROWS, (k + 1) * ROWS)
        for n, acc in enumerate((acc_a, acc_b)):
            for half in range(2):
                nat[2 * n + half, pl.ds(k, ROWS, stride=4), :] = acc[rows, half * 128 : half * 128 + 128]
    masked = feat[...].reshape(640, C).astype(F32) * present
    out_v[...] = (jnp.concatenate([nat[0], nat[1]], axis=1) + masked).astype(BF16).reshape(10, 64, C)
    upstream = cot[...].reshape(640, C).astype(F32)
    back = jnp.concatenate([nat[2], nat[3]], axis=1)
    gf_v[...] = ((upstream + back) * present).astype(BF16).reshape(10, 64, C)
    stores = [pltpu.make_async_copy(out_v, out_hbm, osem.at[0]), pltpu.make_async_copy(gf_v, gf_hbm, osem.at[1])]
    for store in stores:
        store.start()

    for copy in tails_y:
        copy.wait_recv()
    tail = total(tail_y[y], *[tail_y_in[d] for d in range(3)]) * factor
    for _, copy in stage_z:
        copy.wait_recv()
    whole = total(zsend[z_hi, z_lo], *[zrecv[d] for d in range(7)]) * factor
    padded = jnp.concatenate([whole, tail, jnp.zeros((16, 128), F32)], axis=0)
    fin_t[...] = padded.T.reshape(8, 16, 128)

    stage_f = []
    for d in range(1, 8):
        to = (yc + d) % 8
        stage_f.append(remote(fin_t.at[to], fin_recv.at[d - 1], fs.at[d - 1], fr.at[d - 1], f_peers[d - 1]))
    for copy in stage_f:
        copy.start()
    fin_ref[yc] = fin_t[yc]
    sent = list(first) + list(second) + [copy for _, copy in stage_z + tails_z] + tails_x + tails_y
    for h in range(2):
        sent += [copy for group in copies_of[h].values() for copy in group]
        sent += second_copies[h][0] + second_copies[h][1]
    for copy in sent:
        copy.wait_send()
    for store in stores:
        store.wait()

    each(0, 9, lambda g: to_peer(g).wait_send())
    for d in range(1, 8):
        stage_f[d - 1].wait_recv()
    for d in range(1, 8):
        fin_ref[(yc + 8 - d) % 8] = fin_recv[d - 1]
    for copy in stage_f:
        copy.wait_send()


def closing(out_in, gf_in, fin, out_ref, gf_ref, g1_ref, g2_ref):
    out_ref[...] = out_in[...]
    gf_ref[...] = gf_in[...]
    for src_core, target in ((0, g1_ref), (1, g2_ref)):
        for src_y in range(4):
            part = fin[src_y * 2 + src_core]
            target[:, 96 * src_y : 96 * src_y + 96] = part[:, 0:96]
            if src_y < 3:
                target[:, 384 + 16 * src_y : 400 + 16 * src_y] = part[:, 96:112]


def per_device(features, cotangent, neighbour_table, send_lists, block_counts, weight_one, weight_two):
    factor = 1.0 / math.sqrt(lax.axis_size("dp") * lax.axis_size("slab") * 10 * 64)
    smem = pl.BlockSpec(memory_space=pltpu.SMEM)
    vmem = pl.BlockSpec(memory_space=pltpu.VMEM)
    hbm = pl.BlockSpec(memory_space=pl.ANY)
    dma = pltpu.SemaphoreType.DMA
    big = jax.ShapeDtypeStruct((10, 64, C), BF16)
    out, gf, fin = pl.pallas_call(
        lambda *refs: kernel(factor, *refs),
        out_shape=(big, big, jax.ShapeDtypeStruct((8, 16, 128), F32)),
        in_specs=[smem, smem, vmem, hbm, hbm, hbm, hbm],
        out_specs=(hbm, hbm, vmem),
        scratch_shapes=[
            pltpu.VMEM((9, 3, C, C), BF16),
            pltpu.VMEM((9, 3, C, C), BF16),
            pltpu.VMEM((10, 64, C), BF16),
            pltpu.VMEM((10, 64, C), BF16),
            pltpu.VMEM((10, 64, C), BF16),
            pltpu.VMEM((10, 64, C), BF16),
            pltpu.VMEM((4, 640, 128), F32),
            pltpu.VMEM((10, 4, 16, 2 * C), BF16),
            pltpu.VMEM((11, 4, 16, 2 * C), BF16),
            pltpu.VMEM((2, 2, 16, 2 * C), BF16),
            pltpu.VMEM((2, 2, 16, 2 * C), BF16),
            pltpu.VMEM((10, 4, 16, 2 * C), BF16),
            pltpu.VMEM((2, 2, 16, 2 * C), BF16),
            pltpu.VMEM((2, 2, 16, 2 * C), BF16),
            pltpu.VMEM((3, 3, 3 * ROWS, REACH), BF16),
            pltpu.VMEM((9, 6, ROWS, 2 * C), BF16),
            pltpu.VMEM((640, C), F32),
            pltpu.VMEM((640, C), F32),
            pltpu.VMEM((C, 640), BF16),
            pltpu.VMEM((C, 640), BF16),
            pltpu.VMEM((2, 6912, C), BF16),
            pltpu.VMEM((6912, C), BF16),
            pltpu.VMEM((2, 2, 384, 128), BF16),
            pltpu.VMEM((2, 2, 384, 128), BF16),
            pltpu.VMEM((2, 2, 384, 128), BF16),
            pltpu.VMEM((2, 2, 384, 128), BF16),
            pltpu.VMEM((2, 2, 4, 96, 128), BF16),
            pltpu.VMEM((2, 2, 4, 96, 128), BF16),
            pltpu.VMEM((2, 2, 4, 96, 128), BF16),
            pltpu.VMEM((2, 2, 4, 96, 128), BF16),
            pltpu.VMEM((2, 384, C), BF16),
            pltpu.VMEM((2, 4, 96, C), BF16),
            pltpu.VMEM((2, 3, 96, C), BF16),
            pltpu.VMEM((2, 3, 96, C), BF16),
            pltpu.VMEM((2, 4, 96, 128), BF16),
            pltpu.VMEM((7, 96, 128), BF16),
            pltpu.VMEM((2, 4, 4, 48, 128), BF16),
            pltpu.VMEM((7, 4, 48, 128), BF16),
            pltpu.VMEM((4, 48, 128), BF16),
            pltpu.VMEM((3, 48, 128), BF16),
            pltpu.VMEM((4, 16, 128), BF16),
            pltpu.VMEM((3, 16, 128), BF16),
            pltpu.VMEM((8, 16, 128), F32),
            pltpu.VMEM((7, 16, 128), F32),
            dma((4,)),
            dma((2,)),
            dma((2, 2)),
            dma((2, 2)),
            dma((9,)),
            dma((9,)),
            dma((2, 3, 2)),
            dma((2, 3, 2)),
            dma((2, 3, 2, 4)),
            dma((2, 3, 2, 4)),
            dma((2, 3)),
            dma((2, 3)),
            dma((2, 3)),
            dma((2, 3)),
            dma((7,)),
            dma((7,)),
            dma((7,)),
            dma((7,)),
            dma((7,)),
            dma((7,)),
            dma((3,)),
            dma((3,)),
            dma((3,)),
            dma((3,)),
        ],
        compiler_params=pltpu.CompilerParams(
            collective_id=0, has_side_effects=True, vmem_limit_bytes=60 * 1024 * 1024
        ),
        name="step",
    )(
        block_counts,
        send_lists[0, 0],
        jnp.transpose(neighbour_table, (1, 0, 2)),
        features[0],
        cotangent[0],
        weight_one.reshape(9, 3, C, C),
        weight_two.reshape(9, 3, C, C),
    )
    piece = jax.ShapeDtypeStruct((16, 432), F32)
    out, gf, g1, g2 = pl.pallas_call(
        closing,
        out_shape=(big, big, piece, piece),
        in_specs=[vmem, vmem, vmem],
        out_specs=(vmem, vmem, vmem, vmem),
        name="closing",
    )(out, gf, fin)
    return (out[None], gf[None], g1.T, g2.T)


def solution(mesh):
    in_specs = (
        P("dp", "slab", None, None),
        P("dp", "slab", None, None),
        P("dp", "slab", None),
        P("dp", "slab", None, None),
        P("dp", "slab"),
        P(),
        P(),
    )
    out_specs = (
        P("dp", "slab", None, None),
        P("dp", "slab", None, None),
        P("slab", "dp"),
        P("slab", "dp"),
    )
    return jax.shard_map(
        per_device, mesh=mesh, in_specs=in_specs, out_specs=out_specs, check_vma=False
    )
```

```python
import math

import jax
import jax.numpy as jnp
from jax import lax
from jax.experimental import pallas as pl
from jax.experimental.pallas import tpu as pltpu
from jax.sharding import PartitionSpec as P

F32 = jnp.float32
BF16 = jnp.bfloat16
MESH = pl.DeviceIdType.MESH
ROWS = 160
REACH = 176
C = 256
NT = (((1,), (1,)), ((), ()))
TN = (((0,), (0,)), ((), ()))


def dot(a, b, dims=(((1,), (0,)), ((), ()))):
    return lax.dot_general(a, b, dims, preferred_element_type=F32)


def kernel(
    factor,
    counts, lists, table_ref, feat_hbm, cot_hbm, w1_hbm, w2_hbm,
    out_hbm, gf_hbm, fin_ref,
    w1, w2, feat, cot, out_v, gf_v, nat, t_own, t_ext, pack, hrecv, t_own2, pack2, hrecv2, sel, win, acc_a, acc_b,
    hid_t, gh_t, mine, precv, relay_a, direct_a, summed_a, stage_a, relay_b, direct_b, summed_b, stage_b,
    sum_a, sum_b, recv_a2, recv_b2, zsend, zrecv,
    tail_z, tail_z_in, tail_x, tail_x_in, tail_y, tail_y_in, fin_t, fin_recv,
    lsem, osem, hs, hr, ps, pr, as_, ar, bs, br, a2s, a2r, b2s, b2r, zs, zr, fs, fr, tzs, tzr, txs, txr, tys, tyr,
):
    loads = [
        pltpu.make_async_copy(source, target, lsem.at[n])
        for n, (source, target) in enumerate(((feat_hbm, feat), (cot_hbm, cot), (w1_hbm, w1), (w2_hbm, w2)))
    ]
    for load in loads:
        load.start()

    dp = lax.axis_index("dp")
    slab = lax.axis_index("slab")
    core = dp % 2
    y = dp // 2 % 4
    z_hi = dp // 8
    x = slab % 4
    z_lo = slab // 4
    z = z_hi * 4 + z_lo

    def dev(x_=x, y_=y, z_=z, core_=core):
        return ((z_ // 4) * 8 + y_ * 2 + core_, (z_ % 4) * 4 + x_)

    after = (slab + 1) % 16
    before = (slab + 15) % 16
    peer = dev(core_=1 - core)
    x_peers = [dev(x_=(x + d) % 4) for d in range(1, 4)]
    y_peers = [dev(y_=(y + d) % 4) for d in range(1, 4)]
    z_peers = [dev(z_=(z + d) % 8) for d in range(1, 8)]
    yc = y * 2 + core
    f_peers = [dev(y_=(yc + d) % 8 // 2, core_=(yc + d) % 2) for d in range(1, 8)]

    barrier = pltpu.get_barrier_semaphore()
    everyone = [(dp, after), (dp, before)] + x_peers + z_peers + f_peers
    for d in everyone:
        pl.semaphore_signal(barrier, inc=1, device_id=d, device_id_type=MESH)

    def remote(src, dst, send, recv, to):
        return pltpu.make_async_remote_copy(
            src_ref=src, dst_ref=dst, send_sem=send, recv_sem=recv, device_id=to, device_id_type=MESH
        )

    row = lax.broadcasted_iota(jnp.int32, (640, 1), 0)
    present = jnp.where(row < counts[0, 0] * 64, 1.0, 0.0)
    loads[0].wait()
    loads[1].wait()
    for part, value in (
        (0, feat[...].reshape(640, C).astype(F32) * present),
        (2, cot[...].reshape(640, C).astype(F32)),
    ):
        nat[part], nat[part + 1] = value[:, 0:128], value[:, 128:]
    for k in range(4):
        part = jnp.concatenate([nat[n, pl.ds(k, ROWS, stride=4), :] for n in range(4)], axis=1)
        part = part.astype(BF16).reshape(10, 16, 2 * C)
        t_own[:, k] = part
        t_ext[0:10, k] = part

    def pack_edges(source, target):
        for side in range(2):
            inside = jnp.where(side == 0, slab > 0, slab < 15)
            for q in range(2):
                named = lists[side, q]
                keep = jnp.where(inside & (named < 10), 1.0, 0.0)
                block = source[jnp.minimum(named, 9)].astype(F32) * keep
                plane = [block[k, 12 * side : 12 * side + 4] for k in range(4)]
                target[side, q] = jnp.concatenate(plane, axis=0).astype(BF16)

    def halo(source, target, e):
        return (
            remote(source.at[1], target.at[0], hs.at[e, 0], hr.at[e, 0], (dp, after)),
            remote(source.at[0], target.at[1], hs.at[e, 1], hr.at[e, 1], (dp, before)),
        )

    pack_edges(t_own, pack)
    pl.semaphore_wait(barrier, len(everyone))
    first = halo(pack, hrecv, 0)
    for copy in first:
        copy.start()

    r = lax.broadcasted_iota(jnp.int32, (ROWS, 1), 0)
    spread = (r // 16 == lax.broadcasted_iota(jnp.int32, (ROWS, 10), 1)).astype(BF16)
    rows_of = dot(spread, table_ref[...].reshape(10, 27).astype(BF16)).astype(BF16)
    named = lax.broadcasted_iota(jnp.int32, (27, 27), 0)

    def step_of(shape):
        m = lax.broadcasted_iota(jnp.int32, shape, 1)
        return m // 9, m // 3 % 3, m % 3

    step_x, step_y, step_z = step_of((27, 27))
    low = (jnp.minimum(step_x, 1), jnp.minimum(step_y, 1))
    high = (jnp.maximum(step_x, 1), jnp.maximum(step_y, 1))

    def blocks(bx, by):
        return dot(rows_of, (named == 9 * bx + 3 * by + step_z).astype(BF16))

    step_x, step_y, _ = step_of((ROWS, 27))
    at_x, at_y = r // 4 % 4 + step_x - 1, r % 4 + step_y - 1
    first_x = at_x < jnp.where(step_x == 0, 0, 4)
    first_y = at_y < jnp.where(step_y == 0, 0, 4)
    block = jnp.where(
        first_x,
        jnp.where(first_y, blocks(low[0], low[1]), blocks(low[0], high[1])),
        jnp.where(first_y, blocks(high[0], low[1]), blocks(high[0], high[1])),
    ).astype(jnp.int32)
    spot_y = (at_y + 4) % 4
    from_own = block * 16 + (at_x + 4) % 4 * 4 + spot_y
    source = jnp.where(block < 10, from_own, 160 + (block - 10) * 4 + spot_y)
    lane = lax.broadcasted_iota(jnp.int32, (ROWS, REACH), 1)
    for m in range(27):
        chosen = jnp.where(lane == source[:, m : m + 1], 1.0, 0.0).astype(BF16)
        sel[m // 9, m % 3, m // 3 % 3 * ROWS : (m // 3 % 3 + 1) * ROWS] = chosen

    def finish_halo(copies, received, ext):
        for copy in copies:
            copy.wait_recv()
        planes = [received[side, q].astype(F32) for side in range(2) for q in range(2)]
        for k in range(4):
            ext[10, k] = jnp.concatenate([plane[4 * k : 4 * k + 4] for plane in planes], axis=0).astype(BF16)

    def build(ext, dx):
        for k in range(4):
            parts = [(k + 1, 1)] + ([(5, 2)] if k == 0 else [(0, 0)] if k == 3 else [])
            left = jnp.concatenate([sel[dx, bz] for _, bz in parts], axis=0)
            rows = dot(left, ext[:, k].reshape(REACH, 2 * C)).astype(BF16)
            for n, (spot, _) in enumerate(parts):
                for dy in range(3):
                    at = (3 * n + dy) * ROWS
                    win[dx * 3 + dy, spot] = rows[at : at + ROWS]

    def view(g, dz, low):
        return win[g, dz : dz + 4, :, low : low + C].reshape(640, C)

    def views(gs, low):
        return jnp.concatenate([view(g, dz, low) for g in gs for dz in range(3)], axis=1)

    def forward(gs, w):
        right = jnp.concatenate([w[g].reshape(3 * C, C) for g in gs], axis=0)
        acc_a[...] += dot(views(gs, 0), right)

    def backward(gs, w):
        right = jnp.concatenate([w[8 - g, 2 - dz] for g in gs for dz in range(3)], axis=1)
        acc_b[...] += dot(views(gs, C), right, NT)

    def each(start, end, step):
        def one(n, carry):
            step(n)
            return carry

        lax.fori_loop(start, end, one, 0)

    def sides(step):
        each(0, 3, lambda n: step((n, n + 6)))

    acc_a[...] = jnp.zeros_like(acc_a)
    acc_b[...] = jnp.zeros_like(acc_b)
    for k in range(4):
        t_ext[10, k] = jnp.zeros((16, 2 * C), BF16)
    build(t_ext, 1)
    loads[2].wait()
    forward((3, 4, 5), w1)
    loads[3].wait()
    backward((3, 4, 5), w2)
    finish_halo(first, hrecv, t_ext)
    each(0, 2, lambda n: build(t_ext, 2 * n))
    sides(lambda gs: forward(gs, w1))

    hidden = jnp.maximum(acc_a[...], 0.0)
    hid_t[...] = hidden.T.astype(BF16)
    hidden = hidden.astype(BF16)
    for k in range(4):
        rows = hidden[k * ROWS : (k + 1) * ROWS].reshape(10, 16, C)
        t_own2[:, k, :, 0:C] = rows
        t_ext[0:10, k, :, 0:C] = rows

    def three(g):
        return pl.ds(pl.multiple_of(g * 768, 768), 768)

    def to_peer(g):
        return remote(mine.at[1, three(g)], precv.at[three(g)], ps.at[g], pr.at[g], peer)

    def grad_two_at(g):
        value = dot(hid_t[...], jnp.concatenate([view(8 - g, 2 - dz, C) for dz in range(3)], axis=1)).astype(BF16)
        for dz in range(3):
            mine[1 - core, pl.ds(g * 768 + dz * C, C)] = value[:, dz * C : dz * C + C]

    def grad_one_at(g):
        mine[core, three(g)] = dot(gh_t[...], views((g,), 0)).astype(BF16).T

    def join(g):
        to_peer(g).wait_recv()
        for n in range(3):
            at = pl.ds(g * 768 + n * C, C)
            xy[at] = (xy[at].astype(F32) + precv[at].astype(F32)).astype(BF16)

    xy = mine.at[0]

    def rows_at(start, size):
        return pl.ds(pl.multiple_of(start, 16), size)

    def slab_rows(zl, owner_x):
        return rows_at(432 * (zl * 4 + owner_x), 384)

    def part_rows(zl, s, owner_y):
        return rows_at(432 * (zl * 4 + s) + 96 * owner_y, 96)

    LOW, HIGH = slice(0, 128), slice(128, 256)
    next_x, last_x, far_x = (x + 1) % 4, (x + 3) % 4, (x + 2) % 4
    next_y, last_y, far_y = (y + 1) % 4, (y + 3) % 4, (y + 2) % 4

    def first_copies(h):
        copies = {}
        for phase, (buf_a, buf_b) in enumerate(((relay_a, relay_b), (direct_a, direct_b))):
            for way in range(2):
                to_x, to_y = (x_peers[0], y_peers[0]) if way == 0 else (x_peers[2], y_peers[2])
                if phase == 0:
                    owner_x, owner_y, lanes = far_x, far_y, LOW if way == 0 else HIGH
                else:
                    owner_x, owner_y = (next_x, next_y) if way == 0 else (last_x, last_y)
                    lanes = HIGH if way == 0 else LOW
                copies[phase, way] = [
                    remote(
                        xy.at[slab_rows(h, owner_x), lanes], buf_a.at[h, way],
                        as_.at[h, phase, way], ar.at[h, phase, way], to_x,
                    )
                ] + [
                    remote(
                        xy.at[part_rows(3 - h, s, owner_y), lanes], buf_b.at[h, way, s],
                        bs.at[h, phase, way, s], br.at[h, phase, way, s], to_y,
                    )
                    for s in range(4)
                ]
        for way in range(2):
            to_x, to_y = (x_peers[0], y_peers[0]) if way == 0 else (x_peers[2], y_peers[2])
            copies[2, way] = [
                remote(stage_a.at[h, way], summed_a.at[h, way], as_.at[h, 2, way], ar.at[h, 2, way], to_x),
                remote(stage_b.at[h, way], summed_b.at[h, way], bs.at[h, 2, way, 0], br.at[h, 2, way, 0], to_y),
            ]
        return copies

    copies_of = [first_copies(0), first_copies(1)]

    def start_slab(s):
        h = min(s // 4, 3 - s // 4)
        for way in range(2):
            if s < 8:
                owner = next_x if way == 0 else last_x

                @pl.when(far_x == s % 4)
                def _():
                    copies_of[h][0, way][0].start()

                @pl.when(owner == s % 4)
                def _():
                    copies_of[h][1, way][0].start()

            else:
                for phase in range(2):
                    copies_of[h][phase, way][1 + s % 4].start()

    def total(*parts):
        value = parts[0].astype(F32)
        for part in parts[1:]:
            value = value + part.astype(F32)
        return value

    def pass_on(h):
        for way in range(2):
            for copy in copies_of[h][0, way]:
                copy.wait_recv()
        for way, lanes, owner_x, owner_y in ((0, LOW, next_x, next_y), (1, HIGH, last_x, last_y)):
            stage_a[h, way] = total(xy[slab_rows(h, owner_x), lanes], relay_a[h, way]).astype(BF16)
            for s in range(4):
                own = xy[part_rows(3 - h, s, owner_y), lanes]
                stage_b[h, way, s] = total(own, relay_b[h, way, s]).astype(BF16)
            for copy in copies_of[h][2, way]:
                copy.start()

    second_copies = []
    for h in range(2):
        to_y = [
            remote(
                sum_a.at[h, rows_at(96 * ((y + d) % 4), 96)], recv_a2.at[h, d - 1], a2s.at[h, d - 1], a2r.at[h, d - 1],
                y_peers[d - 1],
            )
            for d in (2, 1, 3)
        ]
        to_x = [
            remote(sum_b.at[h, (x + d) % 4], recv_b2.at[h, d - 1], b2s.at[h, d - 1], b2r.at[h, d - 1], x_peers[d - 1])
            for d in (2, 1, 3)
        ]
        second_copies.append((to_y, to_x))

    def end_first(h):
        for phase in (1, 2):
            for way in range(2):
                for copy in copies_of[h][phase, way]:
                    copy.wait_recv()
        for lanes, a, b, a_buf, b_buf in (
            (LOW, summed_a, direct_a, 0, 1),
            (HIGH, direct_a, summed_a, 0, 1),
        ):
            value = total(xy[slab_rows(h, x), lanes], a[h, a_buf], b[h, b_buf])
            sum_a[h, :, lanes] = value.astype(BF16)
        for copy in second_copies[h][0]:
            copy.start()
        for s in range(4):
            for lanes, a, b in ((LOW, summed_b, direct_b), (HIGH, direct_b, summed_b)):
                value = total(xy[part_rows(3 - h, s, y), lanes], a[h, 0, s], b[h, 1, s])
                sum_b[h, s, :, lanes] = value.astype(BF16)
        for copy in second_copies[h][1]:
            copy.start()

    stage_z = []
    for d in (4, 3, 5, 2, 6, 1, 7):
        to = (z + d) % 8
        copy = remote(zsend.at[to // 4, to % 4], zrecv.at[d - 1], zs.at[d - 1], zr.at[d - 1], z_peers[d - 1])
        stage_z.append((to, copy))

    def end_second(h):
        for copy in second_copies[h][0]:
            copy.wait_recv()
        full = total(sum_a[h, rows_at(96 * y, 96)], *[recv_a2[h, d] for d in range(3)]).astype(BF16)
        zsend[0, h], zsend[1, h] = full[:, LOW], full[:, HIGH]
        for copy in second_copies[h][1]:
            copy.wait_recv()
        full = total(sum_b[h, x], *[recv_b2[h, d] for d in range(3)]).astype(BF16)
        zsend[0, 3 - h], zsend[1, 3 - h] = full[:, LOW], full[:, HIGH]
        for to, copy in stage_z:
            outer = (to % 4 == 0) | (to % 4 == 3)

            @pl.when(outer if h == 0 else jnp.logical_not(outer))
            def _():
                copy.start()

    tails_z = []
    for d in (4, 3, 5, 2, 6, 1, 7):
        to = (z + d) % 8
        copy = remote(tail_z.at[to // 4, to % 4], tail_z_in.at[d - 1], tzs.at[d - 1], tzr.at[d - 1], z_peers[d - 1])
        tails_z.append((to, copy))
    tails_x = [
        remote(tail_x.at[(x + d) % 4], tail_x_in.at[d - 1], txs.at[d - 1], txr.at[d - 1], x_peers[d - 1]) for d in (2, 1, 3)
    ]
    tails_y = [
        remote(tail_y.at[(y + d) % 4], tail_y_in.at[d - 1], tys.at[d - 1], tyr.at[d - 1], y_peers[d - 1]) for d in (2, 1, 3)
    ]

    def pack_tail(s):
        rows = xy[432 * s + 384 : 432 * s + 432]
        tail_z[0, s // 4, s % 4], tail_z[1, s // 4, s % 4] = rows[:, LOW], rows[:, HIGH]

    def start_tails(h):
        for to, copy in tails_z:
            outer = (to % 4 == 0) | (to % 4 == 3)

            @pl.when(outer if h == 0 else jnp.logical_not(outer))
            def _():
                copy.start()

    def tail_after_z(_):
        for _, copy in tails_z:
            copy.wait_recv()
        for s in range(4):
            tail_x[s] = total(tail_z[z_hi, z_lo, s], *[tail_z_in[d, s] for d in range(7)]).astype(BF16)
        for copy in tails_x:
            copy.start()

    def tail_after_x(_):
        for copy in tails_x:
            copy.wait_recv()
        value = total(tail_x[x], *[tail_x_in[d] for d in range(3)]).astype(BF16)
        for part in range(3):
            tail_y[part] = value[16 * part : 16 * part + 16]
        tail_y[3] = jnp.zeros((16, 128), BF16)
        for copy in tails_y:
            copy.start()

    def on(which, *steps):
        @pl.when(core == which)
        def _():
            for step, arg in steps:
                step(arg)

    READY = ((0, 15), (1, 14, 2, 13), (3, 12, 4, 11), (5, 10, 6, 9), (7, 8))

    def gradients(at, keeper, between):
        def finish(n):
            for g in (n, 8 - n) if n < 4 else (4,):
                join(g)
            for s in READY[n]:
                start_slab(s)
                pack_tail(s)
            if n in (2, 4):
                start_tails(0 if n == 2 else 1)

        def send(g):
            to_peer(g).start()

        for n in range(5):
            gs = (n, 8 - n) if n < 4 else (4,)
            for g in gs:
                at(g)
            on(1 - keeper, *[(send, g) for g in gs])
            if n > 0:
                on(keeper, (finish, n - 1))
            between(n)
        on(keeper, (finish, 4))

    gradients(grad_two_at, 1, lambda n: None)

    sides(lambda gs: backward(gs, w2))
    grad_hidden = jnp.where(hidden > 0, acc_b[...].astype(BF16), jnp.zeros((), BF16))
    gh_t[...] = grad_hidden.T
    for k in range(4):
        rows = grad_hidden[k * ROWS : (k + 1) * ROWS].reshape(10, 16, C)
        t_own2[:, k, :, C:] = rows
        t_ext[0:10, k, :, C:] = rows
    pack_edges(t_own2, pack2)
    second = halo(pack2, hrecv2, 1)
    for copy in second:
        copy.start()
    on(1, (pass_on, 0))

    gradients(grad_one_at, 0, lambda n: on(1, (pass_on, 1)) if n == 2 else None)

    finish_halo(second, hrecv2, t_ext)
    each(0, 3, lambda dx: build(t_ext, dx))
    on(0, (pass_on, 0), (pass_on, 1))
    on(1, (end_first, 0))
    acc_a[...] = jnp.zeros_like(acc_a)
    acc_b[...] = jnp.zeros_like(acc_b)
    each(0, 3, lambda n: forward((3 * n, 3 * n + 1, 3 * n + 2), w2))
    on(0, (end_first, 0), (tail_after_z, 0), (end_first, 1))
    on(1, (end_first, 1), (end_second, 0), (tail_after_z, 0))
    each(0, 3, lambda n: backward((3 * n, 3 * n + 1, 3 * n + 2), w1))
    on(1, (end_second, 1), (tail_after_x, 0))
    on(0, (end_second, 0), (tail_after_x, 0), (end_second, 1))
    for k in range(4):
        rows = slice(k * ROWS, (k + 1) * ROWS)
        for n, acc in enumerate((acc_a, acc_b)):
            for half in range(2):
                nat[2 * n + half, pl.ds(k, ROWS, stride=4), :] = acc[rows, half * 128 : half * 128 + 128]
    masked = feat[...].reshape(640, C).astype(F32) * present
    out_v[...] = (jnp.concatenate([nat[0], nat[1]], axis=1) + masked).astype(BF16).reshape(10, 64, C)
    upstream = cot[...].reshape(640, C).astype(F32)
    back = jnp.concatenate([nat[2], nat[3]], axis=1)
    gf_v[...] = ((upstream + back) * present).astype(BF16).reshape(10, 64, C)
    stores = [pltpu.make_async_copy(out_v, out_hbm, osem.at[0]), pltpu.make_async_copy(gf_v, gf_hbm, osem.at[1])]
    for store in stores:
        store.start()

    for copy in tails_y:
        copy.wait_recv()
    tail = total(tail_y[y], *[tail_y_in[d] for d in range(3)]) * factor
    for _, copy in stage_z:
        copy.wait_recv()
    whole = total(zsend[z_hi, z_lo], *[zrecv[d] for d in range(7)]) * factor
    padded = jnp.concatenate([whole, tail, jnp.zeros((16, 128), F32)], axis=0)
    fin_t[...] = padded.T.reshape(8, 16, 128)

    stage_f = []
    for d in range(1, 8):
        to = (yc + d) % 8
        stage_f.append(remote(fin_t.at[to], fin_recv.at[d - 1], fs.at[d - 1], fr.at[d - 1], f_peers[d - 1]))
    for copy in stage_f:
        copy.start()
    fin_ref[yc] = fin_t[yc]
    sent = list(first) + list(second) + [copy for _, copy in stage_z + tails_z] + tails_x + tails_y
    for h in range(2):
        sent += [copy for group in copies_of[h].values() for copy in group]
        sent += second_copies[h][0] + second_copies[h][1]
    for copy in sent:
        copy.wait_send()
    for store in stores:
        store.wait()

    each(0, 9, lambda g: to_peer(g).wait_send())
    for d in range(1, 8):
        stage_f[d - 1].wait_recv()
    for d in range(1, 8):
        fin_ref[(yc + 8 - d) % 8] = fin_recv[d - 1]
    for copy in stage_f:
        copy.wait_send()


def closing(out_in, gf_in, fin, out_ref, gf_ref, g1_ref, g2_ref):
    out_ref[...] = out_in[...]
    gf_ref[...] = gf_in[...]
    for src_core, target in ((0, g1_ref), (1, g2_ref)):
        for src_y in range(4):
            part = fin[src_y * 2 + src_core]
            target[:, 96 * src_y : 96 * src_y + 96] = part[:, 0:96]
            if src_y < 3:
                target[:, 384 + 16 * src_y : 400 + 16 * src_y] = part[:, 96:112]


def per_device(features, cotangent, neighbour_table, send_lists, block_counts, weight_one, weight_two):
    factor = 1.0 / math.sqrt(lax.axis_size("dp") * lax.axis_size("slab") * 10 * 64)
    smem = pl.BlockSpec(memory_space=pltpu.SMEM)
    vmem = pl.BlockSpec(memory_space=pltpu.VMEM)
    hbm = pl.BlockSpec(memory_space=pl.ANY)
    dma = pltpu.SemaphoreType.DMA
    big = jax.ShapeDtypeStruct((10, 64, C), BF16)
    out, gf, fin = pl.pallas_call(
        lambda *refs: kernel(factor, *refs),
        out_shape=(big, big, jax.ShapeDtypeStruct((8, 16, 128), F32)),
        in_specs=[smem, smem, vmem, hbm, hbm, hbm, hbm],
        out_specs=(hbm, hbm, vmem),
        scratch_shapes=[
            pltpu.VMEM((9, 3, C, C), BF16),
            pltpu.VMEM((9, 3, C, C), BF16),
            pltpu.VMEM((10, 64, C), BF16),
            pltpu.VMEM((10, 64, C), BF16),
            pltpu.VMEM((10, 64, C), BF16),
            pltpu.VMEM((10, 64, C), BF16),
            pltpu.VMEM((4, 640, 128), F32),
            pltpu.VMEM((10, 4, 16, 2 * C), BF16),
            pltpu.VMEM((11, 4, 16, 2 * C), BF16),
            pltpu.VMEM((2, 2, 16, 2 * C), BF16),
            pltpu.VMEM((2, 2, 16, 2 * C), BF16),
            pltpu.VMEM((10, 4, 16, 2 * C), BF16),
            pltpu.VMEM((2, 2, 16, 2 * C), BF16),
            pltpu.VMEM((2, 2, 16, 2 * C), BF16),
            pltpu.VMEM((3, 3, 3 * ROWS, REACH), BF16),
            pltpu.VMEM((9, 6, ROWS, 2 * C), BF16),
            pltpu.VMEM((640, C), F32),
            pltpu.VMEM((640, C), F32),
            pltpu.VMEM((C, 640), BF16),
            pltpu.VMEM((C, 640), BF16),
            pltpu.VMEM((2, 6912, C), BF16),
            pltpu.VMEM((6912, C), BF16),
            pltpu.VMEM((2, 2, 384, 128), BF16),
            pltpu.VMEM((2, 2, 384, 128), BF16),
            pltpu.VMEM((2, 2, 384, 128), BF16),
            pltpu.VMEM((2, 2, 384, 128), BF16),
            pltpu.VMEM((2, 2, 4, 96, 128), BF16),
            pltpu.VMEM((2, 2, 4, 96, 128), BF16),
            pltpu.VMEM((2, 2, 4, 96, 128), BF16),
            pltpu.VMEM((2, 2, 4, 96, 128), BF16),
            pltpu.VMEM((2, 384, C), BF16),
            pltpu.VMEM((2, 4, 96, C), BF16),
            pltpu.VMEM((2, 3, 96, C), BF16),
            pltpu.VMEM((2, 3, 96, C), BF16),
            pltpu.VMEM((2, 4, 96, 128), BF16),
            pltpu.VMEM((7, 96, 128), BF16),
            pltpu.VMEM((2, 4, 4, 48, 128), BF16),
            pltpu.VMEM((7, 4, 48, 128), BF16),
            pltpu.VMEM((4, 48, 128), BF16),
            pltpu.VMEM((3, 48, 128), BF16),
            pltpu.VMEM((4, 16, 128), BF16),
            pltpu.VMEM((3, 16, 128), BF16),
            pltpu.VMEM((8, 16, 128), F32),
            pltpu.VMEM((7, 16, 128), F32),
            dma((4,)),
            dma((2,)),
            dma((2, 2)),
            dma((2, 2)),
            dma((9,)),
            dma((9,)),
            dma((2, 3, 2)),
            dma((2, 3, 2)),
            dma((2, 3, 2, 4)),
            dma((2, 3, 2, 4)),
            dma((2, 3)),
            dma((2, 3)),
            dma((2, 3)),
            dma((2, 3)),
            dma((7,)),
            dma((7,)),
            dma((7,)),
            dma((7,)),
            dma((7,)),
            dma((7,)),
            dma((3,)),
            dma((3,)),
            dma((3,)),
            dma((3,)),
        ],
        compiler_params=pltpu.CompilerParams(
            collective_id=0, has_side_effects=True, vmem_limit_bytes=60 * 1024 * 1024
        ),
        name="step",
    )(
        block_counts,
        send_lists[0, 0],
        jnp.transpose(neighbour_table, (1, 0, 2)),
        features[0],
        cotangent[0],
        weight_one.reshape(9, 3, C, C),
        weight_two.reshape(9, 3, C, C),
    )
    piece = jax.ShapeDtypeStruct((16, 432), F32)
    out, gf, g1, g2 = pl.pallas_call(
        closing,
        out_shape=(big, big, piece, piece),
        in_specs=[vmem, vmem, vmem],
        out_specs=(vmem, vmem, vmem, vmem),
        name="closing",
    )(out, gf, fin)
    return (out[None], gf[None], g1.T, g2.T)


def solution(mesh):
    in_specs = (
        P("dp", "slab", None, None),
        P("dp", "slab", None, None),
        P("dp", "slab", None),
        P("dp", "slab", None, None),
        P("dp", "slab"),
        P(),
        P(),
    )
    out_specs = (
        P("dp", "slab", None, None),
        P("dp", "slab", None, None),
        P("slab", "dp"),
        P("slab", "dp"),
    )
    return jax.shard_map(
        per_device, mesh=mesh, in_specs=in_specs, out_specs=out_specs, check_vma=False
    )
```
